256 devices in a mesh: ctx: 128 (over x_hi, y, z, core), tp: 2 (over x_lo).
Axes of the slice: x: 4 (x_hi: 2, x_lo: 2; x = x_hi * 2 + x_lo), y: 4, z: 8, core: 2. Of those that a mesh axis runs over, the one named last changes fastest.
Arguments:
- cache_k: bfloat16 [32768, 1024], P('ctx', 'tp'), may hold values from -8 to 8
- cache_v: bfloat16 [32768, 1024], P('ctx', 'tp'), may hold values from -6 to 6
- span_q: bfloat16 [512, 4096], P('ctx', 'tp'), may hold values from -8 to 8
- span_k: bfloat16 [512, 1024], P('ctx', 'tp'), may hold values from -6 to 6
- span_v: bfloat16 [512, 1024], P('ctx', 'tp'), may hold values from -6 to 6
- span_frames: int32 [512], replicated, may hold values from 0 to 7, never falling along the last dimension, each value on 1 to 128 neighbouring positions
- action_ids: int32 [512], P('ctx'), may hold values from 0 to 17
- action_table: bfloat16 [18, 1024], P(None, 'tp'), may hold values from -6 to 6
- frame_q: bfloat16 [512, 4096], P('ctx', 'tp'), may hold values from -8 to 8
- frame_k: bfloat16 [512, 1024], P('ctx', 'tp'), may hold values from -6 to 6
- frame_v: bfloat16 [512, 1024], P('ctx', 'tp'), may hold values from -6 to 6
- revealed_k: bfloat16 [512, 1024], P('ctx', 'tp'), may hold values from -6 to 6
- revealed_v: bfloat16 [512, 1024], P('ctx', 'tp'), may hold values from -6 to 6
- mask_k: bfloat16 [1024], P('tp'), may hold values from -6 to 6
- mask_v: bfloat16 [1024], P('tp'), may hold values from -6 to 6
- pass1_idx: int32 [256], replicated, may hold values from 0 to 511, as said below
- pass2_idx: int32 [128], replicated, may hold values from 0 to 511, as said below
- out_gain: float32 [4096], P('tp'), may hold values from 0.5 to 1.5
Outputs:
- span_out: bfloat16 [512, 4096], P('ctx', 'tp')
- first_out: bfloat16 [256, 4096], P('ctx', 'tp')
- second_out: bfloat16 [128, 4096], P('ctx', 'tp')
The draws below stay inside these ranges and needn't reach their ends.
Inputs may be any that keep to these rules, and one draw needn't show every extreme that they name: `pass1_idx`: 256 distinct frame positions, 0 and 511 among them. `pass2_idx`: 128 distinct entries of pass1_idx, 0 and 511 among them.
All inputs are finite; a program needn't handle non-finite values.
Results may differ from the reference program's by a relative error of at most 0.0095.
Values may be sent and summed in bfloat16 or wider, within the bound.
A program may use at most 64 MiB of HBM per device.

```python
import math
import jax
import jax.numpy as jnp
import numpy as np
from jax import lax

H = 32
KVH = 8
HD = 128
ACTIONS = 18
CACHE = 32768
SPAN = 512
FRAME = 512
MASK1 = 256
MASK2 = 128


def masked_base(key):
    middle = jax.random.permutation(jax.random.fold_in(key, 5), FRAME - 2).astype(jnp.int32) + 1
    return jnp.concatenate([jnp.array([0, FRAME - 1], jnp.int32), middle[:MASK1 - 2]])


def draw_cache_k(key, part):
    backdrop = jnp.clip(jax.random.normal(jax.random.fold_in(key, 1), (CACHE, KVH * HD), jnp.float32), -6.0, 6.0)
    return backdrop.astype(jnp.bfloat16)


def draw_span_q(key, part):
    backdrop = jnp.clip(jax.random.normal(jax.random.fold_in(key, 2), (SPAN, H * HD), jnp.float32), -6.0, 6.0)
    return backdrop.astype(jnp.bfloat16)


def draw_frame_q(key, part):
    backdrop = jnp.clip(jax.random.normal(jax.random.fold_in(key, 3), (FRAME, H * HD), jnp.float32), -6.0, 6.0)
    return backdrop.astype(jnp.bfloat16)


def draw_pass1_idx(key, part):
    base_rows = masked_base(key)
    order = jax.random.permutation(jax.random.fold_in(key, 6), MASK1)
    return base_rows[order].astype(jnp.int32)


def draw_pass2_idx(key, part):
    base_rows = masked_base(key)[:MASK2]
    order = jax.random.permutation(jax.random.fold_in(key, 7), MASK2)
    return base_rows[order].astype(jnp.int32)


def place_ends(drawn, own_key, low, high):
    extent = drawn.shape
    index_at = [jax.random.randint(jax.random.fold_in(own_key, axis), (), 0, extent[axis]) for axis in range(len(extent))]
    drawn = drawn.at[tuple(index_at)].set(low)
    longest = extent.index(max(extent))
    index_at[longest] = (index_at[longest] + 1) % extent[longest]
    return drawn.at[tuple(index_at)].set(high)


def levels(rng, dims, shards, least, top_value):
    factor_of = 1.0
    for position, shards_of in shards:
        draws = jax.random.uniform(jax.random.fold_in(jax.random.fold_in(rng, 6), position), (shards_of,), jnp.float32, least / len(shards), top_value / len(shards))
        factor_of = factor_of * jnp.repeat(jnp.exp(draws), dims[position] // shards_of).reshape((-1,) + (1,) * (len(dims) - 1 - position))
    return factor_of


def length_profile(number_of, total, bound, lean):
    loads = [(1 << 20) // math.isqrt(rank ** lean) + 1 for rank in range(2, number_of + 1)]
    surplus, given = total - bound - (number_of - 1), [1] * (number_of - 1)
    while surplus > 0:
        movable = [i for i in range(number_of - 1) if given[i] < bound]
        whole, remaining = sum([loads[i] for i in movable]), surplus
        for i in movable:
            extra = min(bound - given[i], max(1, remaining * loads[i] // whole), surplus)
            given[i] = given[i] + extra
            surplus = surplus - extra
    return np.array([bound] + given)


def uneven_parts(own_key, count, total, bound, slope):
    if count == 2:
        one = jax.random.randint(own_key, (), max(1, total - bound), min(bound, total - 1) + 1)
        return jnp.stack([one, total - one])
    tallies = jnp.asarray(length_profile(count, total, bound, slope), jnp.int32)
    couples = (count - 1) // 2
    source_of, taker = tallies[1:1 + 2 * couples:2], tallies[2:2 + 2 * couples:2]
    slack = jnp.minimum(source_of - 1, bound - taker)
    moved = jax.random.randint(jax.random.fold_in(own_key, 1), (couples,), 0, 1 << 20) % (slack + 1)
    tallies = tallies.at[1:1 + 2 * couples:2].set(source_of - moved).at[2:2 + 2 * couples:2].set(taker + moved)
    return tallies[jax.random.permutation(jax.random.fold_in(own_key, 2), count)]


def bell_draw(own_key, dims, scale, bound, pieces=(), held_as=jnp.bfloat16):
    values = jax.random.normal(own_key, dims, jnp.float32) * scale
    if len(pieces) > 0:
        values = levels(own_key, dims, pieces, -0.22, 0.18) * values
    return jnp.clip(values, min=-bound, max=bound).astype(held_as)


def setup_inputs(seed: int = 0) -> dict:
    seeds = jax.random.split(jax.random.key(seed), 19)
    return {
        "cache_k": draw_cache_k(jax.random.fold_in(seeds[18], 71), 0),
        "cache_v": bell_draw(seeds[1], (CACHE, KVH * HD), 1.0, 6.0, ((0, 128), (1, 2))),
        "span_q": draw_span_q(jax.random.fold_in(seeds[18], 71), 0),
        "span_k": bell_draw(seeds[3], (SPAN, KVH * HD), 1.0, 6.0, ((0, 128), (1, 2))),
        "span_v": bell_draw(seeds[4], (SPAN, KVH * HD), 1.0, 6.0, ((0, 128), (1, 2))),
        "span_frames": jnp.searchsorted(jnp.cumsum(uneven_parts(seeds[5], 8, SPAN, SPAN // 4, 2)), jnp.arange(SPAN), side="right").astype(jnp.int32),
        "action_ids": place_ends(jax.random.randint(seeds[6], (SPAN,), 0, ACTIONS), jax.random.fold_in(seeds[6], 1), 0, ACTIONS - 1).astype(jnp.int32),
        "action_table": bell_draw(seeds[7], (ACTIONS, KVH * HD), 1.0, 6.0, ((1, 2),)),
        "frame_q": draw_frame_q(jax.random.fold_in(seeds[18], 71), 0),
        "frame_k": bell_draw(seeds[9], (FRAME, KVH * HD), 1.0, 6.0, ((0, 128), (1, 2))),
        "frame_v": bell_draw(seeds[10], (FRAME, KVH * HD), 1.0, 6.0, ((0, 128), (1, 2))),
        "revealed_k": bell_draw(seeds[11], (FRAME, KVH * HD), 1.0, 6.0, ((0, 128), (1, 2))),
        "revealed_v": bell_draw(seeds[12], (FRAME, KVH * HD), 1.0, 6.0, ((0, 128), (1, 2))),
        "mask_k": bell_draw(seeds[13], (KVH * HD,), 1.0, 6.0, ((0, 2),)),
        "mask_v": bell_draw(seeds[14], (KVH * HD,), 1.0, 6.0, ((0, 2),)),
        "pass1_idx": draw_pass1_idx(jax.random.fold_in(seeds[18], 71), 0),
        "pass2_idx": draw_pass2_idx(jax.random.fold_in(seeds[18], 71), 0),
        "out_gain": jnp.clip(1.0 + 0.1 * jax.random.normal(seeds[17], (H * HD,), jnp.float32), 0.5, 1.5),
    }


def reference_attend(queries, groups):
    group_size = H // KVH
    scaling = HD ** (-0.5)

    def one_head(head):
        kv_head = head // group_size
        query_cols = lax.dynamic_slice_in_dim(queries, head * HD, HD, 1)
        logits_all = []
        for key_rows, value_rows, allowed in groups:
            key_cols = lax.dynamic_slice_in_dim(key_rows, kv_head * HD, HD, 1)
            logits = jnp.dot(query_cols, key_cols.T, preferred_element_type=jnp.float32) * scaling
            if allowed is not None:
                logits = jnp.where(allowed, logits, -1e+30)
            logits_all.append(logits)
        maxima = logits_all[0].max(axis=1)
        for logits in logits_all[1:]:
            maxima = jnp.maximum(maxima, logits.max(axis=1))
        numerator = jnp.zeros((queries.shape[0], HD), jnp.float32)
        denominator = jnp.zeros((queries.shape[0],), jnp.float32)
        for (key_rows, value_rows, allowed), logits in zip(groups, logits_all):
            weights = jnp.exp(logits - maxima[:, None])
            denominator = denominator + weights.sum(axis=1)
            value_cols = lax.dynamic_slice_in_dim(value_rows, kv_head * HD, HD, 1)
            numerator = numerator + jnp.dot(weights.astype(jnp.bfloat16), value_cols, preferred_element_type=jnp.float32)
        return numerator / denominator[:, None]
    heads_out = lax.map(one_head, jnp.arange(H, dtype=jnp.int32))
    return heads_out.transpose(1, 0, 2).reshape(queries.shape[0], H * HD)

def normalize(attended, out_gain):
    mean_sq = lax.optimization_barrier(jnp.mean(attended * attended, axis=1, keepdims=True))
    return (attended * lax.rsqrt(mean_sq + 1e-06) * out_gain[None, :]).astype(jnp.bfloat16)

def reference(cache_k, cache_v, span_q, span_k, span_v, span_frames, action_ids, action_table, frame_q, frame_k, frame_v, revealed_k, revealed_v, mask_k, mask_v, pass1_idx, pass2_idx, out_gain):
    action_rows = jnp.take(action_table, action_ids, axis=0).astype(jnp.float32)
    span_keys = (span_k.astype(jnp.float32) + action_rows).astype(jnp.bfloat16)
    positions = jnp.arange(FRAME, dtype=jnp.int32)
    in_first = jnp.any(positions[:, None] == pass1_idx[None, :], axis=1)[:, None]
    in_second = jnp.any(positions[:, None] == pass2_idx[None, :], axis=1)[:, None]
    first_keys = jnp.where(in_first, mask_k[None, :], frame_k)
    first_values = jnp.where(in_first, mask_v[None, :], frame_v)
    second_keys = jnp.where(in_second, mask_k[None, :], jnp.where(in_first, revealed_k, frame_k))
    second_values = jnp.where(in_second, mask_v[None, :], jnp.where(in_first, revealed_v, frame_v))
    allowed = span_frames[None, :] <= span_frames[:, None]
    cache_group = (cache_k, cache_v, None)
    prefill_att = reference_attend(span_q, [cache_group, (span_keys, span_v, allowed)])
    first_att = reference_attend(jnp.take(frame_q, pass1_idx, axis=0), [cache_group, (span_keys, span_v, None), (first_keys, first_values, None)])
    second_att = reference_attend(jnp.take(frame_q, pass2_idx, axis=0), [cache_group, (span_keys, span_v, None), (second_keys, second_values, None)])
    return (normalize(prefill_att, out_gain), normalize(first_att, out_gain), normalize(second_att, out_gain))
```

```python
import functools

import jax
import jax.numpy as jnp
from jax import lax
from jax.experimental import pallas as pl
from jax.experimental.pallas import tpu as pltpu
from jax.sharding import PartitionSpec as P

H = 32
HD = 128
NX, NY, NZ, NC = 2, 4, 8, 2
LOG2E = 1.4426950408889634
MESH = pl.DeviceIdType.MESH
F32 = jnp.float32
BF16 = jnp.bfloat16
NEG = -1e30


def kernel(
    dims,
    ck, cv, sq, sk, sv, frames, ids, table, fq, fk, fv, rk, rv, mk, mv, p1, p2, gain,
    span_out, first_out, second_out,
    kv, ex, exst, ex32, q32, qa, qast, t32, qbuf, qfs, qf, biasfs, kfr,
    nbuf, nst, sbuf, sst, at32, sq32, abst, ab, sqst, sqr,
    loc_sem, qa_s, qa_r, kv_s, kv_r, ex_s, ex_r, kvr_s,
    qz_s, qz_r, n_s, n_r, st_s, st_r, ab_s, ab_r, sq_s, sq_r,
):
    nx, nz = dims
    nb = nx * nz
    ny, nc = NY, NC
    ng = ny * nc
    total = ny * nc * nb * 4
    scale = HD ** (-0.5) * LOG2E
    me = lax.axis_index("ctx")
    tp = lax.axis_index("tp")
    c = me % nc
    z = (me // nc) % nz
    y = (me // (nc * nz)) % ny
    x = me // (nc * nz * ny)
    g = y * nc + c
    b = x * nz + z

    def ctx_of(xx, yy, zz, cc):
        return ((xx * ny + yy) * nz + zz) * nc + cc

    def in_group(d):
        return {"ctx": ctx_of(x, d // nc, z, d % nc), "tp": tp}

    def twin(d):
        return {"ctx": ctx_of(x, d // nc, z, d % nc), "tp": 1 - tp}

    def across(dx, dz):
        return {"ctx": ctx_of((x + dx) % nx, y, (z + dz) % nz, c), "tp": tp}

    def remote(src, dst, ss, rs, dev):
        return pltpu.make_async_remote_copy(
            src_ref=src, dst_ref=dst, send_sem=ss, recv_sem=rs, device_id=dev, device_id_type=MESH
        )

    barrier = pltpu.get_barrier_semaphore()

    def greet(k, _):
        pl.semaphore_signal(barrier, inc=1, device_id=in_group((g + k) % ng), device_id_type=MESH)
        return 0

    def greet_twin(k, _):
        pl.semaphore_signal(barrier, inc=1, device_id=twin((g + k) % ng), device_id_type=MESH)
        return 0

    def greet_across(j, _):
        pl.semaphore_signal(
            barrier, inc=1, device_id=across(j // nz, j % nz), device_id_type=MESH
        )
        return 0

    lax.fori_loop(1, nb, greet_across, 0)
    lax.fori_loop(1, ng, greet, 0)
    lax.fori_loop(0, ng, greet_twin, 0)

    col = pl.ds(pl.multiple_of(y * HD, HD), HD)
    own_k = pltpu.make_async_copy(ck.at[:, col], kv.at[0, g], loc_sem.at[0])
    own_v = pltpu.make_async_copy(cv.at[:, col], kv.at[1, g], loc_sem.at[1])
    own_k.start()
    own_v.start()

    q32[0:4, :] = sq[...].astype(F32)
    q32[4:8, :] = fq[...].astype(F32)
    for d in range(ng):
        qast[d] = q32[:, d * 256 : (d + 1) * 256].astype(BF16)

    row4 = lax.broadcasted_iota(jnp.int32, (4, 4), 0)
    lane4 = lax.broadcasted_iota(jnp.int32, (4, 4), 1)
    ids_col = jnp.sum(jnp.where(row4 == lane4, ids[...], 0), axis=1, keepdims=True)
    action = jnp.zeros(sk.shape, F32)
    actions = table.shape[0]
    tab = table[...].astype(F32)
    for a in range(actions):
        action = jnp.where(ids_col == a, tab[a : a + 1, :], action)
    pos = me * 4 + lax.broadcasted_iota(jnp.int32, (4, 1), 0)
    in1 = jnp.sum(jnp.where(p1[...] == pos, 1.0, 0.0), axis=1, keepdims=True) > 0.5
    in2 = jnp.sum(jnp.where(p2[...] == pos, 1.0, 0.0), axis=1, keepdims=True) > 0.5

    def masked(frame, revealed, mask):
        shape = frame.shape
        frame, revealed = frame[...].astype(F32), revealed[...].astype(F32)
        mask = jnp.broadcast_to(mask[...].astype(F32), shape)
        first = jnp.where(in1, mask, frame)
        second = jnp.where(in2, mask, jnp.where(in1, revealed, frame))
        return first, second

    for n, (span, pair) in enumerate(
        (
            (sk[...].astype(F32) + action, masked(fk, rk, mk)),
            (sv[...].astype(F32), masked(fv, rv, mv)),
        )
    ):
        ex32[0:4, :] = span
        ex32[4:8, :] = pair[0]
        ex32[8:12, :] = pair[1]
        ex32[12:16, :] = jnp.zeros_like(span)
        for d in range(ny):
            exst[n, d] = ex32[:, d * HD : (d + 1) * HD].astype(BF16)

    pl.semaphore_wait(barrier, (nb - 1) + (ng - 1) + ng)

    def qa_copy(k):
        d = (g + k) % ng
        return remote(qast.at[d], qa.at[g], qa_s.at[k], qa_r.at[k], in_group(d))

    def ex_copy(k):
        d = (g + k) % ng
        return remote(exst.at[:, d // nc], ex.at[:, g], ex_s.at[k], ex_r.at[k], in_group(d))

    def kv_copy(n, k):
        d = (g + nc * k) % ng
        head = pl.ds(pl.multiple_of((d // nc) * HD, HD), HD)
        source = (ck, cv)[n]
        return remote(
            source.at[:, head], kv.at[n, g], kv_s.at[n, k], kv_r.at[n, k], in_group(d)
        )

    def relay(n, k):
        origin = (g + ng - nc * k) % ng
        peer = y * nc + 1 - c
        src = ((ck, cv)[n].at[:, col]) if k == 0 else kv.at[n, origin]
        return remote(src, kv.at[n, origin], kvr_s.at[n, k], kv_r.at[n, ny + k], in_group(peer))

    for k in range(1, ng):
        qa_copy(k).start()
    for k in range(1, ny):
        for n in range(2):
            kv_copy(n, k).start()
    for n in range(2):
        relay(n, 0).start()
    for k in range(1, ng):
        ex_copy(k).start()
    qa[g] = qast[g]
    for n in range(2):
        ex[n, g] = exst[n, y]

    for k in range(1, ng):
        qa_copy(k).wait_recv()
    for h in range(2):
        cols = slice(h * HD, (h + 1) * HD)
        t32[h] = qa[:, :, cols].astype(F32).reshape(64, HD)
        for i in range(4):
            pair = [t32[h, pl.ds(2 * i + r, 8, stride=8), :] for r in range(2)]
            qbuf[b, 16 * i : 16 * i + 16, cols] = jnp.concatenate(pair, axis=0).astype(BF16)

    def qz_copy(half, j):
        part = pl.ds(half * 32, 32)
        return remote(
            qbuf.at[b, part], qbuf.at[b, part], qz_s.at[half, j], qz_r.at[half, j],
            across(j // nz, j % nz),
        )

    def far_first(i):
        step = (i + 1) // 2
        dz = nz // 2 + step * (2 * (i % 2) - 1)
        return (dz + nz) % nz

    def start_q(half):
        def body(j, _):
            qz_copy(half, j).start()
            return 0

        return body

    lax.fori_loop(1, nb, start_q(1), 0)
    lax.fori_loop(1, nb, start_q(0), 0)

    rows = 32 * nb
    r = lax.broadcasted_iota(jnp.int32, (rows, total), 0)
    lane = lax.broadcasted_iota(jnp.int32, (rows, total), 1)
    rb, rt, ro = r >> 5, (r >> 3) & 3, r & 7
    rx, rz = jnp.where(rb >= nz, 1, 0), jnp.where(rb >= nz, rb - nz, rb)
    want = 4 * (((rx * ny + (ro >> 1)) * nz + rz) * nc + (ro & 1)) + rt
    fr = jnp.broadcast_to(frames[...].astype(F32), (rows, total))
    qframe = jnp.sum(jnp.where(lane == want, fr, 0.0), axis=1, keepdims=True)
    qf[...] = jnp.broadcast_to(qframe, (rows, 128)).reshape(nb, 32, 128)

    key = lax.broadcasted_iota(jnp.int32, (total, 128), 0)
    kl = lax.broadcasted_iota(jnp.int32, (total, 128), 1)
    ko, ks = kl >> 4, kl & 15
    kwant = 4 * (((x * ny + (ko >> 1)) * nz + z) * nc + (ko & 1)) + ks
    khit = jnp.where((key == kwant) & (ks < 4), 1.0, 0.0).astype(BF16)
    fr8 = jnp.broadcast_to(frames[...].astype(F32), (8, total)).astype(BF16)
    kfr[...] = jnp.dot(fr8, khit, preferred_element_type=F32)

    frows = 24 * nx
    fr_i = lax.broadcasted_iota(jnp.int32, (frows, 128), 0)
    fslot = lax.broadcasted_iota(jnp.int32, (frows, 128), 1) & 15
    ftt = (jnp.where(fr_i >= 24, fr_i - 24, fr_i)) >> 3
    allowed = (
        (fslot < 4)
        | ((fslot >= 4) & (fslot < 8) & (ftt < 2))
        | ((fslot >= 8) & (fslot < 12) & (ftt == 2))
    )
    biasfs[...] = jnp.where(allowed, 0.0, NEG)

    def picks(step):
        def place(width):
            rr = lax.broadcasted_iota(jnp.int32, (frows, width), 0)
            ll = lax.broadcasted_iota(jnp.int32, (frows, width), 1)
            xx = jnp.where(rr >= 24, 1, 0)
            tt = (rr - 24 * xx) >> 3
            oo = rr & 7
            owner = ((xx * ny + (oo >> 1)) * nz + step) * nc + (oo & 1)
            return ll, tt, owner

        l1, t1, o1 = place(p1.shape[1])
        l2, t2, o2 = place(p2.shape[1])
        v1 = jnp.broadcast_to(p1[...], l1.shape).astype(F32)
        v2 = jnp.broadcast_to(p2[...], l2.shape).astype(F32)
        found = jnp.sum(
            jnp.where((l1 == 2 * o1 + t1) & (t1 < 2), v1, 0.0), axis=1, keepdims=True
        ) + jnp.sum(jnp.where((l2 == o2) & (t2 == 2), v2, 0.0), axis=1, keepdims=True)
        return found.astype(jnp.int32)

    def located(found):
        bits = nz.bit_length() - 1
        row = found & 3
        dev = found >> 2
        cc = dev & 1
        zz = (dev >> 1) & (nz - 1)
        yy = (dev >> (1 + bits)) & (ny - 1)
        xx = dev >> (3 + bits)
        return (xx * nz + zz) * 32 + row * 8 + yy * nc + cc

    for k in range(1, ny):
        for n in range(2):
            kv_copy(n, k).wait_recv()
            relay(n, k).start()

    def wait_q(half):
        def body(j, _):
            qz_copy(half, j).wait_recv()
            return 0

        return body

    lax.fori_loop(1, nb, wait_q(1), 0)
    frame_q = qbuf[:, 32:64, :].reshape(32 * nb, 256)
    for step in range(nz):
        at = located(picks(step))
        lanes = lax.broadcasted_iota(jnp.int32, (frows, 32 * nb), 1)
        hot = jnp.where(lanes == at, 1.0, 0.0).astype(BF16)
        qfs[step] = jnp.dot(hot, frame_q, preferred_element_type=F32).astype(BF16)

    for k in range(1, ng):
        ex_copy(k).wait_recv()
    own_k.wait()
    own_v.wait()
    for k in range(ny):
        for n in range(2):
            relay(n, k).wait_recv()
    lax.fori_loop(1, nb, wait_q(0), 0)

    def n_copy(j, blk):
        return remote(nst.at[blk], nbuf.at[b], n_s.at[j], n_r.at[j], across(j // nz, j % nz))

    def st_copy(j, blk):
        return remote(sst.at[blk], sbuf.at[b], st_s.at[j], st_r.at[j], across(j // nz, j % nz))

    keys = kv.shape[1] * kv.shape[2]
    nt = (((1,), (1,)), ((), ()))
    per = 56 * nx

    def attend(i, _):
        dz = far_first(i)
        zz = (z + dz) % nz
        blocks = [((x + dx) % nx) * nz + zz for dx in range(nx)]
        order = [lax.rem(jnp.int32(xx), nx) * nz + zz for xx in range(nx)]
        kframe = kfr[0:1, :]
        slot = lax.broadcasted_iota(jnp.int32, (32, 128), 1) & 15
        bias = []
        for blk in order:
            ok = (slot < 4) & (kframe <= qf[blk])
            bias.append(jnp.where(ok, 0.0, NEG))
        bias.append(biasfs[...])
        bias = jnp.concatenate(bias, axis=0)
        bias = jnp.concatenate([bias, bias], axis=0)
        parts = []
        for h in range(2):
            cols = slice(h * HD, (h + 1) * HD)
            parts += [qbuf[blk, 0:32, cols] for blk in order]
            parts.append(qfs[zz, :, cols])
        q = jnp.concatenate(parts, axis=0)
        s1 = lax.dot_general(q, kv[0].reshape(keys, HD), nt, preferred_element_type=F32)
        s2 = lax.dot_general(q, ex[0].reshape(128, HD), nt, preferred_element_type=F32) + bias
        m = jnp.maximum(s1.max(axis=1, keepdims=True), s2.max(axis=1, keepdims=True))
        w1 = jnp.exp2((s1 - m) * scale)
        w2 = jnp.exp2((s2 - m) * scale)
        tot = w1.sum(axis=1, keepdims=True) + w2.sum(axis=1, keepdims=True)
        o = jnp.dot(w1.astype(BF16), kv[1].reshape(keys, HD), preferred_element_type=F32)
        o = o + jnp.dot(w2.astype(BF16), ex[1].reshape(128, HD), preferred_element_type=F32)
        lanes = lax.broadcasted_iota(jnp.int32, (2 * per, 128), 1)
        stats = jnp.where(lanes == 0, m, tot)
        for xx in range(nx):
            blk = order[xx]

            def piece(v):
                out = []
                for h in range(2):
                    base = h * per
                    out.append(v[base + 32 * xx : base + 32 * xx + 32])
                    low = base + 32 * nx + 24 * xx
                    out.append(v[low : low + 24])
                return out

            nst[blk] = jnp.concatenate(piece(o), axis=0).astype(BF16)
            full = jnp.concatenate(piece(stats) + [jnp.zeros((16, 128), F32)], axis=0)
            sst[blk] = full.T[0:8, :]
        for dx in range(nx):
            j = dx * nz + dz
            if dx == 0:

                @pl.when(i < nz - 1)
                def _():
                    n_copy(j, blocks[0]).start()
                    st_copy(j, blocks[0]).start()
            else:
                n_copy(j, blocks[dx]).start()
                st_copy(j, blocks[dx]).start()
        return 0

    lax.fori_loop(0, nz, attend, 0)
    nbuf[b] = nst[b]
    sbuf[b] = sst[b]

    def wait_n(j, _):
        n_copy(j, b).wait_recv()
        st_copy(j, b).wait_recv()
        return 0

    lax.fori_loop(1, nb, wait_n, 0)

    st = sbuf[...].reshape(nb * 8, 128)
    if nb < 16:
        st = jnp.concatenate([st, jnp.zeros((128 - nb * 8, 128), F32)], axis=0)
    st = st.T
    lanes = lax.broadcasted_iota(jnp.int32, (128, 128), 1)
    is_m = ((lanes & 7) == 0) & (lanes < 8 * nb)
    top = jnp.max(jnp.where(is_m, st, NEG), axis=1, keepdims=True)
    tot = pltpu.roll(st, 127, 1)
    e = jnp.where(is_m, jnp.exp2((jnp.where(is_m, st, top) - top) * scale), 0.0)
    den = jnp.sum(jnp.where(is_m, e * tot, 0.0), axis=1, keepdims=True)
    w = e[0:112] / den[0:112]
    acc = jnp.zeros((112, HD), F32)
    for s in range(nb):
        acc = acc + w[:, 8 * s : 8 * s + 1] * nbuf[s].astype(F32)
    squares = jnp.sum(acc * acc, axis=1, keepdims=True)
    at32[0, 0:56, :] = acc[0:56]
    at32[1, 0:56, :] = acc[56:112]
    at32[:, 56:64, :] = jnp.zeros((2, 8, HD), F32)
    sq32[0:56, :] = jnp.broadcast_to(squares[0:56] + squares[56:112], (56, 128))
    sq32[56:64, :] = jnp.zeros((8, 128), F32)
    for d in range(ng):
        for h in range(2):
            abst[d, :, h * HD : (h + 1) * HD] = at32[h, pl.ds(d, 8, stride=8), :]
        sqst[d] = sq32[pl.ds(d, 8, stride=8), :]

    def ab_copy(k):
        d = (g + k) % ng
        return remote(abst.at[d], ab.at[g], ab_s.at[k], ab_r.at[k], in_group(d))

    def sq_copy(k):
        d = (g + k) % ng
        return remote(sqst.at[d], sqr.at[g], sq_s.at[k], sq_r.at[k], twin(d))

    for k in range(1, ng):
        ab_copy(k).start()
    for k in range(ng):
        sq_copy(k).start()
    ab[g] = abst[g]
    for k in range(1, ng):
        ab_copy(k).wait_recv()
    for k in range(ng):
        sq_copy(k).wait_recv()
    pieces = [ab[d] for d in range(ng)]
    square = sqr[0]
    for d in range(1, ng):
        square = square + sqr[d]
    square = square[:, 0:1]
    for piece_ in pieces:
        square = square + jnp.sum(piece_ * piece_, axis=1, keepdims=True)
    inv = lax.rsqrt(square / (H * HD) + 1e-06)
    for d in range(ng):
        cols = slice(d * 256, (d + 1) * 256)
        done = pieces[d] * inv * gain[:, cols]
        span_out[:, cols] = done[0:4].astype(BF16)
        first_out[:, cols] = done[4:6].astype(BF16)
        second_out[:, cols] = done[6:7].astype(BF16)

    def drain(j, _):
        qz_copy(0, j).wait_send()
        qz_copy(1, j).wait_send()
        n_copy(j, b).wait_send()
        st_copy(j, b).wait_send()
        return 0

    lax.fori_loop(1, nb, drain, 0)
    for k in range(1, ng):
        qa_copy(k).wait_send()
        ex_copy(k).wait_send()
        ab_copy(k).wait_send()
    for k in range(ng):
        sq_copy(k).wait_send()
    for n in range(2):
        for k in range(1, ny):
            kv_copy(n, k).wait_send()
        for k in range(ny):
            relay(n, k).wait_send()


def per_device(
    dims, cache_k, cache_v, span_q, span_k, span_v, span_frames, action_ids, action_table,
    frame_q, frame_k, frame_v, revealed_k, revealed_v, mask_k, mask_v, pass1_idx, pass2_idx,
    out_gain,
):
    nx, nz = dims
    nb = nx * nz
    ng = NY * NC
    rows = cache_k.shape[0]
    cols = span_k.shape[1]
    dma = pltpu.SemaphoreType.DMA
    vm = pltpu.VMEM
    anywhere = pl.BlockSpec(memory_space=pl.ANY)
    local = pl.BlockSpec(memory_space=pltpu.VMEM)
    outs = [
        jax.ShapeDtypeStruct((n, span_q.shape[1]), BF16) for n in (4, 2, 1)
    ]
    row = lambda v: v.reshape(1, -1)
    return pl.pallas_call(
        functools.partial(kernel, dims),
        out_shape=outs,
        in_specs=[anywhere, anywhere] + [local] * 16,
        out_specs=[local] * 3,
        scratch_shapes=[
            vm((2, ng, rows, HD), BF16),
            vm((2, ng, 16, HD), BF16),
            vm((2, NY, 16, HD), BF16),
            vm((16, cols), F32),
            vm((8, span_q.shape[1]), F32),
            vm((ng, 8, 256), BF16),
            vm((ng, 8, 256), BF16),
            vm((2, 64, HD), F32),
            vm((nb, 64, 256), BF16),
            vm((nz, 24 * nx, 256), BF16),
            vm((nb, 32, 128), F32),
            vm((24 * nx, 128), F32),
            vm((8, 128), F32),
            vm((nb, 112, HD), BF16),
            vm((nb, 112, HD), BF16),
            vm((nb, 8, 128), F32),
            vm((nb, 8, 128), F32),
            vm((2, 64, HD), F32),
            vm((64, 128), F32),
            vm((ng, 8, 256), F32),
            vm((ng, 8, 256), F32),
            vm((ng, 8, 128), F32),
            vm((ng, 8, 128), F32),
            dma((2,)),
            dma((ng,)),
            dma((ng,)),
            dma((2, NY)),
            dma((2, 2 * NY)),
            dma((ng,)),
            dma((ng,)),
            dma((2, NY)),
            dma((2, nb)),
            dma((2, nb)),
            dma((nb,)),
            dma((nb,)),
            dma((nb,)),
            dma((nb,)),
            dma((ng,)),
            dma((ng,)),
            dma((ng,)),
            dma((ng,)),
        ],
        compiler_params=pltpu.CompilerParams(
            collective_id=0, has_side_effects=True, vmem_limit_bytes=60 << 20
        ),
        name="frame_attention",
    )(
        cache_k, cache_v, span_q, span_k, span_v, row(span_frames), row(action_ids), action_table,
        frame_q, frame_k, frame_v, revealed_k, revealed_v, row(mask_k), row(mask_v),
        row(pass1_idx), row(pass2_idx), row(out_gain),
    )


def solution(mesh):
    both = P("ctx", "tp")
    in_specs = (
        both, both, both, both, both, P(), P("ctx"), P(None, "tp"), both, both, both, both, both,
        P("tp"), P("tp"), P(), P(), P("tp"),
    )
    nz = NZ
    nx = mesh.shape["ctx"] // (NY * NC * nz)
    return jax.shard_map(
        functools.partial(per_device, (nx, nz)),
        mesh=mesh,
        in_specs=in_specs,
        out_specs=(both, both, both),
        check_vma=False,
    )
```

```python
import functools

import jax
import jax.numpy as jnp
from jax import lax
from jax.experimental import pallas as pl
from jax.experimental.pallas import tpu as pltpu
from jax.sharding import PartitionSpec as P

H = 32
HD = 128
NX, NY, NZ, NC = 2, 4, 8, 2
LOG2E = 1.4426950408889634
MESH = pl.DeviceIdType.MESH
F32 = jnp.float32
BF16 = jnp.bfloat16
NEG = -1e30


def kernel(
    dims,
    ck, cv, *refs,
):
    nx, nz = dims
    hbm, refs = refs[:16], refs[16:]
    (span_out, first_out, second_out), refs = refs[:3], refs[3:]
    vmem, refs = refs[:16], refs[16:]
    sq, sk, sv, frames, ids, table, fq, fk, fv, rk, rv, mk, mv, p1, p2, gain = vmem
    (
        kv, ex, exst, ex32, q32, qa, qast, t32, qbuf, hot, qfs, qf, kfr,
        nst, nbuf, fst, fbuf, sst, sbuf, gst, gbuf, m32, at32, sq32, abst, ab, sqst, sqr,
        loc_sem, qa_s, qa_r, kv_s, kv_r, ex_s, ex_r, kvr_s,
        qz_s, qz_r, qx_s, qx_r, n_s, n_r, st_s, st_r, f_s, f_r, gt_s, gt_r,
        ab_s, ab_r, sq_s, sq_r,
    ) = refs
    nb = nx * nz
    ny, nc = NY, NC
    ng = ny * nc
    total = ny * nc * nb * 4
    scale = HD ** (-0.5) * LOG2E
    me = lax.axis_index("ctx")
    tp = lax.axis_index("tp")
    c = me % nc
    z = (me // nc) % nz
    y = (me // (nc * nz)) % ny
    x = me // (nc * nz * ny)
    g = y * nc + c
    b = x * nz + z

    def ctx_of(xx, yy, zz, cc):
        return ((xx * ny + yy) * nz + zz) * nc + cc

    def in_group(d):
        return {"ctx": ctx_of(x, d // nc, z, d % nc), "tp": tp}

    def twin(d):
        return {"ctx": ctx_of(x, d // nc, z, d % nc), "tp": 1 - tp}

    def at_block(xx, zz):
        return {"ctx": ctx_of(xx, y, zz, c), "tp": tp}

    def remote(src, dst, ss, rs, dev):
        return pltpu.make_async_remote_copy(
            src_ref=src, dst_ref=dst, send_sem=ss, recv_sem=rs, device_id=dev, device_id_type=MESH
        )

    barrier = pltpu.get_barrier_semaphore()

    def greet(k, _):
        pl.semaphore_signal(barrier, inc=1, device_id=in_group((g + k) % ng), device_id_type=MESH)
        return 0

    def greet_twin(k, _):
        pl.semaphore_signal(barrier, inc=1, device_id=twin((g + k) % ng), device_id_type=MESH)
        return 0

    def greet_across(j, _):
        dev = at_block((x + j // nz) % nx, (z + j % nz) % nz)
        pl.semaphore_signal(barrier, inc=1, device_id=dev, device_id_type=MESH)
        return 0

    lax.fori_loop(1, nb, greet_across, 0)
    lax.fori_loop(1, ng, greet, 0)
    lax.fori_loop(0, ng, greet_twin, 0)

    def load(i):
        return pltpu.make_async_copy(hbm[i], vmem[i], loc_sem.at[2 + i])

    for i in (0, 6, 1, 2, 3, 4, 5, 7, 8, 9, 10, 11, 12, 13, 14, 15):
        load(i).start()
    col = pl.ds(pl.multiple_of(y * HD, HD), HD)
    own_k = pltpu.make_async_copy(ck.at[:, col], kv.at[0, g], loc_sem.at[0])
    own_v = pltpu.make_async_copy(cv.at[:, col], kv.at[1, g], loc_sem.at[1])
    own_k.start()
    own_v.start()

    load(0).wait()
    load(6).wait()
    q32[0:4, :] = sq[...].astype(F32)
    q32[4:8, :] = fq[...].astype(F32)
    for d in range(ng):
        qast[d] = q32[:, d * 256 : (d + 1) * 256].astype(BF16)

    def qa_copy(k):
        d = (g + k) % ng
        return remote(qast.at[d], qa.at[g], qa_s.at[k], qa_r.at[k], in_group(d))

    def ex_copy(k):
        d = (g + k) % ng
        return remote(exst.at[:, d // nc], ex.at[:, g], ex_s.at[k], ex_r.at[k], in_group(d))

    def kv_copy(n, k):
        d = (g + nc * k) % ng
        head = pl.ds(pl.multiple_of((d // nc) * HD, HD), HD)
        source = (ck, cv)[n]
        return remote(
            source.at[:, head], kv.at[n, g], kv_s.at[n, k], kv_r.at[n, k], in_group(d)
        )

    def relay(n, k):
        origin = (g + ng - nc * k) % ng
        peer = y * nc + 1 - c
        src = ((ck, cv)[n].at[:, col]) if k == 0 else kv.at[n, origin]
        return remote(src, kv.at[n, origin], kvr_s.at[n, k], kv_r.at[n, ny + k], in_group(peer))

    with jax.named_scope("w_barrier"):
        pl.semaphore_wait(barrier, (nb - 1) + (ng - 1) + ng)

    for k in range(1, ng):
        qa_copy(k).start()
    for k in range(1, ny):
        for n in range(2):
            kv_copy(n, k).start()
    for n in range(2):
        relay(n, 0).start()
    qa[g] = qast[g]

    for i in (1, 2, 3, 4, 5, 7, 8, 9, 10, 11, 12, 13, 14, 15):
        load(i).wait()

    row4 = lax.broadcasted_iota(jnp.int32, (4, 4), 0)
    lane4 = lax.broadcasted_iota(jnp.int32, (4, 4), 1)
    ids_col = jnp.sum(jnp.where(row4 == lane4, ids[...], 0), axis=1, keepdims=True)
    action = jnp.zeros(sk.shape, F32)
    tab = table[...].astype(F32)
    for a in range(table.shape[0]):
        action = jnp.where(ids_col == a, tab[a : a + 1, :], action)
    pos = me * 4 + lax.broadcasted_iota(jnp.int32, (4, 1), 0)
    in1 = jnp.sum(jnp.where(p1[...] == pos, 1.0, 0.0), axis=1, keepdims=True) > 0.5
    in2 = jnp.sum(jnp.where(p2[...] == pos, 1.0, 0.0), axis=1, keepdims=True) > 0.5

    def masked(frame, revealed, mask):
        shape = frame.shape
        frame, revealed = frame[...].astype(F32), revealed[...].astype(F32)
        mask = jnp.broadcast_to(mask[...].astype(F32).reshape(1, -1), shape)
        first = jnp.where(in1, mask, frame)
        second = jnp.where(in2, mask, jnp.where(in1, revealed, frame))
        return first, second

    for n, (span, pair) in enumerate(
        (
            (sk[...].astype(F32) + action, masked(fk, rk, mk)),
            (sv[...].astype(F32), masked(fv, rv, mv)),
        )
    ):
        ex32[0:4, :] = span
        ex32[4:8, :] = pair[0]
        ex32[8:12, :] = pair[1]
        ex32[12:16, :] = jnp.zeros_like(span)
        for d in range(ny):
            exst[n, d] = ex32[:, d * HD : (d + 1) * HD].astype(BF16)
    for k in range(1, ng):
        ex_copy(k).start()
    for n in range(2):
        ex[n, g] = exst[n, y]

    with jax.named_scope("w_qa"):
        for k in range(1, ng):
            qa_copy(k).wait_recv()
    for h in range(2):
        cols = slice(h * HD, (h + 1) * HD)
        t32[h] = qa[:, :, cols].astype(F32).reshape(64, HD)
        for i in range(4):
            pair = [t32[h, pl.ds(2 * i + r, 8, stride=8), :] for r in range(2)]
            qbuf[b, 16 * i : 16 * i + 16, cols] = jnp.concatenate(pair, axis=0).astype(BF16)

    def off(k):
        near = k // 2
        return near + 1 if k % 2 else (nz - near) % nz

    def off_dyn(k):
        near = k // 2
        odd = k % 2
        return (odd * (near + 1) + (1 - odd) * (nz - near)) % nz

    def qz_copy(k):
        return remote(
            qbuf.at[b], qbuf.at[b], qz_s.at[k], qz_r.at[k], at_block(x, (z + off(k)) % nz)
        )

    def qx_copy(k):
        blk = x * nz + (z + nz - off(k)) % nz
        return remote(
            qbuf.at[blk], qbuf.at[blk], qx_s.at[k], qx_r.at[k], at_block((x + 1) % nx, z)
        )

    for k in range(1, nz):
        qz_copy(k).start()
    qx_copy(0).start()

    rows = 32 * nb

    def owners(width):
        r = lax.broadcasted_iota(jnp.int32, (rows, width), 0)
        ll = lax.broadcasted_iota(jnp.int32, (rows, width), 1)
        rb, rt, ro = r >> 5, (r >> 3) & 3, r & 7
        rx = jnp.where(rb >= nz, 1, 0)
        rz = rb - nz * rx
        return ll, rt, ((rx * ny + (ro >> 1)) * nz + rz) * nc + (ro & 1)

    lane, rt, owner = owners(total)
    fr = jnp.broadcast_to(frames[...].astype(F32), (rows, total))
    qframe = jnp.sum(jnp.where(lane == 4 * owner + rt, fr, 0.0), axis=1, keepdims=True)
    qf[...] = jnp.broadcast_to(qframe, (rows, 128)).reshape(nb, 32, 128)

    key = lax.broadcasted_iota(jnp.int32, (total, 128), 0)
    kl = lax.broadcasted_iota(jnp.int32, (total, 128), 1)
    ko, ks = kl >> 4, kl & 15
    kwant = 4 * (((x * ny + (ko >> 1)) * nz + z) * nc + (ko & 1)) + ks
    khit = jnp.where((key == kwant) & (ks < 4), 1.0, 0.0).astype(BF16)
    fr8 = jnp.broadcast_to(frames[...].astype(F32), (8, total)).astype(BF16)
    kfr[...] = jnp.dot(fr8, khit, preferred_element_type=F32)

    l1, t1, o1 = owners(p1.shape[1])
    l2, t2, o2 = owners(p2.shape[1])
    v1 = jnp.broadcast_to(p1[...].astype(F32), l1.shape)
    v2 = jnp.broadcast_to(p2[...].astype(F32), l2.shape)
    found = jnp.sum(
        jnp.where((l1 == 2 * o1 + t1) & (t1 < 2), v1, 0.0), axis=1, keepdims=True
    ) + jnp.sum(jnp.where((l2 == o2) & (t2 == 2), v2, 0.0), axis=1, keepdims=True)
    found = found.astype(jnp.int32)
    bits = nz.bit_length() - 1
    dev = found >> 2
    from_z = (dev >> 1) & (nz - 1)
    from_y = (dev >> (1 + bits)) & (ny - 1)
    from_x = dev >> (3 + bits)
    place = (from_x * nz + from_z) * 32 + (found & 3) * 8 + from_y * nc + (dev & 1)
    lanes = lax.broadcasted_iota(jnp.int32, (rows, rows), 1)
    hot[...] = jnp.where(lanes == place, 1.0, 0.0).astype(BF16)

    with jax.named_scope("w_kv"):
        for k in range(1, ny):
            for n in range(2):
                kv_copy(n, k).wait_recv()
                relay(n, k).start()

    def from_z_half(k):
        qz_copy(k).wait_recv()
        qx_copy(k).start()

    with jax.named_scope("w_qz"):
        for k in range(1, 4):
            from_z_half(k)

    with jax.named_scope("w_relay"):
        for k in range(1, ng):
            ex_copy(k).wait_recv()
        own_k.wait()
        own_v.wait()
        for k in range(ny):
            for n in range(2):
                relay(n, k).wait_recv()

    keys = kv.shape[1] * kv.shape[2]
    nt = (((1,), (1,)), ((), ()))

    def dest(k):
        return (x + k // nz) % nx, (z + nz - off_dyn(k % nz)) % nz

    def attention(q, bias):
        s1 = lax.dot_general(q, kv[0].reshape(keys, HD), nt, preferred_element_type=F32)
        s2 = lax.dot_general(q, ex[0].reshape(128, HD), nt, preferred_element_type=F32) + bias
        m = jnp.maximum(s1.max(axis=1, keepdims=True), s2.max(axis=1, keepdims=True))
        w1 = jnp.exp2((s1 - m) * scale)
        w2 = jnp.exp2((s2 - m) * scale)
        tot = w1.sum(axis=1, keepdims=True) + w2.sum(axis=1, keepdims=True)
        o = jnp.dot(w1.astype(BF16), kv[1].reshape(keys, HD), preferred_element_type=F32)
        o = o + jnp.dot(w2.astype(BF16), ex[1].reshape(128, HD), preferred_element_type=F32)
        return o, jnp.where(lax.broadcasted_iota(jnp.int32, o.shape, 1) == 0, m, tot)

    def n_copy(k, blk, dev):
        return remote(nst.at[blk], nbuf.at[b], n_s.at[k], n_r.at[k], dev)

    def st_copy(k, blk, dev):
        return remote(sst.at[blk], sbuf.at[b], st_s.at[k], st_r.at[k], dev)

    def f_copy(k, blk, dev):
        return remote(fst.at[blk], fbuf.at[b], f_s.at[k], f_r.at[k], dev)

    def gt_copy(k, blk, dev):
        return remote(gst.at[blk], gbuf.at[b], gt_s.at[k], gt_r.at[k], dev)

    def put_stats(stats, into, blks):
        turned = stats.T[0:8, :]
        for q in range(4):
            tile = turned[:, (q // 2) * 128 : (q // 2) * 128 + 128]
            if q % 2:
                tile = pltpu.roll(tile, 64, 1)
            into[blks[q]] = tile[0:2]

    def push(s, blks, dests, copies):
        for q in range(4):
            dev = at_block(*dests[q])

            def go(q=q, dev=dev):
                for copy in copies:
                    copy(4 * s + q, blks[q], dev).start()

            if q == 0:
                pl.when(s > 0)(go)
            else:
                go()

    slot32 = lax.broadcasted_iota(jnp.int32, (32, 128), 1) & 15
    half = nz // 4

    def spans(s, _):
        for u in range(half, 2 * half):

            @pl.when(s == u)
            def _(u=u):
                for q in range(4):
                    qx_copy(4 * (u - half) + q).wait_recv()

        for u in range(1, half):

            @pl.when(s == u)
            def _(u=u):
                for q in range(4):
                    from_z_half(4 * u + q)

        dests = [dest(4 * s + q) for q in range(4)]
        blks = [xx * nz + zz for xx, zz in dests]
        parts, bias = [], []
        for blk in blks:
            mask = jnp.where((slot32 < 4) & (kfr[0:1, :] <= qf[blk]), 0.0, NEG)
            bias += [mask, mask]
            parts += [qbuf[blk, 0:32, 0:HD], qbuf[blk, 0:32, HD : 2 * HD]]
        o, stats = attention(jnp.concatenate(parts, axis=0), jnp.concatenate(bias, axis=0))
        for q in range(4):
            nst[blks[q]] = o[64 * q : 64 * q + 64].astype(BF16)
        put_stats(stats, sst, blks)
        push(s, blks, dests, (n_copy, st_copy))
        return 0

    with jax.named_scope("spans"):
        lax.fori_loop(0, 2 * half, spans, 0)

    frame_q = qbuf[:, 32:64, :].reshape(rows, 256)
    picked = jnp.dot(hot[...], frame_q, preferred_element_type=F32)
    for blk in range(nb):
        both = [picked[32 * blk : 32 * blk + 24, h * HD : (h + 1) * HD] for h in range(2)]
        qfs[blk] = jnp.concatenate(both, axis=0).astype(BF16)

    r48 = lax.broadcasted_iota(jnp.int32, (48, 128), 0)
    slot48 = lax.broadcasted_iota(jnp.int32, (48, 128), 1) & 15
    t48 = (jnp.where(r48 >= 24, r48 - 24, r48)) >> 3
    allowed = (slot48 < 4) | ((slot48 < 8) & (t48 < 2)) | (
        (slot48 >= 8) & (slot48 < 12) & (t48 == 2)
    )
    mask48 = jnp.where(allowed, 0.0, NEG)

    def picks(s, _):
        dests = [dest(4 * s + q) for q in range(4)]
        blks = [xx * nz + zz for xx, zz in dests]
        q_rows = jnp.concatenate([qfs[blk] for blk in blks], axis=0)
        o, stats = attention(q_rows, jnp.concatenate([mask48] * 4, axis=0))
        pad = jnp.zeros((16, 128), F32)
        padded = []
        for q in range(4):
            fst[blks[q]] = o[48 * q : 48 * q + 48].astype(BF16)
            padded += [stats[48 * q : 48 * q + 48], pad]
        put_stats(jnp.concatenate(padded, axis=0), gst, blks)
        push(s, blks, dests, (f_copy, gt_copy))
        return 0

    with jax.named_scope("picks"):
        lax.fori_loop(0, 2 * half, picks, 0)
    nbuf[b] = nst[b]
    sbuf[b] = sst[b]
    fbuf[b] = fst[b]
    gbuf[b] = gst[b]
    home = at_block((x + 1) % nx, z)

    def arrive(copies):
        def body(k, _):
            for copy in copies:
                copy(k, b, home).wait_recv()
            return 0

        lax.fori_loop(1, nb, body, 0)

    def merge(data, stats, n):
        for s in range(nb):
            m32[2 * s : 2 * s + 2, :] = stats[s]
        st = m32[...].T[0:n]
        lanes = lax.broadcasted_iota(jnp.int32, (n, 128), 1)
        is_m = ((lanes & 1) == 0) & (lanes < 2 * nb)
        top = jnp.max(jnp.where(is_m, st, NEG), axis=1, keepdims=True)
        tot = pltpu.roll(st, 127, 1)
        e = jnp.where(is_m, jnp.exp2((jnp.where(is_m, st, top) - top) * scale), 0.0)
        den = jnp.sum(jnp.where(is_m, e * tot, 0.0), axis=1, keepdims=True)
        w = e / den
        acc = jnp.zeros((n, HD), F32)
        for s in range(nb):
            acc = acc + w[:, 2 * s : 2 * s + 1] * data[s].astype(F32)
        return acc

    def settle(acc, low, n):
        squares = jnp.sum(acc * acc, axis=1, keepdims=True)
        at32[0, low : low + n, :] = acc[0:n]
        at32[1, low : low + n, :] = acc[n : 2 * n]
        sq32[low : low + n, :] = jnp.broadcast_to(squares[0:n] + squares[n : 2 * n], (n, 128))

    m32[...] = jnp.zeros((128, 128), F32)
    with jax.named_scope("w_n"):
        arrive((n_copy, st_copy))
    settle(merge(nbuf, sbuf, 64), 0, 32)
    with jax.named_scope("w_f"):
        arrive((f_copy, gt_copy))
    settle(merge(fbuf, gbuf, 48), 32, 24)
    at32[:, 56:64, :] = jnp.zeros((2, 8, HD), F32)
    sq32[56:64, :] = jnp.zeros((8, 128), F32)
    for d in range(ng):
        for h in range(2):
            abst[d, :, h * HD : (h + 1) * HD] = at32[h, pl.ds(d, 8, stride=8), :]
        sqst[d] = sq32[pl.ds(d, 8, stride=8), :]

    def ab_copy(k):
        d = (g + k) % ng
        return remote(abst.at[d], ab.at[g], ab_s.at[k], ab_r.at[k], in_group(d))

    def sq_copy(k):
        d = (g + k) % ng
        return remote(sqst.at[d], sqr.at[g], sq_s.at[k], sq_r.at[k], twin(d))

    for k in range(ng):
        if k:
            ab_copy(k).start()
        sq_copy(k).start()
    ab[g] = abst[g]
    with jax.named_scope("w_ab"):
        for k in range(1, ng):
            ab_copy(k).wait_recv()
        for k in range(ng):
            sq_copy(k).wait_recv()
    pieces = [ab[d] for d in range(ng)]
    square = sqr[0]
    for d in range(1, ng):
        square = square + sqr[d]
    square = square[:, 0:1]
    for piece in pieces:
        square = square + jnp.sum(piece * piece, axis=1, keepdims=True)
    inv = lax.rsqrt(square / (H * HD) + 1e-06)
    for d in range(ng):
        cols = slice(d * 256, (d + 1) * 256)
        done = pieces[d] * inv * gain[:, cols]
        span_out[:, cols] = done[0:4].astype(BF16)
        first_out[:, cols] = done[4:6].astype(BF16)
        second_out[:, cols] = done[6:7].astype(BF16)

    def drain(k, _):
        for copy in (n_copy, st_copy, f_copy, gt_copy):
            copy(k, b, home).wait_send()
        return 0

    with jax.named_scope("drain"):
        lax.fori_loop(1, nb, drain, 0)
        for k in range(nz):
            if k:
                qz_copy(k).wait_send()
            qx_copy(k).wait_send()
        for k in range(ng):
            if k:
                qa_copy(k).wait_send()
                ex_copy(k).wait_send()
                ab_copy(k).wait_send()
            sq_copy(k).wait_send()
        for n in range(2):
            for k in range(ny):
                if k:
                    kv_copy(n, k).wait_send()
                relay(n, k).wait_send()


def per_device(
    dims, cache_k, cache_v, span_q, span_k, span_v, span_frames, action_ids, action_table,
    frame_q, frame_k, frame_v, revealed_k, revealed_v, mask_k, mask_v, pass1_idx, pass2_idx,
    out_gain,
):
    nx, nz = dims
    nb = nx * nz
    ng = NY * NC
    rows = cache_k.shape[0]
    cols = span_k.shape[1]
    dma = pltpu.SemaphoreType.DMA
    vm = pltpu.VMEM
    anywhere = pl.BlockSpec(memory_space=pl.ANY)
    local = pl.BlockSpec(memory_space=pltpu.VMEM)
    outs = [jax.ShapeDtypeStruct((n, span_q.shape[1]), BF16) for n in (4, 2, 1)]
    row = lambda v: v.reshape(1, -1)
    small = (
        span_q, span_k, span_v, row(span_frames), row(action_ids), action_table, frame_q, frame_k,
        frame_v, revealed_k, revealed_v, mask_k, mask_v, row(pass1_idx), row(pass2_idx),
        row(out_gain),
    )
    return pl.pallas_call(
        functools.partial(kernel, dims),
        out_shape=outs,
        in_specs=[anywhere] * 18,
        out_specs=[local] * 3,
        scratch_shapes=[vm(v.shape, v.dtype) for v in small]
        + [
            vm((2, ng, rows, HD), BF16),
            vm((2, ng, 16, HD), BF16),
            vm((2, NY, 16, HD), BF16),
            vm((16, cols), F32),
            vm((8, span_q.shape[1]), F32),
            vm((ng, 8, 256), BF16),
            vm((ng, 8, 256), BF16),
            vm((2, 64, HD), F32),
            vm((nb, 64, 256), BF16),
            vm((32 * nb, 32 * nb), BF16),
            vm((nb, 48, HD), BF16),
            vm((nb, 32, 128), F32),
            vm((8, 128), F32),
            vm((nb, 64, HD), BF16),
            vm((nb, 64, HD), BF16),
            vm((nb, 48, HD), BF16),
            vm((nb, 48, HD), BF16),
            vm((nb, 2, 128), F32),
            vm((nb, 2, 128), F32),
            vm((nb, 2, 128), F32),
            vm((nb, 2, 128), F32),
            vm((128, 128), F32),
            vm((2, 64, HD), F32),
            vm((64, 128), F32),
            vm((ng, 8, 256), F32),
            vm((ng, 8, 256), F32),
            vm((ng, 8, 128), F32),
            vm((ng, 8, 128), F32),
            dma((18,)),
            dma((ng,)),
            dma((ng,)),
            dma((2, NY)),
            dma((2, 2 * NY)),
            dma((ng,)),
            dma((ng,)),
            dma((2, NY)),
            dma((nz,)),
            dma((nz,)),
            dma((nz,)),
            dma((nz,)),
        ]
        + [dma((nb,))] * 8
        + [dma((ng,))] * 4,
        compiler_params=pltpu.CompilerParams(
            collective_id=0, has_side_effects=True, vmem_limit_bytes=60 << 20
        ),
        name="frame_attention",
    )(cache_k, cache_v, *small)


def solution(mesh):
    both = P("ctx", "tp")
    in_specs = (
        both, both, both, both, both, P(), P("ctx"), P(None, "tp"), both, both, both, both, both,
        P("tp"), P("tp"), P(), P(), P("tp"),
    )
    nz = NZ
    nx = mesh.shape["ctx"] // (NY * NC * nz)
    return jax.shard_map(
        functools.partial(per_device, (nx, nz)),
        mesh=mesh,
        in_specs=in_specs,
        out_specs=(both, both, both),
        check_vma=False,
    )
```

```python
import functools

import jax
import jax.numpy as jnp
from jax import lax
from jax.experimental import pallas as pl
from jax.experimental.pallas import tpu as pltpu
from jax.sharding import PartitionSpec as P

H = 32
HD = 128
NX, NY, NZ, NC = 2, 4, 8, 2
LOG2E = 1.4426950408889634
MESH = pl.DeviceIdType.MESH
F32 = jnp.float32
BF16 = jnp.bfloat16
NEG = -1e30


def kernel(
    dims,
    ck, cv, *refs,
):
    nx, nz = dims
    hbm, refs = refs[:16], refs[16:]
    out, refs = refs[0], refs[1:]
    vmem, refs = refs[:16], refs[16:]
    sq, sk, sv, frames, ids, table, fq, fk, fv, rk, rv, mk, mv, p1, p2, gain = vmem
    (
        kv, ex, exst, ex32, q32, qa, qast, t32, qbuf, hot, qfs, qf, kfr,
        nst, nbuf, fst, fbuf, sst, sbuf, gst, gbuf, m32, at32, sq32, abst, ab, sqst, sqr,
        loc_sem, qa_s, qa_r, kv_s, kv_r, ex_s, ex_r, kvr_s,
        qz_s, qz_r, qx_s, qx_r, n_s, n_r, st_s, st_r, f_s, f_r, gt_s, gt_r,
        ab_s, ab_r, sq_s, sq_r,
    ) = refs
    nb = nx * nz
    ny, nc = NY, NC
    ng = ny * nc
    total = ny * nc * nb * 4
    scale = HD ** (-0.5) * LOG2E
    me = lax.axis_index("ctx")
    tp = lax.axis_index("tp")
    c = me % nc
    z = (me // nc) % nz
    y = (me // (nc * nz)) % ny
    x = me // (nc * nz * ny)
    g = y * nc + c
    b = x * nz + z

    def ctx_of(xx, yy, zz, cc):
        return ((xx * ny + yy) * nz + zz) * nc + cc

    def in_group(d):
        return {"ctx": ctx_of(x, d // nc, z, d % nc), "tp": tp}

    def twin(d):
        return {"ctx": ctx_of(x, d // nc, z, d % nc), "tp": 1 - tp}

    def at_block(xx, zz):
        return {"ctx": ctx_of(xx, y, zz, c), "tp": tp}

    def remote(src, dst, ss, rs, dev):
        return pltpu.make_async_remote_copy(
            src_ref=src, dst_ref=dst, send_sem=ss, recv_sem=rs, device_id=dev, device_id_type=MESH
        )

    barrier = pltpu.get_barrier_semaphore()

    def greet(k, _):
        pl.semaphore_signal(barrier, inc=1, device_id=in_group((g + k) % ng), device_id_type=MESH)
        return 0

    def greet_twin(k, _):
        pl.semaphore_signal(barrier, inc=1, device_id=twin((g + k) % ng), device_id_type=MESH)
        return 0

    def greet_across(j, _):
        dev = at_block(x, (z + j) % nz)
        pl.semaphore_signal(barrier, inc=1, device_id=dev, device_id_type=MESH)
        return 0

    lax.fori_loop(1, nz, greet_across, 0)
    pl.semaphore_signal(barrier, inc=1, device_id=at_block((x + 1) % nx, z), device_id_type=MESH)
    lax.fori_loop(1, ng, greet, 0)
    lax.fori_loop(0, ng, greet_twin, 0)

    def load(i):
        return pltpu.make_async_copy(hbm[i], vmem[i], loc_sem.at[2 + i])

    for i in (0, 6, 1, 2, 3, 4, 5, 7, 8, 9, 10, 11, 12, 13, 14, 15):
        load(i).start()
    col = pl.ds(pl.multiple_of(y * HD, HD), HD)
    own_k = pltpu.make_async_copy(ck.at[:, col], kv.at[0, g], loc_sem.at[0])
    own_v = pltpu.make_async_copy(cv.at[:, col], kv.at[1, g], loc_sem.at[1])
    own_k.start()
    own_v.start()

    load(0).wait()
    load(6).wait()
    q32[0:4, :] = sq[...].astype(F32)
    q32[4:8, :] = fq[...].astype(F32)
    for d in range(ng):
        qast[d] = q32[:, d * 256 : (d + 1) * 256].astype(BF16)

    def qa_copy(k):
        d = (g + k) % ng
        return remote(qast.at[d], qa.at[g], qa_s.at[k], qa_r.at[k], in_group(d))

    def ex_copy(k):
        d = (g + k) % ng
        return remote(exst.at[:, d // nc], ex.at[:, g], ex_s.at[k], ex_r.at[k], in_group(d))

    def kv_copy(n, k):
        d = (g + nc * k) % ng
        head = pl.ds(pl.multiple_of((d // nc) * HD, HD), HD)
        source = (ck, cv)[n]
        return remote(
            source.at[:, head], kv.at[n, g], kv_s.at[n, k], kv_r.at[n, k], in_group(d)
        )

    def relay(n, k):
        origin = (g + ng - nc * k) % ng
        peer = y * nc + 1 - c
        src = ((ck, cv)[n].at[:, col]) if k == 0 else kv.at[n, origin]
        return remote(src, kv.at[n, origin], kvr_s.at[n, k], kv_r.at[n, ny + k], in_group(peer))

    with jax.named_scope("w_barrier"):
        pl.semaphore_wait(barrier, nz + (ng - 1) + ng)

    for k in range(1, ng):
        qa_copy(k).start()
    for k in range(1, ny):
        for n in range(2):
            kv_copy(n, k).start()
    for n in range(2):
        relay(n, 0).start()
    qa[g] = qast[g]

    for i in (1, 2, 3, 4, 5, 7, 8, 9, 10, 11, 12, 13, 14, 15):
        load(i).wait()

    row4 = lax.broadcasted_iota(jnp.int32, (4, 4), 0)
    lane4 = lax.broadcasted_iota(jnp.int32, (4, 4), 1)
    ids_col = jnp.sum(jnp.where(row4 == lane4, ids[...], 0), axis=1, keepdims=True)
    action = jnp.zeros(sk.shape, F32)
    tab = table[...].astype(F32)
    for a in range(table.shape[0]):
        action = jnp.where(ids_col == a, tab[a : a + 1, :], action)
    pos = me * 4 + lax.broadcasted_iota(jnp.int32, (4, 1), 0)
    in1 = jnp.sum(jnp.where(p1[...] == pos, 1.0, 0.0), axis=1, keepdims=True) > 0.5
    in2 = jnp.sum(jnp.where(p2[...] == pos, 1.0, 0.0), axis=1, keepdims=True) > 0.5

    def masked(frame, revealed, mask):
        shape = frame.shape
        frame, revealed = frame[...].astype(F32), revealed[...].astype(F32)
        mask = jnp.broadcast_to(mask[...].astype(F32).reshape(1, -1), shape)
        first = jnp.where(in1, mask, frame)
        second = jnp.where(in2, mask, jnp.where(in1, revealed, frame))
        return first, second

    for n, (span, pair) in enumerate(
        (
            (sk[...].astype(F32) + action, masked(fk, rk, mk)),
            (sv[...].astype(F32), masked(fv, rv, mv)),
        )
    ):
        ex32[0:4, :] = span
        ex32[4:8, :] = pair[0]
        ex32[8:12, :] = pair[1]
        ex32[12:16, :] = jnp.zeros_like(span)
        for d in range(ny):
            exst[n, d] = ex32[:, d * HD : (d + 1) * HD].astype(BF16)
    for k in range(1, ng):
        ex_copy(k).start()
    for n in range(2):
        ex[n, g] = exst[n, y]

    with jax.named_scope("w_qa"):
        for k in range(1, ng):
            qa_copy(k).wait_recv()
    for h in range(2):
        cols = slice(h * HD, (h + 1) * HD)
        t32[h] = qa[:, :, cols].astype(F32).reshape(64, HD)
        for i in range(4):
            pair = [t32[h, pl.ds(2 * i + r, 8, stride=8), :] for r in range(2)]
            qbuf[b, 16 * i : 16 * i + 16, cols] = jnp.concatenate(pair, axis=0).astype(BF16)

    def off(k):
        near = k // 2
        return near + 1 if k % 2 else (nz - near) % nz

    def off_dyn(k):
        near = k // 2
        odd = k % 2
        return (odd * (near + 1) + (1 - odd) * (nz - near)) % nz

    def qz_copy(k):
        return remote(
            qbuf.at[b], qbuf.at[b], qz_s.at[k], qz_r.at[k], at_block(x, (z + off(k)) % nz)
        )

    def qx_copy(k):
        blk = x * nz + (z + nz - off(k)) % nz
        return remote(
            qbuf.at[blk], qbuf.at[blk], qx_s.at[k], qx_r.at[k], at_block((x + 1) % nx, z)
        )

    for k in range(1, nz):
        qz_copy(k).start()
    qx_copy(0).start()

    rows = 32 * nb

    def owners(width):
        r = lax.broadcasted_iota(jnp.int32, (rows, width), 0)
        ll = lax.broadcasted_iota(jnp.int32, (rows, width), 1)
        rb, rt, ro = r >> 5, (r >> 3) & 3, r & 7
        rx = jnp.where(rb >= nz, 1, 0)
        rz = rb - nz * rx
        return ll, rt, ((rx * ny + (ro >> 1)) * nz + rz) * nc + (ro & 1)

    lane, rt, owner = owners(total)
    fr = jnp.broadcast_to(frames[...].astype(F32), (rows, total))
    qframe = jnp.sum(jnp.where(lane == 4 * owner + rt, fr, 0.0), axis=1, keepdims=True)
    qf[...] = jnp.broadcast_to(qframe, (rows, 128)).reshape(nb, 32, 128)

    key = lax.broadcasted_iota(jnp.int32, (total, 128), 0)
    kl = lax.broadcasted_iota(jnp.int32, (total, 128), 1)
    ko, ks = kl >> 4, kl & 15
    kwant = 4 * (((x * ny + (ko >> 1)) * nz + z) * nc + (ko & 1)) + ks
    khit = jnp.where((key == kwant) & (ks < 4), 1.0, 0.0).astype(BF16)
    fr8 = jnp.broadcast_to(frames[...].astype(F32), (8, total)).astype(BF16)
    kfr[...] = jnp.dot(fr8, khit, preferred_element_type=F32)

    l1, t1, o1 = owners(p1.shape[1])
    l2, t2, o2 = owners(p2.shape[1])
    v1 = jnp.broadcast_to(p1[...].astype(F32), l1.shape)
    v2 = jnp.broadcast_to(p2[...].astype(F32), l2.shape)
    found = jnp.sum(
        jnp.where((l1 == 2 * o1 + t1) & (t1 < 2), v1, 0.0), axis=1, keepdims=True
    ) + jnp.sum(jnp.where((l2 == o2) & (t2 == 2), v2, 0.0), axis=1, keepdims=True)
    found = found.astype(jnp.int32)
    bits = nz.bit_length() - 1
    dev = found >> 2
    from_z = (dev >> 1) & (nz - 1)
    from_y = (dev >> (1 + bits)) & (ny - 1)
    from_x = dev >> (3 + bits)
    place = (from_x * nz + from_z) * 32 + (found & 3) * 8 + from_y * nc + (dev & 1)
    lanes = lax.broadcasted_iota(jnp.int32, (rows, rows), 1)
    hot[...] = jnp.where(lanes == place, 1.0, 0.0).astype(BF16)

    with jax.named_scope("w_kv"):
        for k in range(1, ny):
            for n in range(2):
                kv_copy(n, k).wait_recv()
                relay(n, k).start()

    def from_z_half(k):
        qz_copy(k).wait_recv()
        qx_copy(k).start()

    with jax.named_scope("w_qz"):
        for k in range(1, 4):
            from_z_half(k)

    with jax.named_scope("w_relay"):
        for k in range(1, ng):
            ex_copy(k).wait_recv()
        own_k.wait()
        own_v.wait()
        for k in range(ny):
            for n in range(2):
                relay(n, k).wait_recv()

    keys = kv.shape[1] * kv.shape[2]
    nt = (((1,), (1,)), ((), ()))

    def dest(k):
        return (x + k // nz) % nx, (z + nz - off_dyn(k % nz)) % nz

    def attention(q, bias):
        s1 = lax.dot_general(q, kv[0].reshape(keys, HD), nt, preferred_element_type=F32)
        s2 = lax.dot_general(q, ex[0].reshape(128, HD), nt, preferred_element_type=F32) + bias
        m = jnp.maximum(s1.max(axis=1, keepdims=True), s2.max(axis=1, keepdims=True))
        w1 = jnp.exp2((s1 - m) * scale)
        w2 = jnp.exp2((s2 - m) * scale)
        tot = w1.sum(axis=1, keepdims=True) + w2.sum(axis=1, keepdims=True)
        o = jnp.dot(w1.astype(BF16), kv[1].reshape(keys, HD), preferred_element_type=F32)
        o = o + jnp.dot(w2.astype(BF16), ex[1].reshape(128, HD), preferred_element_type=F32)
        return o, jnp.where(lax.broadcasted_iota(jnp.int32, o.shape, 1) == 0, m, tot)

    def n_copy(k, blk, dev):
        return remote(nst.at[blk], nbuf.at[b], n_s.at[k], n_r.at[k], dev)

    def st_copy(k, blk, dev):
        return remote(sst.at[blk], sbuf.at[b], st_s.at[k], st_r.at[k], dev)

    def f_copy(k, blk, dev):
        return remote(fst.at[blk], fbuf.at[b], f_s.at[k], f_r.at[k], dev)

    def gt_copy(k, blk, dev):
        return remote(gst.at[blk], gbuf.at[b], gt_s.at[k], gt_r.at[k], dev)

    def put_stats(stats, into, blks):
        turned = stats.T[0:8, :]
        for q in range(4):
            tile = turned[:, (q // 2) * 128 : (q // 2) * 128 + 128]
            if q % 2:
                tile = pltpu.roll(tile, 64, 1)
            into[blks[q]] = tile[0:2]

    def push(s, blks, dests, copies):
        for q in range(4):
            dev = at_block(*dests[q])

            def go(q=q, dev=dev):
                for copy in copies:
                    copy(4 * s + q, blks[q], dev).start()

            if q == 0:
                pl.when(s > 0)(go)
            else:
                go()

    slot32 = lax.broadcasted_iota(jnp.int32, (32, 128), 1) & 15
    half = nz // 4

    def spans(s, _):
        for u in range(half, 2 * half):

            @pl.when(s == u)
            def _(u=u):
                for q in range(4):
                    qx_copy(4 * (u - half) + q).wait_recv()

        for u in range(1, half):

            @pl.when(s == u)
            def _(u=u):
                for q in range(4):
                    from_z_half(4 * u + q)

        dests = [dest(4 * s + q) for q in range(4)]
        blks = [xx * nz + zz for xx, zz in dests]
        parts, bias = [], []
        for blk in blks:
            mask = jnp.where((slot32 < 4) & (kfr[0:1, :] <= qf[blk]), 0.0, NEG)
            bias += [mask, mask]
            parts += [qbuf[blk, 0:32, 0:HD], qbuf[blk, 0:32, HD : 2 * HD]]
        o, stats = attention(jnp.concatenate(parts, axis=0), jnp.concatenate(bias, axis=0))
        for q in range(4):
            nst[blks[q]] = o[64 * q : 64 * q + 64].astype(BF16)
        put_stats(stats, sst, blks)
        push(s, blks, dests, (n_copy, st_copy))
        return 0

    with jax.named_scope("spans"):
        lax.fori_loop(0, 2 * half, spans, 0)

    frame_q = qbuf[:, 32:64, :].reshape(rows, 256)
    picked = jnp.dot(hot[...], frame_q, preferred_element_type=F32)
    for blk in range(nb):
        both = [picked[32 * blk : 32 * blk + 24, h * HD : (h + 1) * HD] for h in range(2)]
        qfs[blk] = jnp.concatenate(both, axis=0).astype(BF16)

    r48 = lax.broadcasted_iota(jnp.int32, (48, 128), 0)
    slot48 = lax.broadcasted_iota(jnp.int32, (48, 128), 1) & 15
    t48 = (jnp.where(r48 >= 24, r48 - 24, r48)) >> 3
    allowed = (slot48 < 4) | ((slot48 < 8) & (t48 < 2)) | (
        (slot48 >= 8) & (slot48 < 12) & (t48 == 2)
    )
    mask48 = jnp.where(allowed, 0.0, NEG)

    def picks(i, _):
        s = 2 * half - 1 - i
        dests = [dest(4 * s + q) for q in range(4)]
        blks = [xx * nz + zz for xx, zz in dests]
        q_rows = jnp.concatenate([qfs[blk] for blk in blks], axis=0)
        o, stats = attention(q_rows, jnp.concatenate([mask48] * 4, axis=0))
        pad = jnp.zeros((16, 128), F32)
        padded = []
        for q in range(4):
            fst[blks[q]] = o[48 * q : 48 * q + 48].astype(BF16)
            padded += [stats[48 * q : 48 * q + 48], pad]
        put_stats(jnp.concatenate(padded, axis=0), gst, blks)
        push(s, blks, dests, (f_copy, gt_copy))
        return 0

    with jax.named_scope("picks"):
        lax.fori_loop(0, 2 * half, picks, 0)
    nbuf[b] = nst[b]
    sbuf[b] = sst[b]
    fbuf[b] = fst[b]
    gbuf[b] = gst[b]
    home = at_block((x + 1) % nx, z)

    def arrive(copies):
        def body(k, _):
            for copy in copies:
                copy(k, b, home).wait_recv()
            return 0

        lax.fori_loop(1, nb, body, 0)

    def merge(data, stats, n):
        for s in range(nb):
            m32[2 * s : 2 * s + 2, :] = stats[s]
        st = m32[...].T[0:n]
        lanes = lax.broadcasted_iota(jnp.int32, (n, 128), 1)
        is_m = ((lanes & 1) == 0) & (lanes < 2 * nb)
        top = jnp.max(jnp.where(is_m, st, NEG), axis=1, keepdims=True)
        tot = pltpu.roll(st, 127, 1)
        e = jnp.where(is_m, jnp.exp2((jnp.where(is_m, st, top) - top) * scale), 0.0)
        den = jnp.sum(jnp.where(is_m, e * tot, 0.0), axis=1, keepdims=True)
        w = e / den
        acc = jnp.zeros((n, HD), F32)
        for s in range(nb):
            acc = acc + w[:, 2 * s : 2 * s + 1] * data[s].astype(F32)
        return acc

    def settle(acc, low, n):
        squares = jnp.sum(acc * acc, axis=1, keepdims=True)
        at32[0, low : low + n, :] = acc[0:n]
        at32[1, low : low + n, :] = acc[n : 2 * n]
        sq32[low : low + n, :] = jnp.broadcast_to(squares[0:n] + squares[n : 2 * n], (n, 128))

    m32[...] = jnp.zeros((128, 128), F32)
    with jax.named_scope("w_n"):
        arrive((n_copy, st_copy))
    settle(merge(nbuf, sbuf, 64), 0, 32)
    with jax.named_scope("w_f"):
        arrive((f_copy, gt_copy))
    settle(merge(fbuf, gbuf, 48), 32, 24)
    at32[:, 56:64, :] = jnp.zeros((2, 8, HD), F32)
    sq32[56:64, :] = jnp.zeros((8, 128), F32)
    for d in range(ng):
        for h in range(2):
            abst[d, :, h * HD : (h + 1) * HD] = at32[h, pl.ds(d, 8, stride=8), :]
        sqst[d] = sq32[pl.ds(d, 8, stride=8), :]

    def ab_copy(k):
        d = (g + k) % ng
        return remote(abst.at[d], ab.at[g], ab_s.at[k], ab_r.at[k], in_group(d))

    def sq_copy(k):
        d = (g + k) % ng
        return remote(sqst.at[d], sqr.at[g], sq_s.at[k], sq_r.at[k], twin(d))

    for k in range(ng):
        if k:
            ab_copy(k).start()
        sq_copy(k).start()
    ab[g] = abst[g]
    with jax.named_scope("w_ab"):
        for k in range(1, ng):
            ab_copy(k).wait_recv()
        for k in range(ng):
            sq_copy(k).wait_recv()
    pieces = [ab[d] for d in range(ng)]
    square = sqr[0]
    for d in range(1, ng):
        square = square + sqr[d]
    square = square[:, 0:1]
    for piece in pieces:
        square = square + jnp.sum(piece * piece, axis=1, keepdims=True)
    inv = lax.rsqrt(square / (H * HD) + 1e-06)
    for d in range(ng):
        cols = slice(d * 256, (d + 1) * 256)
        out[:, cols] = pieces[d] * inv * gain[:, cols]

    def drain(k, _):
        for copy in (n_copy, st_copy, f_copy, gt_copy):
            copy(k, b, home).wait_send()
        return 0

    with jax.named_scope("drain"):
        lax.fori_loop(1, nb, drain, 0)
        for k in range(nz):
            if k:
                qz_copy(k).wait_send()
            qx_copy(k).wait_send()
        for k in range(ng):
            if k:
                qa_copy(k).wait_send()
                ex_copy(k).wait_send()
                ab_copy(k).wait_send()
            sq_copy(k).wait_send()
        for n in range(2):
            for k in range(ny):
                if k:
                    kv_copy(n, k).wait_send()
                relay(n, k).wait_send()


def spread(done, span_out, first_out, second_out, span, first, second, sems):
    span[...] = done[0:4, :].astype(BF16)
    first[...] = done[4:6, :].astype(BF16)
    second[...] = done[6:7, :].astype(BF16)
    pairs = ((span, span_out), (first, first_out), (second, second_out))
    copies = [pltpu.make_async_copy(a, o, sems.at[i]) for i, (a, o) in enumerate(pairs)]
    for copy in copies:
        copy.start()
    for copy in copies:
        copy.wait()


def per_device(
    dims, cache_k, cache_v, span_q, span_k, span_v, span_frames, action_ids, action_table,
    frame_q, frame_k, frame_v, revealed_k, revealed_v, mask_k, mask_v, pass1_idx, pass2_idx,
    out_gain,
):
    nx, nz = dims
    nb = nx * nz
    ng = NY * NC
    rows = cache_k.shape[0]
    cols = span_k.shape[1]
    dma = pltpu.SemaphoreType.DMA
    vm = pltpu.VMEM
    anywhere = pl.BlockSpec(memory_space=pl.ANY)
    local = pl.BlockSpec(memory_space=pltpu.VMEM)
    outs = [jax.ShapeDtypeStruct((n, span_q.shape[1]), BF16) for n in (4, 2, 1)]
    row = lambda v: v.reshape(1, -1)
    small = (
        span_q, span_k, span_v, row(span_frames), row(action_ids), action_table, frame_q, frame_k,
        frame_v, revealed_k, revealed_v, mask_k, mask_v, row(pass1_idx), row(pass2_idx),
        row(out_gain),
    )
    done = pl.pallas_call(
        functools.partial(kernel, dims),
        out_shape=pltpu.VMEM((8, span_q.shape[1]), F32),
        in_specs=[anywhere] * 18,
        out_specs=local,
        scratch_shapes=[vm(v.shape, v.dtype) for v in small]
        + [
            vm((2, ng, rows, HD), BF16),
            vm((2, ng, 16, HD), BF16),
            vm((2, NY, 16, HD), BF16),
            vm((16, cols), F32),
            vm((8, span_q.shape[1]), F32),
            vm((ng, 8, 256), BF16),
            vm((ng, 8, 256), BF16),
            vm((2, 64, HD), F32),
            vm((nb, 64, 256), BF16),
            vm((32 * nb, 32 * nb), BF16),
            vm((nb, 48, HD), BF16),
            vm((nb, 32, 128), F32),
            vm((8, 128), F32),
            vm((nb, 64, HD), BF16),
            vm((nb, 64, HD), BF16),
            vm((nb, 48, HD), BF16),
            vm((nb, 48, HD), BF16),
            vm((nb, 2, 128), F32),
            vm((nb, 2, 128), F32),
            vm((nb, 2, 128), F32),
            vm((nb, 2, 128), F32),
            vm((128, 128), F32),
            vm((2, 64, HD), F32),
            vm((64, 128), F32),
            vm((ng, 8, 256), F32),
            vm((ng, 8, 256), F32),
            vm((ng, 8, 128), F32),
            vm((ng, 8, 128), F32),
            dma((18,)),
            dma((ng,)),
            dma((ng,)),
            dma((2, NY)),
            dma((2, 2 * NY)),
            dma((ng,)),
            dma((ng,)),
            dma((2, NY)),
            dma((nz,)),
            dma((nz,)),
            dma((nz,)),
            dma((nz,)),
        ]
        + [dma((nb,))] * 8
        + [dma((ng,))] * 4,
        compiler_params=pltpu.CompilerParams(
            collective_id=0, has_side_effects=True, vmem_limit_bytes=60 << 20
        ),
        name="frame_attention",
    )(cache_k, cache_v, *small)
    return pl.pallas_call(
        spread,
        out_shape=outs,
        in_specs=[local],
        out_specs=[anywhere] * 3,
        scratch_shapes=[vm(v.shape, v.dtype) for v in outs] + [dma((3,))],
        name="spread",
    )(pltpu.with_memory_space_constraint(done, pltpu.VMEM))


def solution(mesh):
    both = P("ctx", "tp")
    in_specs = (
        both, both, both, both, both, P(), P("ctx"), P(None, "tp"), both, both, both, both, both,
        P("tp"), P("tp"), P(), P(), P("tp"),
    )
    nz = NZ
    nx = mesh.shape["ctx"] // (NY * NC * nz)
    return jax.shard_map(
        functools.partial(per_device, (nx, nz)),
        mesh=mesh,
        in_specs=in_specs,
        out_specs=(both, both, both),
        check_vma=False,
    )
```

```python
import functools

import jax
import jax.numpy as jnp
from jax import lax
from jax.experimental import pallas as pl
from jax.experimental.pallas import tpu as pltpu
from jax.sharding import PartitionSpec as P

H = 32
HD = 128
NX, NY, NZ, NC = 2, 4, 8, 2
LOG2E = 1.4426950408889634
MESH = pl.DeviceIdType.MESH
F32 = jnp.float32
BF16 = jnp.bfloat16
NEG = -1e30


def kernel(
    dims,
    ck, cv, *refs,
):
    nx, nz = dims
    hbm, refs = refs[:16], refs[16:]
    out, refs = refs[0], refs[1:]
    vmem, refs = refs[:16], refs[16:]
    sq, sk, sv, frames, ids, table, fq, fk, fv, rk, rv, mk, mv, p1, p2, gain = vmem
    (
        kv, ex, exst, ex32, q32, qa, qast, t32, qbuf, hot, qfs, qf, kfr,
        nst, nbuf, fst, fbuf, sst, sbuf, gst, gbuf, m32, at32, sq32, abst, ab, sqst, sqr,
        loc_sem, qa_s, qa_r, kv_s, kv_r, ex_s, ex_r,
        q_s, qz_r, qx_r, n_s, n_r, st_s, st_r, f_s, f_r, gt_s, gt_r,
        ab_s, ab_r, sq_s, sq_r, zr, tr,
    ) = refs
    nb = nx * nz
    ny, nc = NY, NC
    ng = ny * nc
    total = ny * nc * nb * 4
    scale = HD ** (-0.5) * LOG2E
    me = lax.axis_index("ctx")
    tp = lax.axis_index("tp")
    c = me % nc
    z = (me // nc) % nz
    y = (me // (nc * nz)) % ny
    x = me // (nc * nz * ny)
    g = y * nc + c
    b = x * nz + z

    def ctx_of(xx, yy, zz, cc):
        return ((xx * ny + yy) * nz + zz) * nc + cc

    def in_group(d):
        return {"ctx": ctx_of(x, d // nc, z, d % nc), "tp": tp}

    def twin(d):
        return {"ctx": ctx_of(x, d // nc, z, d % nc), "tp": 1 - tp}

    def at_block(xx, zz):
        return {"ctx": ctx_of(xx, y, zz, c), "tp": tp}

    def remote(src, dst, ss, rs, dev):
        return pltpu.make_async_remote_copy(
            src_ref=src, dst_ref=dst, send_sem=ss, recv_sem=rs, device_id=dev, device_id_type=MESH
        )

    def whole(part, ss, rs):
        return remote(part, part, ss, rs, at_block((x + 1) % nx, z))

    barrier = pltpu.get_barrier_semaphore()

    def greet(k, _):
        pl.semaphore_signal(barrier, inc=1, device_id=in_group((g + k) % ng), device_id_type=MESH)
        return 0

    pl.semaphore_signal(barrier, inc=1, device_id=at_block(x, (z + 1) % nz), device_id_type=MESH)
    pl.semaphore_signal(
        barrier, inc=1, device_id=at_block(x, (z + nz - 1) % nz), device_id_type=MESH
    )
    pl.semaphore_signal(barrier, inc=1, device_id=at_block((x + 1) % nx, z), device_id_type=MESH)
    pl.semaphore_signal(barrier, inc=1, device_id=twin(g), device_id_type=MESH)
    lax.fori_loop(1, ng, greet, 0)

    def tell(n):
        for way in range(2):
            zz = (z + 1 + way * (nz - 2)) % nz
            pl.semaphore_signal(
                zr.at[way, n], inc=1, device_id=at_block(x, zz), device_id_type=MESH
            )

    def told(n):
        for way in range(2):
            pl.semaphore_wait(zr.at[way, n], 1)

    def load(i):
        return pltpu.make_async_copy(hbm[i], vmem[i], loc_sem.at[2 + i])

    for i in (0, 6, 1, 2, 3, 4, 5, 7, 8, 9, 10, 11, 12, 13, 14, 15):
        load(i).start()
    col = pl.ds(pl.multiple_of(y * HD, HD), HD)
    own_k = pltpu.make_async_copy(ck.at[:, col], kv.at[0, g], loc_sem.at[0])
    own_v = pltpu.make_async_copy(cv.at[:, col], kv.at[1, g], loc_sem.at[1])
    own_k.start()
    own_v.start()

    load(0).wait()
    load(6).wait()
    q32[0:4, :] = sq[...].astype(F32)
    q32[4:8, :] = fq[...].astype(F32)
    for d in range(ng):
        qast[d] = q32[:, d * 256 : (d + 1) * 256].astype(BF16)

    def qa_copy(k):
        d = (g + k) % ng
        return remote(qast.at[d], qa.at[g], qa_s, qa_r, in_group(d))

    def ex_copy(k):
        d = (g + k) % ng
        return remote(exst.at[:, d // nc], ex.at[:, g], ex_s, ex_r, in_group(d))

    def kv_copy(n, k):
        d = (g + nc * k) % ng
        head = pl.ds(pl.multiple_of((d // nc) * HD, HD), HD)
        source = (ck, cv)[n]
        return remote(
            source.at[:, head], kv.at[n, g], kv_s, kv_r.at[n, k], in_group(d)
        )

    def relay(n, k):
        origin = (g + ng - nc * k) % ng
        peer = y * nc + 1 - c
        src = ((ck, cv)[n].at[:, col]) if k == 0 else kv.at[n, origin]
        return remote(src, kv.at[n, origin], kv_s, kv_r.at[n, ny + k], in_group(peer))

    with jax.named_scope("w_barrier"):
        pl.semaphore_wait(barrier, 4 + (ng - 1))

    reach = nz // 2 - 1
    tell(0)
    for k in range(1, ng):
        qa_copy(k).start()
    pl.semaphore_signal(tr, inc=1, device_id=twin(g), device_id_type=MESH)
    for k in range(1, ny):
        for n in range(2):
            kv_copy(n, k).start()
    for n in range(2):
        relay(n, 0).start()
    qa[g] = qast[g]

    for n in range(reach - 1):
        told(n)
        tell(n + 1)

    with jax.named_scope("w_qa"):
        whole(qa.at[pl.ds(0, ng - 1)], qa_s, qa_r).wait_recv()
    for h in range(2):
        cols = slice(h * HD, (h + 1) * HD)
        t32[h] = qa[:, :, cols].astype(F32).reshape(64, HD)
        for i in range(4):
            pair = [t32[h, pl.ds(2 * i + r, 8, stride=8), :] for r in range(2)]
            qbuf[b, 16 * i : 16 * i + 16, cols] = jnp.concatenate(pair, axis=0).astype(BF16)

    def off(k):
        near = k // 2
        return near + 1 if k % 2 else (nz - near) % nz

    def off_dyn(k):
        near = k // 2
        odd = k % 2
        return (odd * (near + 1) + (1 - odd) * (nz - near)) % nz

    def qz_copy(k):
        return remote(
            qbuf.at[b], qbuf.at[b], q_s, qz_r.at[k], at_block(x, (z + off(k)) % nz)
        )

    def qx_copy(k):
        blk = x * nz + (z + nz - off(k)) % nz
        return remote(
            qbuf.at[blk], qbuf.at[blk], q_s, qx_r.at[k], at_block((x + 1) % nx, z)
        )

    qx_copy(0).start()
    for k in range(1, nz - 1):
        qz_copy(k).start()
    told(reach - 1)
    qz_copy(nz - 1).start()

    for i in (1, 2, 3, 4, 5, 7, 8, 9, 10, 11, 12, 13, 14, 15):
        load(i).wait()

    row4 = lax.broadcasted_iota(jnp.int32, (4, 4), 0)
    lane4 = lax.broadcasted_iota(jnp.int32, (4, 4), 1)
    ids_col = jnp.sum(jnp.where(row4 == lane4, ids[...], 0), axis=1, keepdims=True)
    action = jnp.zeros(sk.shape, F32)
    tab = table[...].astype(F32)
    for a in range(table.shape[0]):
        action = jnp.where(ids_col == a, tab[a : a + 1, :], action)
    pos = me * 4 + lax.broadcasted_iota(jnp.int32, (4, 1), 0)
    in1 = jnp.sum(jnp.where(p1[...] == pos, 1.0, 0.0), axis=1, keepdims=True) > 0.5
    in2 = jnp.sum(jnp.where(p2[...] == pos, 1.0, 0.0), axis=1, keepdims=True) > 0.5

    def masked(frame, revealed, mask):
        shape = frame.shape
        frame, revealed = frame[...].astype(F32), revealed[...].astype(F32)
        mask = jnp.broadcast_to(mask[...].astype(F32).reshape(1, -1), shape)
        first = jnp.where(in1, mask, frame)
        second = jnp.where(in2, mask, jnp.where(in1, revealed, frame))
        return first, second

    for n, (span, pair) in enumerate(
        (
            (sk[...].astype(F32) + action, masked(fk, rk, mk)),
            (sv[...].astype(F32), masked(fv, rv, mv)),
        )
    ):
        ex32[0:4, :] = span
        ex32[4:8, :] = pair[0]
        ex32[8:12, :] = pair[1]
        ex32[12:16, :] = jnp.zeros_like(span)
        for d in range(ny):
            exst[n, d] = ex32[:, d * HD : (d + 1) * HD].astype(BF16)
    for k in range(1, ng):
        ex_copy(k).start()
    for n in range(2):
        ex[n, g] = exst[n, y]


    rows = 32 * nb

    def owners(width):
        r = lax.broadcasted_iota(jnp.int32, (rows, width), 0)
        ll = lax.broadcasted_iota(jnp.int32, (rows, width), 1)
        rb, rt, ro = r >> 5, (r >> 3) & 3, r & 7
        rx = jnp.where(rb >= nz, 1, 0)
        rz = rb - nz * rx
        return ll, rt, ((rx * ny + (ro >> 1)) * nz + rz) * nc + (ro & 1)

    lane, rt, owner = owners(total)
    fr = jnp.broadcast_to(frames[...].astype(F32), (rows, total))
    qframe = jnp.sum(jnp.where(lane == 4 * owner + rt, fr, 0.0), axis=1, keepdims=True)
    qf[...] = jnp.broadcast_to(qframe, (rows, 128)).reshape(nb, 32, 128)

    key = lax.broadcasted_iota(jnp.int32, (total, 128), 0)
    kl = lax.broadcasted_iota(jnp.int32, (total, 128), 1)
    ko, ks = kl >> 4, kl & 15
    kwant = 4 * (((x * ny + (ko >> 1)) * nz + z) * nc + (ko & 1)) + ks
    khit = jnp.where((key == kwant) & (ks < 4), 1.0, 0.0).astype(BF16)
    fr8 = jnp.broadcast_to(frames[...].astype(F32), (8, total)).astype(BF16)
    kfr[...] = jnp.dot(fr8, khit, preferred_element_type=F32)

    l1, t1, o1 = owners(p1.shape[1])
    l2, t2, o2 = owners(p2.shape[1])
    v1 = jnp.broadcast_to(p1[...].astype(F32), l1.shape)
    v2 = jnp.broadcast_to(p2[...].astype(F32), l2.shape)
    found = jnp.sum(
        jnp.where((l1 == 2 * o1 + t1) & (t1 < 2), v1, 0.0), axis=1, keepdims=True
    ) + jnp.sum(jnp.where((l2 == o2) & (t2 == 2), v2, 0.0), axis=1, keepdims=True)
    found = found.astype(jnp.int32)
    bits = nz.bit_length() - 1
    dev = found >> 2
    from_z = (dev >> 1) & (nz - 1)
    from_y = (dev >> (1 + bits)) & (ny - 1)
    from_x = dev >> (3 + bits)
    place = (from_x * nz + from_z) * 32 + (found & 3) * 8 + from_y * nc + (dev & 1)
    lanes = lax.broadcasted_iota(jnp.int32, (rows, rows), 1)
    hot[...] = jnp.where(lanes == place, 1.0, 0.0).astype(BF16)

    with jax.named_scope("w_kv"):
        for k in range(1, ny):
            for n in range(2):
                kv_copy(n, k).wait_recv()
                relay(n, k).start()

    def from_z_half(k):
        qz_copy(k).wait_recv()
        qx_copy(k).start()

    with jax.named_scope("w_qz"):
        for k in range(1, 4):
            from_z_half(k)

    with jax.named_scope("w_relay"):
        whole(ex.at[:, pl.ds(0, ng - 1)], ex_s, ex_r).wait_recv()
        own_k.wait()
        own_v.wait()
        for k in range(ny):
            for n in range(2):
                relay(n, k).wait_recv()

    keys = kv.shape[1] * kv.shape[2]
    nt = (((1,), (1,)), ((), ()))

    def dest(k):
        return (x + k // nz) % nx, (z + nz - off_dyn(k % nz)) % nz

    def scores(q, bias):
        s1 = lax.dot_general(q, kv[0].reshape(keys, HD), nt, preferred_element_type=F32)
        s2 = lax.dot_general(q, ex[0].reshape(128, HD), nt, preferred_element_type=F32) + bias
        return s1, s2

    def weigh(s1, s2):
        m = jnp.maximum(s1.max(axis=1, keepdims=True), s2.max(axis=1, keepdims=True))
        w1 = jnp.exp2((s1 - m) * scale)
        w2 = jnp.exp2((s2 - m) * scale)
        tot = w1.sum(axis=1, keepdims=True) + w2.sum(axis=1, keepdims=True)
        o = jnp.dot(w1.astype(BF16), kv[1].reshape(keys, HD), preferred_element_type=F32)
        o = o + jnp.dot(w2.astype(BF16), ex[1].reshape(128, HD), preferred_element_type=F32)
        return o, jnp.where(lax.broadcasted_iota(jnp.int32, o.shape, 1) == 0, m, tot)

    def attention(tiles):
        return [weigh(*pair) for pair in [scores(*tile) for tile in tiles]]

    def n_copy(k, blk, dev):
        return remote(nst.at[blk], nbuf.at[b], n_s, n_r, dev)

    def st_copy(k, blk, dev):
        return remote(sst.at[blk], sbuf.at[b], st_s, st_r, dev)

    def f_copy(k, blk, dev):
        return remote(fst.at[blk], fbuf.at[b], f_s, f_r, dev)

    def gt_copy(k, blk, dev):
        return remote(gst.at[blk], gbuf.at[b], gt_s, gt_r, dev)

    def put_stats(stats, into, blks):
        turned = stats.T[0:8, :]
        for q in range(4):
            tile = turned[:, (q // 2) * 128 : (q // 2) * 128 + 128]
            if q % 2:
                tile = pltpu.roll(tile, 64, 1)
            into[blks[q]] = tile[0:2]

    def push(s, blks, dests, copies):
        for q in range(4):
            dev = at_block(*dests[q])

            def go(q=q, dev=dev):
                for copy in copies:
                    copy(4 * s + q, blks[q], dev).start()

            if q == 0:
                pl.when(s > 0)(go)
            else:
                go()

    slot32 = lax.broadcasted_iota(jnp.int32, (32, 128), 1) & 15
    half = nz // 4

    def spans(s, _):
        for u in range(half, 2 * half):

            @pl.when(s == u)
            def _(u=u):
                with jax.named_scope(f"wx{u}"):
                    for q in range(4):
                        qx_copy(4 * (u - half) + q).wait_recv()

        for u in range(1, half):

            @pl.when(s == u)
            def _(u=u):
                with jax.named_scope(f"wz{u}"):
                    for q in range(4):
                        from_z_half(4 * u + q)

        dests = [dest(4 * s + q) for q in range(4)]
        blks = [xx * nz + zz for xx, zz in dests]
        parts, bias = [], []
        for blk in blks:
            mask = jnp.where((slot32 < 4) & (kfr[0:1, :] <= qf[blk]), 0.0, NEG)
            bias += [mask, mask]
            parts += [qbuf[blk, 0:32, 0:HD], qbuf[blk, 0:32, HD : 2 * HD]]
        done = attention(
            [
                (jnp.concatenate(parts[u : u + 4], axis=0), jnp.concatenate(bias[u : u + 4], axis=0))
                for u in (0, 4)
            ]
        )
        for q in range(4):
            low = 64 * (q % 2)
            nst[blks[q]] = done[q // 2][0][low : low + 64].astype(BF16)
        put_stats(jnp.concatenate([st for _, st in done], axis=0), sst, blks)
        push(s, blks, dests, (n_copy, st_copy))
        return 0

    with jax.named_scope("spans"):
        lax.fori_loop(0, 2 * half, spans, 0)

    frame_q = qbuf[:, 32:64, :].reshape(rows, 256)
    picked = jnp.dot(hot[...], frame_q, preferred_element_type=F32)
    for blk in range(nb):
        both = [picked[32 * blk : 32 * blk + 24, h * HD : (h + 1) * HD] for h in range(2)]
        qfs[blk] = jnp.concatenate(both, axis=0).astype(BF16)

    r48 = lax.broadcasted_iota(jnp.int32, (48, 128), 0)
    slot48 = lax.broadcasted_iota(jnp.int32, (48, 128), 1) & 15
    t48 = (jnp.where(r48 >= 24, r48 - 24, r48)) >> 3
    allowed = (slot48 < 4) | ((slot48 < 8) & (t48 < 2)) | (
        (slot48 >= 8) & (slot48 < 12) & (t48 == 2)
    )
    mask48 = jnp.where(allowed, 0.0, NEG)

    mask192 = jnp.concatenate([mask48] * 4, axis=0)

    def picks(i, _):
        steps = [2 * half - 1 - 2 * i, 2 * half - 2 - 2 * i]
        dests = [[dest(4 * s + q) for q in range(4)] for s in steps]
        blks = [[xx * nz + zz for xx, zz in group] for group in dests]
        done = attention(
            [(jnp.concatenate([qfs[blk] for blk in group], axis=0), mask192) for group in blks]
        )
        pad = jnp.zeros((16, 128), F32)
        for s, group, where, (o, stats) in zip(steps, blks, dests, done):
            padded = []
            for q in range(4):
                fst[group[q]] = o[48 * q : 48 * q + 48].astype(BF16)
                padded += [stats[48 * q : 48 * q + 48], pad]
            put_stats(jnp.concatenate(padded, axis=0), gst, group)
        for s, group, where in zip(steps, blks, dests):
            push(s, group, where, (f_copy, gt_copy))
        return 0

    with jax.named_scope("picks"):
        lax.fori_loop(0, half, picks, 0)
    nbuf[b] = nst[b]
    sbuf[b] = sst[b]
    fbuf[b] = fst[b]
    gbuf[b] = gst[b]
    most = pl.ds(0, nb - 1)

    def merge(data, stats, n):
        for s in range(nb):
            m32[2 * s : 2 * s + 2, :] = stats[s]
        st = m32[...].T[0:n]
        lanes = lax.broadcasted_iota(jnp.int32, (n, 128), 1)
        is_m = ((lanes & 1) == 0) & (lanes < 2 * nb)
        top = jnp.max(jnp.where(is_m, st, NEG), axis=1, keepdims=True)
        tot = pltpu.roll(st, 127, 1)
        e = jnp.where(is_m, jnp.exp2((jnp.where(is_m, st, top) - top) * scale), 0.0)
        den = jnp.sum(jnp.where(is_m, e * tot, 0.0), axis=1, keepdims=True)
        w = e / den
        acc = jnp.zeros((n, HD), F32)
        for s in range(nb):
            acc = acc + w[:, 2 * s : 2 * s + 1] * data[s].astype(F32)
        return acc

    def settle(acc, low, n):
        squares = jnp.sum(acc * acc, axis=1, keepdims=True)
        at32[0, low : low + n, :] = acc[0:n]
        at32[1, low : low + n, :] = acc[n : 2 * n]
        sq32[low : low + n, :] = jnp.broadcast_to(squares[0:n] + squares[n : 2 * n], (n, 128))

    m32[...] = jnp.zeros((128, 128), F32)
    with jax.named_scope("w_n"):
        whole(nbuf.at[most], n_s, n_r).wait_recv()
        whole(sbuf.at[most], st_s, st_r).wait_recv()
    settle(merge(nbuf, sbuf, 64), 0, 32)
    with jax.named_scope("w_f"):
        whole(fbuf.at[most], f_s, f_r).wait_recv()
        whole(gbuf.at[most], gt_s, gt_r).wait_recv()
    settle(merge(fbuf, gbuf, 48), 32, 24)
    at32[:, 56:64, :] = jnp.zeros((2, 8, HD), F32)
    sq32[56:64, :] = jnp.zeros((8, 128), F32)
    for d in range(ng):
        for h in range(2):
            abst[d, :, h * HD : (h + 1) * HD] = at32[h, pl.ds(d, 8, stride=8), :]
        sqst[d] = sq32[pl.ds(d, 8, stride=8), :]

    pl.semaphore_wait(tr, 1)

    def ab_copy(k):
        d = (g + k) % ng
        return remote(abst.at[d], ab.at[g], ab_s, ab_r, in_group(d))

    def sq_copy(k):
        d = (g + k) % ng
        return remote(sqst.at[d], sqr.at[g], sq_s, sq_r, twin(d))

    for k in range(ng):
        if k:
            ab_copy(k).start()
        sq_copy(k).start()
    ab[g] = abst[g]
    with jax.named_scope("w_ab"):
        whole(ab.at[pl.ds(0, ng - 1)], ab_s, ab_r).wait_recv()
        whole(sqr, sq_s, sq_r).wait_recv()
    pieces = [ab[d] for d in range(ng)]
    square = sqr[0]
    for d in range(1, ng):
        square = square + sqr[d]
    square = square[:, 0:1]
    for piece in pieces:
        square = square + jnp.sum(piece * piece, axis=1, keepdims=True)
    inv = lax.rsqrt(square / (H * HD) + 1e-06)
    for d in range(ng):
        cols = slice(d * 256, (d + 1) * 256)
        out[:, cols] = pieces[d] * inv * gain[:, cols]

    with jax.named_scope("drain"):
        for buf, ss, rs in (
            (nbuf, n_s, n_r), (sbuf, st_s, st_r), (fbuf, f_s, f_r), (gbuf, gt_s, gt_r),
            (qbuf, q_s, qz_r.at[0]),
        ):
            whole(buf.at[most], ss, rs).wait_send()
        few = pl.ds(0, ng - 1)
        whole(qa.at[few], qa_s, qa_r).wait_send()
        whole(ab.at[few], ab_s, ab_r).wait_send()
        whole(ex.at[:, few], ex_s, ex_r).wait_send()
        whole(sqr, sq_s, sq_r).wait_send()
        whole(kv.at[:, few], kv_s, kv_r.at[0, 0]).wait_send()


def spread(done, span_out, first_out, second_out, span, first, second, sems):
    span[...] = done[0:4, :].astype(BF16)
    first[...] = done[4:6, :].astype(BF16)
    second[...] = done[6:7, :].astype(BF16)
    pairs = ((span, span_out), (first, first_out), (second, second_out))
    copies = [pltpu.make_async_copy(a, o, sems.at[i]) for i, (a, o) in enumerate(pairs)]
    for copy in copies:
        copy.start()
    for copy in copies:
        copy.wait()


def per_device(
    dims, cache_k, cache_v, span_q, span_k, span_v, span_frames, action_ids, action_table,
    frame_q, frame_k, frame_v, revealed_k, revealed_v, mask_k, mask_v, pass1_idx, pass2_idx,
    out_gain,
):
    nx, nz = dims
    nb = nx * nz
    ng = NY * NC
    rows = cache_k.shape[0]
    cols = span_k.shape[1]
    dma = pltpu.SemaphoreType.DMA
    vm = pltpu.VMEM
    anywhere = pl.BlockSpec(memory_space=pl.ANY)
    local = pl.BlockSpec(memory_space=pltpu.VMEM)
    outs = [jax.ShapeDtypeStruct((n, span_q.shape[1]), BF16) for n in (4, 2, 1)]
    row = lambda v: v.reshape(1, -1)
    small = (
        span_q, span_k, span_v, row(span_frames), row(action_ids), action_table, frame_q, frame_k,
        frame_v, revealed_k, revealed_v, mask_k, mask_v, row(pass1_idx), row(pass2_idx),
        row(out_gain),
    )
    done = pl.pallas_call(
        functools.partial(kernel, dims),
        out_shape=pltpu.VMEM((8, span_q.shape[1]), F32),
        in_specs=[anywhere] * 18,
        out_specs=local,
        scratch_shapes=[vm(v.shape, v.dtype) for v in small]
        + [
            vm((2, ng, rows, HD), BF16),
            vm((2, ng, 16, HD), BF16),
            vm((2, NY, 16, HD), BF16),
            vm((16, cols), F32),
            vm((8, span_q.shape[1]), F32),
            vm((ng, 8, 256), BF16),
            vm((ng, 8, 256), BF16),
            vm((2, 64, HD), F32),
            vm((nb, 64, 256), BF16),
            vm((32 * nb, 32 * nb), BF16),
            vm((nb, 48, HD), BF16),
            vm((nb, 32, 128), F32),
            vm((8, 128), F32),
            vm((nb, 64, HD), BF16),
            vm((nb, 64, HD), BF16),
            vm((nb, 48, HD), BF16),
            vm((nb, 48, HD), BF16),
            vm((nb, 2, 128), F32),
            vm((nb, 2, 128), F32),
            vm((nb, 2, 128), F32),
            vm((nb, 2, 128), F32),
            vm((128, 128), F32),
            vm((2, 64, HD), F32),
            vm((64, 128), F32),
            vm((ng, 8, 256), F32),
            vm((ng, 8, 256), F32),
            vm((ng, 8, 128), F32),
            vm((ng, 8, 128), F32),
            dma((18,)),
            dma,
            dma,
            dma,
            dma((2, 2 * NY)),
            dma,
            dma,
            dma,
            dma((nz,)),
            dma((nz,)),
        ]
        + [dma] * 12
        + [pltpu.SemaphoreType.REGULAR((2, nz // 2 - 1)), pltpu.SemaphoreType.REGULAR],
        compiler_params=pltpu.CompilerParams(
            collective_id=0, has_side_effects=True, vmem_limit_bytes=60 << 20
        ),
        name="frame_attention",
    )(cache_k, cache_v, *small)
    return pl.pallas_call(
        spread,
        out_shape=outs,
        in_specs=[local],
        out_specs=[anywhere] * 3,
        scratch_shapes=[vm(v.shape, v.dtype) for v in outs] + [dma((3,))],
        name="spread",
    )(pltpu.with_memory_space_constraint(done, pltpu.VMEM))


def solution(mesh):
    both = P("ctx", "tp")
    in_specs = (
        both, both, both, both, both, P(), P("ctx"), P(None, "tp"), both, both, both, both, both,
        P("tp"), P("tp"), P(), P(), P("tp"),
    )
    nz = NZ
    nx = mesh.shape["ctx"] // (NY * NC * nz)
    return jax.shard_map(
        functools.partial(per_device, (nx, nz)),
        mesh=mesh,
        in_specs=in_specs,
        out_specs=(both, both, both),
        check_vma=False,
    )
```

```python
import functools

import jax
import jax.numpy as jnp
from jax import lax
from jax.experimental import pallas as pl
from jax.experimental.pallas import tpu as pltpu
from jax.sharding import PartitionSpec as P

H = 32
HD = 128
NX, NY, NZ, NC = 2, 4, 8, 2
LOG2E = 1.4426950408889634
MESH = pl.DeviceIdType.MESH
F32 = jnp.float32
BF16 = jnp.bfloat16
NEG = -1e30


def kernel(
    dims,
    ck, cv, *refs,
):
    nx, nz = dims
    hbm, refs = refs[:16], refs[16:]
    out, refs = refs[0], refs[1:]
    vmem, refs = refs[:16], refs[16:]
    sq, sk, sv, frames, ids, table, fq, fk, fv, rk, rv, mk, mv, p1, p2, gain = vmem
    (
        kv, ex, exst, ex32, q32, qa, qast, t32, qbuf, hot, qfs, qf, kfr,
        nst, nbuf, fst, fbuf, sst, sbuf, gst, gbuf, m32, at32, sq32, abst, ab, sqst, sqr,
        loc_sem, qa_s, qa_r, kv_s, kv_r, ex_s, ex_r,
        q_s, qz_r, qx_r, n_s, n_r, st_s, st_r, f_s, f_r, gt_s, gt_r,
        ab_s, ab_r, sq_s, sq_r, zr, tr,
    ) = refs
    nb = nx * nz
    ny, nc = NY, NC
    ng = ny * nc
    total = ny * nc * nb * 4
    scale = HD ** (-0.5) * LOG2E
    me = lax.axis_index("ctx")
    tp = lax.axis_index("tp")
    c = me % nc
    z = (me // nc) % nz
    y = (me // (nc * nz)) % ny
    x = me // (nc * nz * ny)
    g = y * nc + c
    b = x * nz + z

    def ctx_of(xx, yy, zz, cc):
        return ((xx * ny + yy) * nz + zz) * nc + cc

    def in_group(d):
        return {"ctx": ctx_of(x, d // nc, z, d % nc), "tp": tp}

    def twin(d):
        return {"ctx": ctx_of(x, d // nc, z, d % nc), "tp": 1 - tp}

    def at_block(xx, zz):
        return {"ctx": ctx_of(xx, y, zz, c), "tp": tp}

    def remote(src, dst, ss, rs, dev):
        return pltpu.make_async_remote_copy(
            src_ref=src, dst_ref=dst, send_sem=ss, recv_sem=rs, device_id=dev, device_id_type=MESH
        )

    def whole(part, ss, rs):
        return remote(part, part, ss, rs, at_block((x + 1) % nx, z))

    barrier = pltpu.get_barrier_semaphore()

    def greet(k, _):
        pl.semaphore_signal(barrier, inc=1, device_id=in_group((g + k) % ng), device_id_type=MESH)
        return 0

    pl.semaphore_signal(barrier, inc=1, device_id=at_block(x, (z + 1) % nz), device_id_type=MESH)
    pl.semaphore_signal(
        barrier, inc=1, device_id=at_block(x, (z + nz - 1) % nz), device_id_type=MESH
    )
    pl.semaphore_signal(barrier, inc=1, device_id=at_block((x + 1) % nx, z), device_id_type=MESH)
    pl.semaphore_signal(barrier, inc=1, device_id=twin(g), device_id_type=MESH)
    lax.fori_loop(1, ng, greet, 0)

    def tell(n):
        for way in range(2):
            zz = (z + 1 + way * (nz - 2)) % nz
            pl.semaphore_signal(
                zr.at[way, n], inc=1, device_id=at_block(x, zz), device_id_type=MESH
            )

    def told(n):
        for way in range(2):
            pl.semaphore_wait(zr.at[way, n], 1)

    def load(i):
        return pltpu.make_async_copy(hbm[i], vmem[i], loc_sem.at[2 + i])

    for i in (0, 6, 1, 2, 3, 4, 5, 7, 8, 9, 10, 11, 12, 13, 14, 15):
        load(i).start()
    col = pl.ds(pl.multiple_of(y * HD, HD), HD)
    own_k = pltpu.make_async_copy(ck.at[:, col], kv.at[0, g], loc_sem.at[0])
    own_v = pltpu.make_async_copy(cv.at[:, col], kv.at[1, g], loc_sem.at[1])
    own_k.start()
    own_v.start()

    load(0).wait()
    load(6).wait()
    q32[0:4, :] = sq[...].astype(F32)
    q32[4:8, :] = fq[...].astype(F32)
    for d in range(ng):
        qast[d] = q32[:, d * 256 : (d + 1) * 256].astype(BF16)

    def qa_copy(k):
        d = (g + k) % ng
        return remote(qast.at[d], qa.at[g], qa_s, qa_r, in_group(d))

    def ex_copy(k):
        d = (g + k) % ng
        return remote(exst.at[:, d // nc], ex.at[:, g], ex_s, ex_r, in_group(d))

    def kv_copy(n, k):
        d = (g + nc * k) % ng
        head = pl.ds(pl.multiple_of((d // nc) * HD, HD), HD)
        source = (ck, cv)[n]
        return remote(
            source.at[:, head], kv.at[n, g], kv_s, kv_r.at[n, k], in_group(d)
        )

    def relay(n, k):
        origin = (g + ng - nc * k) % ng
        peer = y * nc + 1 - c
        src = ((ck, cv)[n].at[:, col]) if k == 0 else kv.at[n, origin]
        return remote(src, kv.at[n, origin], kv_s, kv_r.at[n, ny + k], in_group(peer))

    with jax.named_scope("w_barrier"):
        pl.semaphore_wait(barrier, 4 + (ng - 1))

    reach = nz // 2 - 1
    tell(0)
    for k in range(1, ng):
        qa_copy(k).start()
    pl.semaphore_signal(tr, inc=1, device_id=twin(g), device_id_type=MESH)
    for k in range(1, ny):
        kv_copy(0, k).start()
    relay(0, 0).start()
    qa[g] = qast[g]

    told(0)
    tell(1)
    for k in range(1, ny):
        kv_copy(1, k).start()
    relay(1, 0).start()
    for n in range(1, reach - 1):
        told(n)
        tell(n + 1)

    with jax.named_scope("w_qa"):
        whole(qa.at[pl.ds(0, ng - 1)], qa_s, qa_r).wait_recv()
    for h in range(2):
        cols = slice(h * HD, (h + 1) * HD)
        t32[h] = qa[:, :, cols].astype(F32).reshape(64, HD)
        for i in range(4):
            pair = [t32[h, pl.ds(2 * i + r, 8, stride=8), :] for r in range(2)]
            qbuf[b, 16 * i : 16 * i + 16, cols] = jnp.concatenate(pair, axis=0).astype(BF16)

    def off(k):
        near = k // 2
        return near + 1 if k % 2 else (nz - near) % nz

    def off_dyn(k):
        near = k // 2
        odd = k % 2
        return (odd * (near + 1) + (1 - odd) * (nz - near)) % nz

    def qz_copy(k):
        return remote(
            qbuf.at[b], qbuf.at[b], q_s, qz_r.at[k], at_block(x, (z + off(k)) % nz)
        )

    def qx_copy(k):
        blk = x * nz + (z + nz - off(k)) % nz
        return remote(
            qbuf.at[blk], qbuf.at[blk], q_s, qx_r.at[k], at_block((x + 1) % nx, z)
        )

    qx_copy(0).start()
    for k in range(1, nz - 1):
        qz_copy(k).start()
    told(reach - 1)
    qz_copy(nz - 1).start()

    for i in (1, 2, 3, 4, 5, 7, 8, 9, 10, 11, 12, 13, 14, 15):
        load(i).wait()

    row4 = lax.broadcasted_iota(jnp.int32, (4, 4), 0)
    lane4 = lax.broadcasted_iota(jnp.int32, (4, 4), 1)
    ids_col = jnp.sum(jnp.where(row4 == lane4, ids[...], 0), axis=1, keepdims=True)
    action = jnp.zeros(sk.shape, F32)
    tab = table[...].astype(F32)
    for a in range(table.shape[0]):
        action = jnp.where(ids_col == a, tab[a : a + 1, :], action)
    pos = me * 4 + lax.broadcasted_iota(jnp.int32, (4, 1), 0)
    in1 = jnp.sum(jnp.where(p1[...] == pos, 1.0, 0.0), axis=1, keepdims=True) > 0.5
    in2 = jnp.sum(jnp.where(p2[...] == pos, 1.0, 0.0), axis=1, keepdims=True) > 0.5

    def masked(frame, revealed, mask):
        shape = frame.shape
        frame, revealed = frame[...].astype(F32), revealed[...].astype(F32)
        mask = jnp.broadcast_to(mask[...].astype(F32).reshape(1, -1), shape)
        first = jnp.where(in1, mask, frame)
        second = jnp.where(in2, mask, jnp.where(in1, revealed, frame))
        return first, second

    for n, (span, pair) in enumerate(
        (
            (sk[...].astype(F32) + action, masked(fk, rk, mk)),
            (sv[...].astype(F32), masked(fv, rv, mv)),
        )
    ):
        ex32[0:4, :] = span
        ex32[4:8, :] = pair[0]
        ex32[8:12, :] = pair[1]
        ex32[12:16, :] = jnp.zeros_like(span)
        for d in range(ny):
            exst[n, d] = ex32[:, d * HD : (d + 1) * HD].astype(BF16)
    for k in range(1, ng):
        ex_copy(k).start()
    for n in range(2):
        ex[n, g] = exst[n, y]


    rows = 32 * nb

    def owners(width):
        r = lax.broadcasted_iota(jnp.int32, (rows, width), 0)
        ll = lax.broadcasted_iota(jnp.int32, (rows, width), 1)
        rb, rt, ro = r >> 5, (r >> 3) & 3, r & 7
        rx = jnp.where(rb >= nz, 1, 0)
        rz = rb - nz * rx
        return ll, rt, ((rx * ny + (ro >> 1)) * nz + rz) * nc + (ro & 1)

    lane, rt, owner = owners(total)
    fr = jnp.broadcast_to(frames[...].astype(F32), (rows, total))
    qframe = jnp.sum(jnp.where(lane == 4 * owner + rt, fr, 0.0), axis=1, keepdims=True)
    qf[...] = jnp.broadcast_to(qframe, (rows, 128)).reshape(nb, 32, 128)

    key = lax.broadcasted_iota(jnp.int32, (total, 128), 0)
    kl = lax.broadcasted_iota(jnp.int32, (total, 128), 1)
    ko, ks = kl >> 4, kl & 15
    kwant = 4 * (((x * ny + (ko >> 1)) * nz + z) * nc + (ko & 1)) + ks
    khit = jnp.where((key == kwant) & (ks < 4), 1.0, 0.0).astype(BF16)
    fr8 = jnp.broadcast_to(frames[...].astype(F32), (8, total)).astype(BF16)
    kfr[...] = jnp.dot(fr8, khit, preferred_element_type=F32)

    l1, t1, o1 = owners(p1.shape[1])
    l2, t2, o2 = owners(p2.shape[1])
    v1 = jnp.broadcast_to(p1[...].astype(F32), l1.shape)
    v2 = jnp.broadcast_to(p2[...].astype(F32), l2.shape)
    found = jnp.sum(
        jnp.where((l1 == 2 * o1 + t1) & (t1 < 2), v1, 0.0), axis=1, keepdims=True
    ) + jnp.sum(jnp.where((l2 == o2) & (t2 == 2), v2, 0.0), axis=1, keepdims=True)
    found = found.astype(jnp.int32)
    bits = nz.bit_length() - 1
    dev = found >> 2
    from_z = (dev >> 1) & (nz - 1)
    from_y = (dev >> (1 + bits)) & (ny - 1)
    from_x = dev >> (3 + bits)
    place = (from_x * nz + from_z) * 32 + (found & 3) * 8 + from_y * nc + (dev & 1)
    lanes = lax.broadcasted_iota(jnp.int32, (rows, rows), 1)
    hot[...] = jnp.where(lanes == place, 1.0, 0.0).astype(BF16)

    with jax.named_scope("w_kv"):
        for k in range(1, ny):
            for n in range(2):
                kv_copy(n, k).wait_recv()
                relay(n, k).start()

    def from_z_half(k):
        qz_copy(k).wait_recv()
        qx_copy(k).start()

    with jax.named_scope("w_qz"):
        for k in range(1, 4):
            from_z_half(k)

    with jax.named_scope("w_relay"):
        whole(ex.at[:, pl.ds(0, ng - 1)], ex_s, ex_r).wait_recv()
        own_k.wait()
        own_v.wait()
        for k in range(ny):
            for n in range(2):
                relay(n, k).wait_recv()

    keys = kv.shape[1] * kv.shape[2]
    nt = (((1,), (1,)), ((), ()))

    def dest(k):
        return (x + k // nz) % nx, (z + nz - off_dyn(k % nz)) % nz

    def scores(q, bias):
        s1 = lax.dot_general(q, kv[0].reshape(keys, HD), nt, preferred_element_type=F32)
        s2 = lax.dot_general(q, ex[0].reshape(128, HD), nt, preferred_element_type=F32) + bias
        return s1, s2

    def weigh(s1, s2):
        m = jnp.maximum(s1.max(axis=1, keepdims=True), s2.max(axis=1, keepdims=True))
        w1 = jnp.exp2((s1 - m) * scale)
        w2 = jnp.exp2((s2 - m) * scale)
        tot = w1.sum(axis=1, keepdims=True) + w2.sum(axis=1, keepdims=True)
        o = jnp.dot(w1.astype(BF16), kv[1].reshape(keys, HD), preferred_element_type=F32)
        o = o + jnp.dot(w2.astype(BF16), ex[1].reshape(128, HD), preferred_element_type=F32)
        return o, jnp.where(lax.broadcasted_iota(jnp.int32, o.shape, 1) == 0, m, tot)

    def attention(tiles):
        return [weigh(*pair) for pair in [scores(*tile) for tile in tiles]]

    def n_copy(k, blk, dev):
        return remote(nst.at[blk], nbuf.at[b], n_s, n_r, dev)

    def st_copy(k, blk, dev):
        return remote(sst.at[blk], sbuf.at[b], st_s, st_r, dev)

    def f_copy(k, blk, dev):
        return remote(fst.at[blk], fbuf.at[b], f_s, f_r, dev)

    def gt_copy(k, blk, dev):
        return remote(gst.at[blk], gbuf.at[b], gt_s, gt_r, dev)

    def put_stats(stats, into, blks):
        turned = stats.T[0:8, :]
        for q in range(4):
            tile = turned[:, (q // 2) * 128 : (q // 2) * 128 + 128]
            if q % 2:
                tile = pltpu.roll(tile, 64, 1)
            into[blks[q]] = tile[0:2]

    def push(s, blks, dests, copies):
        for q in range(4):
            dev = at_block(*dests[q])

            def go(q=q, dev=dev):
                for copy in copies:
                    copy(4 * s + q, blks[q], dev).start()

            if q == 0:
                pl.when(s > 0)(go)
            else:
                go()

    slot32 = lax.broadcasted_iota(jnp.int32, (32, 128), 1) & 15
    half = nz // 4

    def spans(s, _):
        for u in range(half, 2 * half):

            @pl.when(s == u)
            def _(u=u):
                with jax.named_scope(f"wx{u}"):
                    for q in range(4):
                        qx_copy(4 * (u - half) + q).wait_recv()

        for u in range(1, half):

            @pl.when(s == u)
            def _(u=u):
                with jax.named_scope(f"wz{u}"):
                    for q in range(4):
                        from_z_half(4 * u + q)

        dests = [dest(4 * s + q) for q in range(4)]
        blks = [xx * nz + zz for xx, zz in dests]
        parts, bias = [], []
        for blk in blks:
            mask = jnp.where((slot32 < 4) & (kfr[0:1, :] <= qf[blk]), 0.0, NEG)
            bias += [mask, mask]
            parts += [qbuf[blk, 0:32, 0:HD], qbuf[blk, 0:32, HD : 2 * HD]]
        done = attention(
            [
                (jnp.concatenate(parts[u : u + 4], axis=0), jnp.concatenate(bias[u : u + 4], axis=0))
                for u in (0, 4)
            ]
        )
        for q in range(4):
            low = 64 * (q % 2)
            nst[blks[q]] = done[q // 2][0][low : low + 64].astype(BF16)
        put_stats(jnp.concatenate([st for _, st in done], axis=0), sst, blks)
        push(s, blks, dests, (st_copy, n_copy))
        return 0

    with jax.named_scope("spans"):
        lax.fori_loop(0, 2 * half, spans, 0)

    frame_q = qbuf[:, 32:64, :].reshape(rows, 256)
    picked = jnp.dot(hot[...], frame_q, preferred_element_type=F32)
    for blk in range(nb):
        both = [picked[32 * blk : 32 * blk + 24, h * HD : (h + 1) * HD] for h in range(2)]
        qfs[blk] = jnp.concatenate(both, axis=0).astype(BF16)

    r48 = lax.broadcasted_iota(jnp.int32, (48, 128), 0)
    slot48 = lax.broadcasted_iota(jnp.int32, (48, 128), 1) & 15
    t48 = (jnp.where(r48 >= 24, r48 - 24, r48)) >> 3
    allowed = (slot48 < 4) | ((slot48 < 8) & (t48 < 2)) | (
        (slot48 >= 8) & (slot48 < 12) & (t48 == 2)
    )
    mask48 = jnp.where(allowed, 0.0, NEG)

    mask192 = jnp.concatenate([mask48] * 4, axis=0)

    def picks(i, _):
        steps = [2 * half - 1 - i, half - 1 - i]
        dests = [[dest(4 * s + q) for q in range(4)] for s in steps]
        blks = [[xx * nz + zz for xx, zz in group] for group in dests]
        done = attention(
            [(jnp.concatenate([qfs[blk] for blk in group], axis=0), mask192) for group in blks]
        )
        pad = jnp.zeros((16, 128), F32)
        for s, group, where, (o, stats) in zip(steps, blks, dests, done):
            padded = []
            for q in range(4):
                fst[group[q]] = o[48 * q : 48 * q + 48].astype(BF16)
                padded += [stats[48 * q : 48 * q + 48], pad]
            put_stats(jnp.concatenate(padded, axis=0), gst, group)
        for s, group, where in zip(steps, blks, dests):
            push(s, group, where, (gt_copy, f_copy))
        return 0

    with jax.named_scope("picks"):
        lax.fori_loop(0, half, picks, 0)
    nbuf[b] = nst[b]
    sbuf[b] = sst[b]
    fbuf[b] = fst[b]
    gbuf[b] = gst[b]
    most = pl.ds(0, nb - 1)

    def shares(stats, n):
        for s in range(nb):
            m32[2 * s : 2 * s + 2, :] = stats[s]
        st = m32[...].T[0:n]
        lanes = lax.broadcasted_iota(jnp.int32, (n, 128), 1)
        is_m = ((lanes & 1) == 0) & (lanes < 2 * nb)
        top = jnp.max(jnp.where(is_m, st, NEG), axis=1, keepdims=True)
        tot = pltpu.roll(st, 127, 1)
        e = jnp.where(is_m, jnp.exp2((jnp.where(is_m, st, top) - top) * scale), 0.0)
        den = jnp.sum(jnp.where(is_m, e * tot, 0.0), axis=1, keepdims=True)
        return e / den

    def merge(data, w, n):
        acc = jnp.zeros((n, HD), F32)
        for s in range(nb):
            acc = acc + w[:, 2 * s : 2 * s + 1] * data[s].astype(F32)
        return acc

    def settle(acc, low, n):
        squares = jnp.sum(acc * acc, axis=1, keepdims=True)
        at32[0, low : low + n, :] = acc[0:n]
        at32[1, low : low + n, :] = acc[n : 2 * n]
        sq32[low : low + n, :] = jnp.broadcast_to(squares[0:n] + squares[n : 2 * n], (n, 128))

    m32[...] = jnp.zeros((128, 128), F32)
    with jax.named_scope("w_st"):
        whole(sbuf.at[most], st_s, st_r).wait_recv()
    w_span = shares(sbuf, 64)
    with jax.named_scope("w_n"):
        whole(nbuf.at[most], n_s, n_r).wait_recv()
    settle(merge(nbuf, w_span, 64), 0, 32)
    with jax.named_scope("w_gt"):
        whole(gbuf.at[most], gt_s, gt_r).wait_recv()
    w_frame = shares(gbuf, 48)
    with jax.named_scope("w_f"):
        whole(fbuf.at[most], f_s, f_r).wait_recv()
    settle(merge(fbuf, w_frame, 48), 32, 24)
    at32[:, 56:64, :] = jnp.zeros((2, 8, HD), F32)
    sq32[56:64, :] = jnp.zeros((8, 128), F32)
    for d in range(ng):
        for h in range(2):
            abst[d, :, h * HD : (h + 1) * HD] = at32[h, pl.ds(d, 8, stride=8), :]
        sqst[d] = sq32[pl.ds(d, 8, stride=8), :]

    pl.semaphore_wait(tr, 1)

    def ab_copy(k):
        d = (g + k) % ng
        return remote(abst.at[d], ab.at[g], ab_s, ab_r, in_group(d))

    def sq_copy(k):
        d = (g + k) % ng
        return remote(sqst.at[d], sqr.at[g], sq_s, sq_r, twin(d))

    for k in range(ng):
        if k:
            ab_copy(k).start()
        sq_copy(k).start()
    ab[g] = abst[g]
    with jax.named_scope("w_ab"):
        whole(ab.at[pl.ds(0, ng - 1)], ab_s, ab_r).wait_recv()
        whole(sqr, sq_s, sq_r).wait_recv()
    pieces = [ab[d] for d in range(ng)]
    square = sqr[0]
    for d in range(1, ng):
        square = square + sqr[d]
    square = square[:, 0:1]
    for piece in pieces:
        square = square + jnp.sum(piece * piece, axis=1, keepdims=True)
    inv = lax.rsqrt(square / (H * HD) + 1e-06)
    for d in range(ng):
        cols = slice(d * 256, (d + 1) * 256)
        out[:, cols] = pieces[d] * inv * gain[:, cols]

    with jax.named_scope("drain"):
        for buf, ss, rs in (
            (nbuf, n_s, n_r), (sbuf, st_s, st_r), (fbuf, f_s, f_r), (gbuf, gt_s, gt_r),
            (qbuf, q_s, qz_r.at[0]),
        ):
            whole(buf.at[most], ss, rs).wait_send()
        few = pl.ds(0, ng - 1)
        whole(qa.at[few], qa_s, qa_r).wait_send()
        whole(ab.at[few], ab_s, ab_r).wait_send()
        whole(ex.at[:, few], ex_s, ex_r).wait_send()
        whole(sqr, sq_s, sq_r).wait_send()
        whole(kv.at[:, few], kv_s, kv_r.at[0, 0]).wait_send()


def spread(done, span_out, first_out, second_out, span, first, second, sems):
    span[...] = done[0:4, :].astype(BF16)
    first[...] = done[4:6, :].astype(BF16)
    second[...] = done[6:7, :].astype(BF16)
    pairs = ((span, span_out), (first, first_out), (second, second_out))
    copies = [pltpu.make_async_copy(a, o, sems.at[i]) for i, (a, o) in enumerate(pairs)]
    for copy in copies:
        copy.start()
    for copy in copies:
        copy.wait()


def per_device(
    dims, cache_k, cache_v, span_q, span_k, span_v, span_frames, action_ids, action_table,
    frame_q, frame_k, frame_v, revealed_k, revealed_v, mask_k, mask_v, pass1_idx, pass2_idx,
    out_gain,
):
    nx, nz = dims
    nb = nx * nz
    ng = NY * NC
    rows = cache_k.shape[0]
    cols = span_k.shape[1]
    dma = pltpu.SemaphoreType.DMA
    vm = pltpu.VMEM
    anywhere = pl.BlockSpec(memory_space=pl.ANY)
    local = pl.BlockSpec(memory_space=pltpu.VMEM)
    outs = [jax.ShapeDtypeStruct((n, span_q.shape[1]), BF16) for n in (4, 2, 1)]
    row = lambda v: v.reshape(1, -1)
    small = (
        span_q, span_k, span_v, row(span_frames), row(action_ids), action_table, frame_q, frame_k,
        frame_v, revealed_k, revealed_v, mask_k, mask_v, row(pass1_idx), row(pass2_idx),
        row(out_gain),
    )
    done = pl.pallas_call(
        functools.partial(kernel, dims),
        out_shape=pltpu.VMEM((8, span_q.shape[1]), F32),
        in_specs=[anywhere] * 18,
        out_specs=local,
        scratch_shapes=[vm(v.shape, v.dtype) for v in small]
        + [
            vm((2, ng, rows, HD), BF16),
            vm((2, ng, 16, HD), BF16),
            vm((2, NY, 16, HD), BF16),
            vm((16, cols), F32),
            vm((8, span_q.shape[1]), F32),
            vm((ng, 8, 256), BF16),
            vm((ng, 8, 256), BF16),
            vm((2, 64, HD), F32),
            vm((nb, 64, 256), BF16),
            vm((32 * nb, 32 * nb), BF16),
            vm((nb, 48, HD), BF16),
            vm((nb, 32, 128), F32),
            vm((8, 128), F32),
            vm((nb, 64, HD), BF16),
            vm((nb, 64, HD), BF16),
            vm((nb, 48, HD), BF16),
            vm((nb, 48, HD), BF16),
            vm((nb, 2, 128), F32),
            vm((nb, 2, 128), F32),
            vm((nb, 2, 128), F32),
            vm((nb, 2, 128), F32),
            vm((128, 128), F32),
            vm((2, 64, HD), F32),
            vm((64, 128), F32),
            vm((ng, 8, 256), F32),
            vm((ng, 8, 256), F32),
            vm((ng, 8, 128), F32),
            vm((ng, 8, 128), F32),
            dma((18,)),
            dma,
            dma,
            dma,
            dma((2, 2 * NY)),
            dma,
            dma,
            dma,
            dma((nz,)),
            dma((nz,)),
        ]
        + [dma] * 12
        + [pltpu.SemaphoreType.REGULAR((2, nz // 2 - 1)), pltpu.SemaphoreType.REGULAR],
        compiler_params=pltpu.CompilerParams(
            collective_id=0, has_side_effects=True, vmem_limit_bytes=60 << 20
        ),
        name="frame_attention",
    )(cache_k, cache_v, *small)
    return pl.pallas_call(
        spread,
        out_shape=outs,
        in_specs=[local],
        out_specs=[anywhere] * 3,
        scratch_shapes=[vm(v.shape, v.dtype) for v in outs] + [dma((3,))],
        name="spread",
    )(pltpu.with_memory_space_constraint(done, pltpu.VMEM))


def solution(mesh):
    both = P("ctx", "tp")
    in_specs = (
        both, both, both, both, both, P(), P("ctx"), P(None, "tp"), both, both, both, both, both,
        P("tp"), P("tp"), P(), P(), P("tp"),
    )
    nz = NZ
    nx = mesh.shape["ctx"] // (NY * NC * nz)
    return jax.shard_map(
        functools.partial(per_device, (nx, nz)),
        mesh=mesh,
        in_specs=in_specs,
        out_specs=(both, both, both),
        check_vma=False,
    )
```

```python
import functools

import jax
import jax.numpy as jnp
from jax import lax
from jax.experimental import pallas as pl
from jax.experimental.pallas import tpu as pltpu
from jax.sharding import PartitionSpec as P

H = 32
HD = 128
NX, NY, NZ, NC = 2, 4, 8, 2
LOG2E = 1.4426950408889634
MESH = pl.DeviceIdType.MESH
F32 = jnp.float32
BF16 = jnp.bfloat16
NEG = -1e30


def kernel(
    dims,
    ck, cv, *refs,
):
    nx, nz = dims
    hbm, refs = refs[:16], refs[16:]
    out, refs = refs[0], refs[1:]
    vmem, refs = refs[:16], refs[16:]
    sq, sk, sv, frames, ids, table, fq, fk, fv, rk, rv, mk, mv, p1, p2, gain = vmem
    (
        kv, ex, exst, ex32, q32, qa, qast, t32, qbuf, hot, qfs, qf, kfr,
        nst, nbuf, fst, fbuf, sst, sbuf, gst, gbuf, m32, at32, sq32, abst, ab, sqst, sqr,
        loc_sem, qa_s, qa_r, kv_s, kv_r, ex_s, ex_r,
        q_s, qz_r, qx_r, n_s, n_r, st_s, st_r, f_s, f_r, gt_s, gt_r,
        ab_s, ab_r, sq_s, sq_r, zr, tr,
    ) = refs
    nb = nx * nz
    ny, nc = NY, NC
    ng = ny * nc
    total = ny * nc * nb * 4
    scale = HD ** (-0.5) * LOG2E
    me = lax.axis_index("ctx")
    tp = lax.axis_index("tp")
    c = me % nc
    z = (me // nc) % nz
    y = (me // (nc * nz)) % ny
    x = me // (nc * nz * ny)
    g = y * nc + c
    b = x * nz + z

    def ctx_of(xx, yy, zz, cc):
        return ((xx * ny + yy) * nz + zz) * nc + cc

    def in_group(d):
        return {"ctx": ctx_of(x, d // nc, z, d % nc), "tp": tp}

    def twin(d):
        return {"ctx": ctx_of(x, d // nc, z, d % nc), "tp": 1 - tp}

    def at_block(xx, zz):
        return {"ctx": ctx_of(xx, y, zz, c), "tp": tp}

    def remote(src, dst, ss, rs, dev):
        return pltpu.make_async_remote_copy(
            src_ref=src, dst_ref=dst, send_sem=ss, recv_sem=rs, device_id=dev, device_id_type=MESH
        )

    def whole(part, ss, rs):
        return remote(part, part, ss, rs, at_block((x + 1) % nx, z))

    barrier = pltpu.get_barrier_semaphore()

    def greet(k, _):
        pl.semaphore_signal(barrier, inc=1, device_id=in_group((g + k) % ng), device_id_type=MESH)
        return 0

    pl.semaphore_signal(barrier, inc=1, device_id=at_block(x, (z + 1) % nz), device_id_type=MESH)
    pl.semaphore_signal(
        barrier, inc=1, device_id=at_block(x, (z + nz - 1) % nz), device_id_type=MESH
    )
    pl.semaphore_signal(barrier, inc=1, device_id=at_block((x + 1) % nx, z), device_id_type=MESH)
    pl.semaphore_signal(barrier, inc=1, device_id=twin(g), device_id_type=MESH)
    lax.fori_loop(1, ng, greet, 0)

    def tell(n):
        for way in range(2):
            zz = (z + 1 + way * (nz - 2)) % nz
            pl.semaphore_signal(
                zr.at[way, n], inc=1, device_id=at_block(x, zz), device_id_type=MESH
            )

    def told(n):
        for way in range(2):
            pl.semaphore_wait(zr.at[way, n], 1)

    def load(i):
        return pltpu.make_async_copy(hbm[i], vmem[i], loc_sem.at[2 + i])

    for i in (0, 6, 1, 2, 3, 4, 5, 7, 8, 9, 10, 11, 12, 13, 14, 15):
        load(i).start()
    col = pl.ds(pl.multiple_of(y * HD, HD), HD)
    own_k = pltpu.make_async_copy(ck.at[:, col], kv.at[0, g], loc_sem.at[0])
    own_v = pltpu.make_async_copy(cv.at[:, col], kv.at[1, g], loc_sem.at[1])
    own_k.start()
    own_v.start()

    load(0).wait()
    load(6).wait()
    q32[0:4, :] = sq[...].astype(F32)
    q32[4:8, :] = fq[...].astype(F32)
    for d in range(ng):
        qast[d] = q32[:, d * 256 : (d + 1) * 256].astype(BF16)

    def qa_copy(k):
        d = (g + k) % ng
        return remote(qast.at[d], qa.at[g], qa_s, qa_r, in_group(d))

    def ex_copy(k):
        d = (g + k) % ng
        return remote(exst.at[:, d // nc], ex.at[:, g], ex_s, ex_r, in_group(d))

    def kv_copy(n, k):
        d = (g + nc * k) % ng
        head = pl.ds(pl.multiple_of((d // nc) * HD, HD), HD)
        source = (ck, cv)[n]
        return remote(
            source.at[:, head], kv.at[n, g], kv_s, kv_r.at[n, k], in_group(d)
        )

    def relay(n, k):
        origin = (g + ng - nc * k) % ng
        peer = y * nc + 1 - c
        src = ((ck, cv)[n].at[:, col]) if k == 0 else kv.at[n, origin]
        return remote(src, kv.at[n, origin], kv_s, kv_r.at[n, ny + k], in_group(peer))

    with jax.named_scope("w_barrier"):
        pl.semaphore_wait(barrier, 4 + (ng - 1))

    reach = nz // 2 - 1
    tell(0)
    for k in range(1, ng):
        qa_copy(k).start()
    pl.semaphore_signal(tr, inc=1, device_id=twin(g), device_id_type=MESH)
    for k in range(1, ny):
        kv_copy(0, k).start()
    relay(0, 0).start()
    qa[g] = qast[g]

    told(0)
    tell(1)
    for k in range(1, ny):
        kv_copy(1, k).start()
    relay(1, 0).start()
    for n in range(1, reach - 1):
        told(n)
        tell(n + 1)

    with jax.named_scope("w_qa"):
        whole(qa.at[pl.ds(0, ng - 1)], qa_s, qa_r).wait_recv()
    for h in range(2):
        cols = slice(h * HD, (h + 1) * HD)
        t32[h] = qa[:, :, cols].astype(F32).reshape(64, HD)
        for i in range(4):
            pair = [t32[h, pl.ds(2 * i + r, 8, stride=8), :] for r in range(2)]
            qbuf[b, 16 * i : 16 * i + 16, cols] = jnp.concatenate(pair, axis=0).astype(BF16)

    def off(k):
        near = k // 2
        return near + 1 if k % 2 else (nz - near) % nz

    def off_dyn(k):
        near = k // 2
        odd = k % 2
        return (odd * (near + 1) + (1 - odd) * (nz - near)) % nz

    def qz_copy(k):
        return remote(
            qbuf.at[b], qbuf.at[b], q_s, qz_r.at[k], at_block(x, (z + off(k)) % nz)
        )

    def qx_copy(k):
        blk = x * nz + (z + nz - off(k)) % nz
        return remote(
            qbuf.at[blk], qbuf.at[blk], q_s, qx_r.at[k], at_block((x + 1) % nx, z)
        )

    qx_copy(0).start()
    for k in range(1, nz - 1):
        qz_copy(k).start()
    told(reach - 1)
    qz_copy(nz - 1).start()

    for i in (1, 2, 3, 4, 5, 7, 8, 9, 10, 11, 12, 13, 14, 15):
        load(i).wait()

    row4 = lax.broadcasted_iota(jnp.int32, (4, 4), 0)
    lane4 = lax.broadcasted_iota(jnp.int32, (4, 4), 1)
    ids_col = jnp.sum(jnp.where(row4 == lane4, ids[...], 0), axis=1, keepdims=True)
    action = jnp.zeros(sk.shape, F32)
    tab = table[...].astype(F32)
    for a in range(table.shape[0]):
        action = jnp.where(ids_col == a, tab[a : a + 1, :], action)
    pos = me * 4 + lax.broadcasted_iota(jnp.int32, (4, 1), 0)
    in1 = jnp.sum(jnp.where(p1[...] == pos, 1.0, 0.0), axis=1, keepdims=True) > 0.5
    in2 = jnp.sum(jnp.where(p2[...] == pos, 1.0, 0.0), axis=1, keepdims=True) > 0.5

    def masked(frame, revealed, mask):
        shape = frame.shape
        frame, revealed = frame[...].astype(F32), revealed[...].astype(F32)
        mask = jnp.broadcast_to(mask[...].astype(F32).reshape(1, -1), shape)
        first = jnp.where(in1, mask, frame)
        second = jnp.where(in2, mask, jnp.where(in1, revealed, frame))
        return first, second

    for n, (span, pair) in enumerate(
        (
            (sk[...].astype(F32) + action, masked(fk, rk, mk)),
            (sv[...].astype(F32), masked(fv, rv, mv)),
        )
    ):
        ex32[0:4, :] = span
        ex32[4:8, :] = pair[0]
        ex32[8:12, :] = pair[1]
        ex32[12:16, :] = jnp.zeros_like(span)
        for d in range(ny):
            exst[n, d] = ex32[:, d * HD : (d + 1) * HD].astype(BF16)
    for k in range(1, ng):
        ex_copy(k).start()
    for n in range(2):
        ex[n, g] = exst[n, y]


    rows = 32 * nb

    def owners(width):
        r = lax.broadcasted_iota(jnp.int32, (rows, width), 0)
        ll = lax.broadcasted_iota(jnp.int32, (rows, width), 1)
        rb, rt, ro = r >> 5, (r >> 3) & 3, r & 7
        rx = jnp.where(rb >= nz, 1, 0)
        rz = rb - nz * rx
        return ll, rt, ((rx * ny + (ro >> 1)) * nz + rz) * nc + (ro & 1)

    lane, rt, owner = owners(total)
    fr = jnp.broadcast_to(frames[...].astype(F32), (rows, total))
    qframe = jnp.sum(jnp.where(lane == 4 * owner + rt, fr, 0.0), axis=1, keepdims=True)
    qf[...] = jnp.broadcast_to(qframe, (rows, 128)).reshape(nb, 32, 128)

    key = lax.broadcasted_iota(jnp.int32, (total, 128), 0)
    kl = lax.broadcasted_iota(jnp.int32, (total, 128), 1)
    ko, ks = kl >> 4, kl & 15
    kwant = 4 * (((x * ny + (ko >> 1)) * nz + z) * nc + (ko & 1)) + ks
    khit = jnp.where((key == kwant) & (ks < 4), 1.0, 0.0).astype(BF16)
    fr8 = jnp.broadcast_to(frames[...].astype(F32), (8, total)).astype(BF16)
    kfr[...] = jnp.dot(fr8, khit, preferred_element_type=F32)

    l1, t1, o1 = owners(p1.shape[1])
    l2, t2, o2 = owners(p2.shape[1])
    v1 = jnp.broadcast_to(p1[...].astype(F32), l1.shape)
    v2 = jnp.broadcast_to(p2[...].astype(F32), l2.shape)
    found = jnp.sum(
        jnp.where((l1 == 2 * o1 + t1) & (t1 < 2), v1, 0.0), axis=1, keepdims=True
    ) + jnp.sum(jnp.where((l2 == o2) & (t2 == 2), v2, 0.0), axis=1, keepdims=True)
    found = found.astype(jnp.int32)
    bits = nz.bit_length() - 1
    dev = found >> 2
    from_z = (dev >> 1) & (nz - 1)
    from_y = (dev >> (1 + bits)) & (ny - 1)
    from_x = dev >> (3 + bits)
    place = (from_x * nz + from_z) * 32 + (found & 3) * 8 + from_y * nc + (dev & 1)
    lanes = lax.broadcasted_iota(jnp.int32, (rows, rows), 1)
    hot[...] = jnp.where(lanes == place, 1.0, 0.0).astype(BF16)

    with jax.named_scope("w_kv"):
        for k in range(1, ny):
            for n in range(2):
                kv_copy(n, k).wait_recv()
                relay(n, k).start()

    def from_z_half(k):
        qz_copy(k).wait_recv()
        qx_copy(k).start()

    with jax.named_scope("w_qz"):
        for k in range(1, 4):
            from_z_half(k)

    with jax.named_scope("w_relay"):
        whole(ex.at[:, pl.ds(0, ng - 1)], ex_s, ex_r).wait_recv()
        own_k.wait()
        own_v.wait()
        for k in range(ny):
            for n in range(2):
                relay(n, k).wait_recv()

    keys = kv.shape[1] * kv.shape[2]
    nt = (((1,), (1,)), ((), ()))

    def dest(k):
        return (x + k // nz) % nx, (z + nz - off_dyn(k % nz)) % nz

    def scores(q, bias):
        s1 = lax.dot_general(q, kv[0].reshape(keys, HD), nt, preferred_element_type=F32)
        s2 = lax.dot_general(q, ex[0].reshape(128, HD), nt, preferred_element_type=F32) + bias
        return s1, s2

    def weigh(s1, s2):
        m = jnp.maximum(s1.max(axis=1, keepdims=True), s2.max(axis=1, keepdims=True))
        w1 = jnp.exp2((s1 - m) * scale)
        w2 = jnp.exp2((s2 - m) * scale)
        tot = w1.sum(axis=1, keepdims=True) + w2.sum(axis=1, keepdims=True)
        o = jnp.dot(w1.astype(BF16), kv[1].reshape(keys, HD), preferred_element_type=F32)
        o = o + jnp.dot(w2.astype(BF16), ex[1].reshape(128, HD), preferred_element_type=F32)
        return o, jnp.where(lax.broadcasted_iota(jnp.int32, o.shape, 1) == 0, m, tot)

    def attention(tiles):
        return [weigh(*pair) for pair in [scores(*tile) for tile in tiles]]

    def n_copy(k, blk, dev):
        return remote(nst.at[blk], nbuf.at[b], n_s, n_r, dev)

    def st_copy(k, blk, dev):
        return remote(sst.at[blk], sbuf.at[b], st_s, st_r, dev)

    def f_copy(k, blk, dev):
        return remote(fst.at[blk], fbuf.at[b], f_s, f_r, dev)

    def gt_copy(k, blk, dev):
        return remote(gst.at[blk], gbuf.at[b], gt_s, gt_r, dev)

    def put_stats(stats, into, blks):
        turned = stats.T[0:8, :]
        for q in range(4):
            tile = turned[:, (q // 2) * 128 : (q // 2) * 128 + 128]
            if q % 2:
                tile = pltpu.roll(tile, 64, 1)
            into[blks[q]] = tile[0:2]

    def push(s, blks, dests, copies):
        for q in (3, 2, 1, 0):
            dev = at_block(*dests[q])

            def go(q=q, dev=dev):
                for copy in copies:
                    copy(4 * s + q, blks[q], dev).start()

            if q == 0:
                pl.when(s > 0)(go)
            else:
                go()

    slot32 = lax.broadcasted_iota(jnp.int32, (32, 128), 1) & 15
    half = nz // 4

    def spans(s, _):
        for u in range(half, 2 * half):

            @pl.when(s == u)
            def _(u=u):
                with jax.named_scope(f"wx{u}"):
                    for q in range(4):
                        qx_copy(4 * (u - half) + q).wait_recv()

        for u in range(1, half):

            @pl.when(s == u)
            def _(u=u):
                with jax.named_scope(f"wz{u}"):
                    for q in range(4):
                        from_z_half(4 * u + q)

        dests = [dest(4 * s + q) for q in range(4)]
        blks = [xx * nz + zz for xx, zz in dests]
        parts, bias = [], []
        for blk in blks:
            mask = jnp.where((slot32 < 4) & (kfr[0:1, :] <= qf[blk]), 0.0, NEG)
            bias += [mask, mask]
            parts += [qbuf[blk, 0:32, 0:HD], qbuf[blk, 0:32, HD : 2 * HD]]
        done = attention(
            [
                (jnp.concatenate(parts[u : u + 4], axis=0), jnp.concatenate(bias[u : u + 4], axis=0))
                for u in (0, 4)
            ]
        )
        for q in range(4):
            low = 64 * (q % 2)
            nst[blks[q]] = done[q // 2][0][low : low + 64].astype(BF16)
        put_stats(jnp.concatenate([st for _, st in done], axis=0), sst, blks)
        push(s, blks, dests, (st_copy, n_copy))
        return 0

    with jax.named_scope("spans"):
        lax.fori_loop(0, 2 * half, spans, 0)

    frame_q = qbuf[:, 32:64, :].reshape(rows, 256)
    picked = jnp.dot(hot[...], frame_q, preferred_element_type=F32)
    for blk in range(nb):
        both = [picked[32 * blk : 32 * blk + 24, h * HD : (h + 1) * HD] for h in range(2)]
        qfs[blk] = jnp.concatenate(both, axis=0).astype(BF16)

    r48 = lax.broadcasted_iota(jnp.int32, (48, 128), 0)
    slot48 = lax.broadcasted_iota(jnp.int32, (48, 128), 1) & 15
    t48 = (jnp.where(r48 >= 24, r48 - 24, r48)) >> 3
    allowed = (slot48 < 4) | ((slot48 < 8) & (t48 < 2)) | (
        (slot48 >= 8) & (slot48 < 12) & (t48 == 2)
    )
    mask48 = jnp.where(allowed, 0.0, NEG)

    mask192 = jnp.concatenate([mask48] * 4, axis=0)

    def picks(i, _):
        steps = [2 * half - 1 - i, half - 1 - i]
        dests = [[dest(4 * s + q) for q in range(4)] for s in steps]
        blks = [[xx * nz + zz for xx, zz in group] for group in dests]
        done = attention(
            [(jnp.concatenate([qfs[blk] for blk in group], axis=0), mask192) for group in blks]
        )
        pad = jnp.zeros((16, 128), F32)
        for s, group, where, (o, stats) in zip(steps, blks, dests, done):
            padded = []
            for q in range(4):
                fst[group[q]] = o[48 * q : 48 * q + 48].astype(BF16)
                padded += [stats[48 * q : 48 * q + 48], pad]
            put_stats(jnp.concatenate(padded, axis=0), gst, group)
        for s, group, where in zip(steps, blks, dests):
            push(s, group, where, (gt_copy, f_copy))
        return 0

    with jax.named_scope("picks"):
        lax.fori_loop(0, half, picks, 0)
    nbuf[b] = nst[b]
    sbuf[b] = sst[b]
    fbuf[b] = fst[b]
    gbuf[b] = gst[b]
    most = pl.ds(0, nb - 1)

    def shares(stats, n):
        for s in range(nb):
            m32[2 * s : 2 * s + 2, :] = stats[s]
        st = m32[...].T[0:n]
        lanes = lax.broadcasted_iota(jnp.int32, (n, 128), 1)
        is_m = ((lanes & 1) == 0) & (lanes < 2 * nb)
        top = jnp.max(jnp.where(is_m, st, NEG), axis=1, keepdims=True)
        tot = pltpu.roll(st, 127, 1)
        e = jnp.where(is_m, jnp.exp2((jnp.where(is_m, st, top) - top) * scale), 0.0)
        den = jnp.sum(jnp.where(is_m, e * tot, 0.0), axis=1, keepdims=True)
        return e / den

    def merge(data, w, n):
        acc = jnp.zeros((n, HD), F32)
        for s in range(nb):
            acc = acc + w[:, 2 * s : 2 * s + 1] * data[s].astype(F32)
        return acc

    def settle(acc, low, n):
        squares = jnp.sum(acc * acc, axis=1, keepdims=True)
        at32[0, low : low + n, :] = acc[0:n]
        at32[1, low : low + n, :] = acc[n : 2 * n]
        sq32[low : low + n, :] = jnp.broadcast_to(squares[0:n] + squares[n : 2 * n], (n, 128))

    m32[...] = jnp.zeros((128, 128), F32)
    with jax.named_scope("w_st"):
        whole(sbuf.at[most], st_s, st_r).wait_recv()
    w_span = shares(sbuf, 64)
    with jax.named_scope("w_n"):
        whole(nbuf.at[most], n_s, n_r).wait_recv()
    settle(merge(nbuf, w_span, 64), 0, 32)
    with jax.named_scope("w_gt"):
        whole(gbuf.at[most], gt_s, gt_r).wait_recv()
    w_frame = shares(gbuf, 48)
    with jax.named_scope("w_f"):
        whole(fbuf.at[most], f_s, f_r).wait_recv()
    settle(merge(fbuf, w_frame, 48), 32, 24)
    at32[:, 56:64, :] = jnp.zeros((2, 8, HD), F32)
    sq32[56:64, :] = jnp.zeros((8, 128), F32)
    for d in range(ng):
        for h in range(2):
            abst[d, :, h * HD : (h + 1) * HD] = at32[h, pl.ds(d, 8, stride=8), :]
        sqst[d] = sq32[pl.ds(d, 8, stride=8), :]

    pl.semaphore_wait(tr, 1)

    def ab_copy(k):
        d = (g + k) % ng
        return remote(abst.at[d], ab.at[g], ab_s, ab_r, in_group(d))

    def sq_copy(k):
        d = (g + k) % ng
        return remote(sqst.at[d], sqr.at[g], sq_s, sq_r, twin(d))

    for k in range(ng):
        if k:
            ab_copy(k).start()
        sq_copy(k).start()
    ab[g] = abst[g]
    with jax.named_scope("w_ab"):
        whole(ab.at[pl.ds(0, ng - 1)], ab_s, ab_r).wait_recv()
        whole(sqr, sq_s, sq_r).wait_recv()
    pieces = [ab[d] for d in range(ng)]
    square = sqr[0]
    for d in range(1, ng):
        square = square + sqr[d]
    square = square[:, 0:1]
    for piece in pieces:
        square = square + jnp.sum(piece * piece, axis=1, keepdims=True)
    inv = lax.rsqrt(square / (H * HD) + 1e-06)
    for d in range(ng):
        cols = slice(d * 256, (d + 1) * 256)
        out[:, cols] = pieces[d] * inv * gain[:, cols]

    with jax.named_scope("drain"):
        for buf, ss, rs in (
            (nbuf, n_s, n_r), (sbuf, st_s, st_r), (fbuf, f_s, f_r), (gbuf, gt_s, gt_r),
            (qbuf, q_s, qz_r.at[0]),
        ):
            whole(buf.at[most], ss, rs).wait_send()
        few = pl.ds(0, ng - 1)
        whole(qa.at[few], qa_s, qa_r).wait_send()
        whole(ab.at[few], ab_s, ab_r).wait_send()
        whole(ex.at[:, few], ex_s, ex_r).wait_send()
        whole(sqr, sq_s, sq_r).wait_send()
        whole(kv.at[:, few], kv_s, kv_r.at[0, 0]).wait_send()


def spread(done, span_out, first_out, second_out, span, first, second, sems):
    span[...] = done[0:4, :].astype(BF16)
    first[...] = done[4:6, :].astype(BF16)
    second[...] = done[6:7, :].astype(BF16)
    pairs = ((span, span_out), (first, first_out), (second, second_out))
    copies = [pltpu.make_async_copy(a, o, sems.at[i]) for i, (a, o) in enumerate(pairs)]
    for copy in copies:
        copy.start()
    for copy in copies:
        copy.wait()


def per_device(
    dims, cache_k, cache_v, span_q, span_k, span_v, span_frames, action_ids, action_table,
    frame_q, frame_k, frame_v, revealed_k, revealed_v, mask_k, mask_v, pass1_idx, pass2_idx,
    out_gain,
):
    nx, nz = dims
    nb = nx * nz
    ng = NY * NC
    rows = cache_k.shape[0]
    cols = span_k.shape[1]
    dma = pltpu.SemaphoreType.DMA
    vm = pltpu.VMEM
    anywhere = pl.BlockSpec(memory_space=pl.ANY)
    local = pl.BlockSpec(memory_space=pltpu.VMEM)
    outs = [jax.ShapeDtypeStruct((n, span_q.shape[1]), BF16) for n in (4, 2, 1)]
    row = lambda v: v.reshape(1, -1)
    small = (
        span_q, span_k, span_v, row(span_frames), row(action_ids), action_table, frame_q, frame_k,
        frame_v, revealed_k, revealed_v, mask_k, mask_v, row(pass1_idx), row(pass2_idx),
        row(out_gain),
    )
    done = pl.pallas_call(
        functools.partial(kernel, dims),
        out_shape=pltpu.VMEM((8, span_q.shape[1]), F32),
        in_specs=[anywhere] * 18,
        out_specs=local,
        scratch_shapes=[vm(v.shape, v.dtype) for v in small]
        + [
            vm((2, ng, rows, HD), BF16),
            vm((2, ng, 16, HD), BF16),
            vm((2, NY, 16, HD), BF16),
            vm((16, cols), F32),
            vm((8, span_q.shape[1]), F32),
            vm((ng, 8, 256), BF16),
            vm((ng, 8, 256), BF16),
            vm((2, 64, HD), F32),
            vm((nb, 64, 256), BF16),
            vm((32 * nb, 32 * nb), BF16),
            vm((nb, 48, HD), BF16),
            vm((nb, 32, 128), F32),
            vm((8, 128), F32),
            vm((nb, 64, HD), BF16),
            vm((nb, 64, HD), BF16),
            vm((nb, 48, HD), BF16),
            vm((nb, 48, HD), BF16),
            vm((nb, 2, 128), F32),
            vm((nb, 2, 128), F32),
            vm((nb, 2, 128), F32),
            vm((nb, 2, 128), F32),
            vm((128, 128), F32),
            vm((2, 64, HD), F32),
            vm((64, 128), F32),
            vm((ng, 8, 256), F32),
            vm((ng, 8, 256), F32),
            vm((ng, 8, 128), F32),
            vm((ng, 8, 128), F32),
            dma((18,)),
            dma,
            dma,
            dma,
            dma((2, 2 * NY)),
            dma,
            dma,
            dma,
            dma((nz,)),
            dma((nz,)),
        ]
        + [dma] * 12
        + [pltpu.SemaphoreType.REGULAR((2, nz // 2 - 1)), pltpu.SemaphoreType.REGULAR],
        compiler_params=pltpu.CompilerParams(
            collective_id=0, has_side_effects=True, vmem_limit_bytes=60 << 20
        ),
        name="frame_attention",
    )(cache_k, cache_v, *small)
    return pl.pallas_call(
        spread,
        out_shape=outs,
        in_specs=[local],
        out_specs=[anywhere] * 3,
        scratch_shapes=[vm(v.shape, v.dtype) for v in outs] + [dma((3,))],
        name="spread",
    )(pltpu.with_memory_space_constraint(done, pltpu.VMEM))


def solution(mesh):
    both = P("ctx", "tp")
    in_specs = (
        both, both, both, both, both, P(), P("ctx"), P(None, "tp"), both, both, both, both, both,
        P("tp"), P("tp"), P(), P(), P("tp"),
    )
    nz = NZ
    nx = mesh.shape["ctx"] // (NY * NC * nz)
    return jax.shard_map(
        functools.partial(per_device, (nx, nz)),
        mesh=mesh,
        in_specs=in_specs,
        out_specs=(both, both, both),
        check_vma=False,
    )
```

```python
import functools

import jax
import jax.numpy as jnp
from jax import lax
from jax.experimental import pallas as pl
from jax.experimental.pallas import tpu as pltpu
from jax.sharding import PartitionSpec as P

H = 32
HD = 128
NX, NY, NZ, NC = 2, 4, 8, 2
LOG2E = 1.4426950408889634
MESH = pl.DeviceIdType.MESH
F32 = jnp.float32
BF16 = jnp.bfloat16
NEG = -1e30


def kernel(
    dims,
    ck, cv, *refs,
):
    nx, nz = dims
    hbm, refs = refs[:16], refs[16:]
    out, refs = refs[0], refs[1:]
    vmem, refs = refs[:16], refs[16:]
    sq, sk, sv, frames, ids, table, fq, fk, fv, rk, rv, mk, mv, p1, p2, gain = vmem
    (
        kv, ex, exst, ex32, q32, qa, qast, t32, qbuf, hot, qfs, qf, kfr,
        nst, nbuf, fst, fbuf, sst, sbuf, gst, gbuf, m32, at32, sq32, abst, ab, sqst, sqr,
        loc_sem, qa_s, qa_r, kv_s, kv_r, ex_s, ex_r,
        q_s, qz_r, qx_r, n_s, n_r, st_s, st_r, f_s, f_r, gt_s, gt_r,
        ab_s, ab_r, sq_s, sq_r, zr, tr,
    ) = refs
    nb = nx * nz
    ny, nc = NY, NC
    ng = ny * nc
    total = ny * nc * nb * 4
    scale = HD ** (-0.5) * LOG2E
    me = lax.axis_index("ctx")
    tp = lax.axis_index("tp")
    c = me % nc
    z = (me // nc) % nz
    y = (me // (nc * nz)) % ny
    x = me // (nc * nz * ny)
    g = y * nc + c
    b = x * nz + z

    def ctx_of(xx, yy, zz, cc):
        return ((xx * ny + yy) * nz + zz) * nc + cc

    def in_group(d):
        return {"ctx": ctx_of(x, d // nc, z, d % nc), "tp": tp}

    def twin(d):
        return {"ctx": ctx_of(x, d // nc, z, d % nc), "tp": 1 - tp}

    def at_block(xx, zz):
        return {"ctx": ctx_of(xx, y, zz, c), "tp": tp}

    def remote(src, dst, ss, rs, dev):
        return pltpu.make_async_remote_copy(
            src_ref=src, dst_ref=dst, send_sem=ss, recv_sem=rs, device_id=dev, device_id_type=MESH
        )

    def whole(part, ss, rs):
        return remote(part, part, ss, rs, at_block((x + 1) % nx, z))

    barrier = pltpu.get_barrier_semaphore()

    def greet(k, _):
        pl.semaphore_signal(barrier, inc=1, device_id=in_group((g + k) % ng), device_id_type=MESH)
        return 0

    pl.semaphore_signal(barrier, inc=1, device_id=at_block(x, (z + 1) % nz), device_id_type=MESH)
    pl.semaphore_signal(
        barrier, inc=1, device_id=at_block(x, (z + nz - 1) % nz), device_id_type=MESH
    )
    pl.semaphore_signal(barrier, inc=1, device_id=at_block((x + 1) % nx, z), device_id_type=MESH)
    pl.semaphore_signal(barrier, inc=1, device_id=twin(g), device_id_type=MESH)
    lax.fori_loop(1, ng, greet, 0)

    def tell(n):
        for way in range(2):
            zz = (z + 1 + way * (nz - 2)) % nz
            pl.semaphore_signal(
                zr.at[way, n], inc=1, device_id=at_block(x, zz), device_id_type=MESH
            )

    def told(n):
        for way in range(2):
            pl.semaphore_wait(zr.at[way, n], 1)

    def load(i):
        return pltpu.make_async_copy(hbm[i], vmem[i], loc_sem.at[2 + i])

    for i in (0, 6, 1, 2, 3, 4, 5, 7, 8, 9, 10, 11, 12, 13, 14, 15):
        load(i).start()
    col = pl.ds(pl.multiple_of(y * HD, HD), HD)
    own_k = pltpu.make_async_copy(ck.at[:, col], kv.at[0, g], loc_sem.at[0])
    own_v = pltpu.make_async_copy(cv.at[:, col], kv.at[1, g], loc_sem.at[1])
    own_k.start()
    own_v.start()

    load(0).wait()
    load(6).wait()
    q32[0:4, :] = sq[...].astype(F32)
    q32[4:8, :] = fq[...].astype(F32)
    for d in range(ng):
        qast[d] = q32[:, d * 256 : (d + 1) * 256].astype(BF16)

    def qa_copy(k):
        d = (g + k) % ng
        return remote(qast.at[d], qa.at[g], qa_s, qa_r, in_group(d))

    def ex_copy(k):
        d = (g + k) % ng
        return remote(exst.at[:, d // nc], ex.at[:, g], ex_s, ex_r, in_group(d))

    def kv_copy(n, k):
        d = (g + nc * k) % ng
        head = pl.ds(pl.multiple_of((d // nc) * HD, HD), HD)
        source = (ck, cv)[n]
        return remote(
            source.at[:, head], kv.at[n, g], kv_s, kv_r.at[n, k], in_group(d)
        )

    def relay(n, k):
        origin = (g + ng - nc * k) % ng
        peer = y * nc + 1 - c
        src = ((ck, cv)[n].at[:, col]) if k == 0 else kv.at[n, origin]
        return remote(src, kv.at[n, origin], kv_s, kv_r.at[n, ny + k], in_group(peer))

    with jax.named_scope("w_barrier"):
        pl.semaphore_wait(barrier, 4 + (ng - 1))

    reach = nz // 2 - 1
    tell(0)
    for k in range(1, ng):
        qa_copy(k).start()
    pl.semaphore_signal(tr, inc=1, device_id=twin(g), device_id_type=MESH)
    for k in (2, 1, 3):
        kv_copy(0, k).start()
    relay(0, 0).start()
    qa[g] = qast[g]

    told(0)
    tell(1)
    for k in (2, 1, 3):
        kv_copy(1, k).start()
    relay(1, 0).start()
    for n in range(1, reach - 1):
        told(n)
        tell(n + 1)

    with jax.named_scope("w_qa"):
        whole(qa.at[pl.ds(0, ng - 1)], qa_s, qa_r).wait_recv()
    for h in range(2):
        cols = slice(h * HD, (h + 1) * HD)
        t32[h] = qa[:, :, cols].astype(F32).reshape(64, HD)
        for i in range(4):
            pair = [t32[h, pl.ds(2 * i + r, 8, stride=8), :] for r in range(2)]
            qbuf[b, 16 * i : 16 * i + 16, cols] = jnp.concatenate(pair, axis=0).astype(BF16)

    def off(k):
        near = k // 2
        return near + 1 if k % 2 else (nz - near) % nz

    def off_dyn(k):
        near = k // 2
        odd = k % 2
        return (odd * (near + 1) + (1 - odd) * (nz - near)) % nz

    def qz_copy(k):
        return remote(
            qbuf.at[b], qbuf.at[b], q_s, qz_r.at[k], at_block(x, (z + off(k)) % nz)
        )

    def qx_copy(k):
        blk = x * nz + (z + nz - off(k)) % nz
        return remote(
            qbuf.at[blk], qbuf.at[blk], q_s, qx_r.at[k], at_block((x + 1) % nx, z)
        )

    qx_copy(0).start()
    for k in range(1, nz - 1):
        qz_copy(k).start()
    told(reach - 1)
    qz_copy(nz - 1).start()

    for i in (1, 2, 3, 4, 5, 7, 8, 9, 10, 11, 12, 13, 14, 15):
        load(i).wait()

    row4 = lax.broadcasted_iota(jnp.int32, (4, 4), 0)
    lane4 = lax.broadcasted_iota(jnp.int32, (4, 4), 1)
    ids_col = jnp.sum(jnp.where(row4 == lane4, ids[...], 0), axis=1, keepdims=True)
    action = jnp.zeros(sk.shape, F32)
    tab = table[...].astype(F32)
    for a in range(table.shape[0]):
        action = jnp.where(ids_col == a, tab[a : a + 1, :], action)
    pos = me * 4 + lax.broadcasted_iota(jnp.int32, (4, 1), 0)
    in1 = jnp.sum(jnp.where(p1[...] == pos, 1.0, 0.0), axis=1, keepdims=True) > 0.5
    in2 = jnp.sum(jnp.where(p2[...] == pos, 1.0, 0.0), axis=1, keepdims=True) > 0.5

    def masked(frame, revealed, mask):
        shape = frame.shape
        frame, revealed = frame[...].astype(F32), revealed[...].astype(F32)
        mask = jnp.broadcast_to(mask[...].astype(F32).reshape(1, -1), shape)
        first = jnp.where(in1, mask, frame)
        second = jnp.where(in2, mask, jnp.where(in1, revealed, frame))
        return first, second

    for n, (span, pair) in enumerate(
        (
            (sk[...].astype(F32) + action, masked(fk, rk, mk)),
            (sv[...].astype(F32), masked(fv, rv, mv)),
        )
    ):
        ex32[0:4, :] = span
        ex32[4:8, :] = pair[0]
        ex32[8:12, :] = pair[1]
        ex32[12:16, :] = jnp.zeros_like(span)
        for d in range(ny):
            exst[n, d] = ex32[:, d * HD : (d + 1) * HD].astype(BF16)
    for k in range(1, ng):
        ex_copy(k).start()
    for n in range(2):
        ex[n, g] = exst[n, y]


    rows = 32 * nb

    def owners(width):
        r = lax.broadcasted_iota(jnp.int32, (rows, width), 0)
        ll = lax.broadcasted_iota(jnp.int32, (rows, width), 1)
        rb, rt, ro = r >> 5, (r >> 3) & 3, r & 7
        rx = jnp.where(rb >= nz, 1, 0)
        rz = rb - nz * rx
        return ll, rt, ((rx * ny + (ro >> 1)) * nz + rz) * nc + (ro & 1)

    lane, rt, owner = owners(total)
    fr = jnp.broadcast_to(frames[...].astype(F32), (rows, total))
    qframe = jnp.sum(jnp.where(lane == 4 * owner + rt, fr, 0.0), axis=1, keepdims=True)
    qf[...] = jnp.broadcast_to(qframe, (rows, 128)).reshape(nb, 32, 128)

    key = lax.broadcasted_iota(jnp.int32, (total, 128), 0)
    kl = lax.broadcasted_iota(jnp.int32, (total, 128), 1)
    ko, ks = kl >> 4, kl & 15
    kwant = 4 * (((x * ny + (ko >> 1)) * nz + z) * nc + (ko & 1)) + ks
    khit = jnp.where((key == kwant) & (ks < 4), 1.0, 0.0).astype(BF16)
    fr8 = jnp.broadcast_to(frames[...].astype(F32), (8, total)).astype(BF16)
    kfr[...] = jnp.dot(fr8, khit, preferred_element_type=F32)

    l1, t1, o1 = owners(p1.shape[1])
    l2, t2, o2 = owners(p2.shape[1])
    v1 = jnp.broadcast_to(p1[...].astype(F32), l1.shape)
    v2 = jnp.broadcast_to(p2[...].astype(F32), l2.shape)
    found = jnp.sum(
        jnp.where((l1 == 2 * o1 + t1) & (t1 < 2), v1, 0.0), axis=1, keepdims=True
    ) + jnp.sum(jnp.where((l2 == o2) & (t2 == 2), v2, 0.0), axis=1, keepdims=True)
    found = found.astype(jnp.int32)
    bits = nz.bit_length() - 1
    dev = found >> 2
    from_z = (dev >> 1) & (nz - 1)
    from_y = (dev >> (1 + bits)) & (ny - 1)
    from_x = dev >> (3 + bits)
    place = (from_x * nz + from_z) * 32 + (found & 3) * 8 + from_y * nc + (dev & 1)
    lanes = lax.broadcasted_iota(jnp.int32, (rows, rows), 1)
    hot[...] = jnp.where(lanes == place, 1.0, 0.0).astype(BF16)

    with jax.named_scope("w_kv"):
        for n in range(2):
            for k in (1, 3, 2):
                kv_copy(n, k).wait_recv()
                relay(n, k).start()

    def from_z_half(k):
        qz_copy(k).wait_recv()
        qx_copy(k).start()

    with jax.named_scope("w_qz"):
        for k in range(1, 4):
            from_z_half(k)

    with jax.named_scope("w_relay"):
        whole(ex.at[:, pl.ds(0, ng - 1)], ex_s, ex_r).wait_recv()
        own_k.wait()
        own_v.wait()
        for k in range(ny):
            for n in range(2):
                relay(n, k).wait_recv()

    keys = kv.shape[1] * kv.shape[2]
    nt = (((1,), (1,)), ((), ()))

    def dest(k):
        return (x + k // nz) % nx, (z + nz - off_dyn(k % nz)) % nz

    def scores(q, bias):
        s1 = lax.dot_general(q, kv[0].reshape(keys, HD), nt, preferred_element_type=F32)
        s2 = lax.dot_general(q, ex[0].reshape(128, HD), nt, preferred_element_type=F32) + bias
        return s1, s2

    def weigh(s1, s2):
        m = jnp.maximum(s1.max(axis=1, keepdims=True), s2.max(axis=1, keepdims=True))
        w1 = jnp.exp2((s1 - m) * scale)
        w2 = jnp.exp2((s2 - m) * scale)
        tot = w1.sum(axis=1, keepdims=True) + w2.sum(axis=1, keepdims=True)
        o = jnp.dot(w1.astype(BF16), kv[1].reshape(keys, HD), preferred_element_type=F32)
        o = o + jnp.dot(w2.astype(BF16), ex[1].reshape(128, HD), preferred_element_type=F32)
        return o, jnp.where(lax.broadcasted_iota(jnp.int32, o.shape, 1) == 0, m, tot)

    def attention(tiles):
        return [weigh(*pair) for pair in [scores(*tile) for tile in tiles]]

    def n_copy(k, blk, dev):
        return remote(nst.at[blk], nbuf.at[b], n_s, n_r, dev)

    def st_copy(k, blk, dev):
        return remote(sst.at[blk], sbuf.at[b], st_s, st_r, dev)

    def f_copy(k, blk, dev):
        return remote(fst.at[blk], fbuf.at[b], f_s, f_r, dev)

    def gt_copy(k, blk, dev):
        return remote(gst.at[blk], gbuf.at[b], gt_s, gt_r, dev)

    def put_stats(stats, into, blks):
        turned = stats.T[0:8, :]
        for q in range(4):
            tile = turned[:, (q // 2) * 128 : (q // 2) * 128 + 128]
            if q % 2:
                tile = pltpu.roll(tile, 64, 1)
            into[blks[q]] = tile[0:2]

    def push(s, blks, dests, copies):
        for q in (3, 2, 1, 0):
            dev = at_block(*dests[q])

            def go(q=q, dev=dev):
                for copy in copies:
                    copy(4 * s + q, blks[q], dev).start()

            if q == 0:
                pl.when(s > 0)(go)
            else:
                go()

    slot32 = lax.broadcasted_iota(jnp.int32, (32, 128), 1) & 15
    half = nz // 4

    def spans(s, _):
        for u in range(half, 2 * half):

            @pl.when(s == u)
            def _(u=u):
                with jax.named_scope(f"wx{u}"):
                    for q in range(4):
                        qx_copy(4 * (u - half) + q).wait_recv()

        for u in range(1, half):

            @pl.when(s == u)
            def _(u=u):
                with jax.named_scope(f"wz{u}"):
                    for q in range(4):
                        from_z_half(4 * u + q)

        dests = [dest(4 * s + q) for q in range(4)]
        blks = [xx * nz + zz for xx, zz in dests]
        parts, bias = [], []
        for blk in blks:
            mask = jnp.where((slot32 < 4) & (kfr[0:1, :] <= qf[blk]), 0.0, NEG)
            bias += [mask, mask]
            parts += [qbuf[blk, 0:32, 0:HD], qbuf[blk, 0:32, HD : 2 * HD]]
        done = attention(
            [
                (jnp.concatenate(parts[u : u + 4], axis=0), jnp.concatenate(bias[u : u + 4], axis=0))
                for u in (0, 4)
            ]
        )
        for q in range(4):
            low = 64 * (q % 2)
            nst[blks[q]] = done[q // 2][0][low : low + 64].astype(BF16)
        put_stats(jnp.concatenate([st for _, st in done], axis=0), sst, blks)
        push(s, blks, dests, (st_copy, n_copy))
        return 0

    with jax.named_scope("spans"):
        lax.fori_loop(0, 2 * half, spans, 0)

    frame_q = qbuf[:, 32:64, :].reshape(rows, 256)
    picked = jnp.dot(hot[...], frame_q, preferred_element_type=F32)
    for blk in range(nb):
        both = [picked[32 * blk : 32 * blk + 24, h * HD : (h + 1) * HD] for h in range(2)]
        qfs[blk] = jnp.concatenate(both, axis=0).astype(BF16)

    r48 = lax.broadcasted_iota(jnp.int32, (48, 128), 0)
    slot48 = lax.broadcasted_iota(jnp.int32, (48, 128), 1) & 15
    t48 = (jnp.where(r48 >= 24, r48 - 24, r48)) >> 3
    allowed = (slot48 < 4) | ((slot48 < 8) & (t48 < 2)) | (
        (slot48 >= 8) & (slot48 < 12) & (t48 == 2)
    )
    mask48 = jnp.where(allowed, 0.0, NEG)

    mask192 = jnp.concatenate([mask48] * 4, axis=0)

    def picks(i, _):
        steps = [2 * half - 1 - i, half - 1 - i]
        dests = [[dest(4 * s + q) for q in range(4)] for s in steps]
        blks = [[xx * nz + zz for xx, zz in group] for group in dests]
        done = attention(
            [(jnp.concatenate([qfs[blk] for blk in group], axis=0), mask192) for group in blks]
        )
        pad = jnp.zeros((16, 128), F32)
        for s, group, where, (o, stats) in zip(steps, blks, dests, done):
            padded = []
            for q in range(4):
                fst[group[q]] = o[48 * q : 48 * q + 48].astype(BF16)
                padded += [stats[48 * q : 48 * q + 48], pad]
            put_stats(jnp.concatenate(padded, axis=0), gst, group)
        for s, group, where in zip(steps, blks, dests):
            push(s, group, where, (gt_copy, f_copy))
        return 0

    with jax.named_scope("picks"):
        lax.fori_loop(0, half, picks, 0)
    nbuf[b] = nst[b]
    sbuf[b] = sst[b]
    fbuf[b] = fst[b]
    gbuf[b] = gst[b]
    most = pl.ds(0, nb - 1)

    def shares(stats, n):
        for s in range(nb):
            m32[2 * s : 2 * s + 2, :] = stats[s]
        st = m32[...].T[0:n]
        lanes = lax.broadcasted_iota(jnp.int32, (n, 128), 1)
        is_m = ((lanes & 1) == 0) & (lanes < 2 * nb)
        top = jnp.max(jnp.where(is_m, st, NEG), axis=1, keepdims=True)
        tot = pltpu.roll(st, 127, 1)
        e = jnp.where(is_m, jnp.exp2((jnp.where(is_m, st, top) - top) * scale), 0.0)
        den = jnp.sum(jnp.where(is_m, e * tot, 0.0), axis=1, keepdims=True)
        return e / den

    def merge(data, w, n):
        acc = jnp.zeros((n, HD), F32)
        for s in range(nb):
            acc = acc + w[:, 2 * s : 2 * s + 1] * data[s].astype(F32)
        return acc

    def settle(acc, low, n):
        squares = jnp.sum(acc * acc, axis=1, keepdims=True)
        at32[0, low : low + n, :] = acc[0:n]
        at32[1, low : low + n, :] = acc[n : 2 * n]
        sq32[low : low + n, :] = jnp.broadcast_to(squares[0:n] + squares[n : 2 * n], (n, 128))

    m32[...] = jnp.zeros((128, 128), F32)
    with jax.named_scope("w_st"):
        whole(sbuf.at[most], st_s, st_r).wait_recv()
    w_span = shares(sbuf, 64)
    with jax.named_scope("w_n"):
        whole(nbuf.at[most], n_s, n_r).wait_recv()
    settle(merge(nbuf, w_span, 64), 0, 32)
    with jax.named_scope("w_gt"):
        whole(gbuf.at[most], gt_s, gt_r).wait_recv()
    w_frame = shares(gbuf, 48)
    with jax.named_scope("w_f"):
        whole(fbuf.at[most], f_s, f_r).wait_recv()
    settle(merge(fbuf, w_frame, 48), 32, 24)
    at32[:, 56:64, :] = jnp.zeros((2, 8, HD), F32)
    sq32[56:64, :] = jnp.zeros((8, 128), F32)
    for d in range(ng):
        for h in range(2):
            abst[d, :, h * HD : (h + 1) * HD] = at32[h, pl.ds(d, 8, stride=8), :]
        sqst[d] = sq32[pl.ds(d, 8, stride=8), :]

    pl.semaphore_wait(tr, 1)

    def ab_copy(k):
        d = (g + k) % ng
        return remote(abst.at[d], ab.at[g], ab_s, ab_r, in_group(d))

    def sq_copy(k):
        d = (g + k) % ng
        return remote(sqst.at[d], sqr.at[g], sq_s, sq_r, twin(d))

    for k in range(ng):
        if k:
            ab_copy(k).start()
        sq_copy(k).start()
    ab[g] = abst[g]
    with jax.named_scope("w_ab"):
        whole(ab.at[pl.ds(0, ng - 1)], ab_s, ab_r).wait_recv()
        whole(sqr, sq_s, sq_r).wait_recv()
    pieces = [ab[d] for d in range(ng)]
    square = sqr[0]
    for d in range(1, ng):
        square = square + sqr[d]
    square = square[:, 0:1]
    for piece in pieces:
        square = square + jnp.sum(piece * piece, axis=1, keepdims=True)
    inv = lax.rsqrt(square / (H * HD) + 1e-06)
    for d in range(ng):
        cols = slice(d * 256, (d + 1) * 256)
        out[:, cols] = pieces[d] * inv * gain[:, cols]

    with jax.named_scope("drain"):
        for buf, ss, rs in (
            (nbuf, n_s, n_r), (sbuf, st_s, st_r), (fbuf, f_s, f_r), (gbuf, gt_s, gt_r),
            (qbuf, q_s, qz_r.at[0]),
        ):
            whole(buf.at[most], ss, rs).wait_send()
        few = pl.ds(0, ng - 1)
        whole(qa.at[few], qa_s, qa_r).wait_send()
        whole(ab.at[few], ab_s, ab_r).wait_send()
        whole(ex.at[:, few], ex_s, ex_r).wait_send()
        whole(sqr, sq_s, sq_r).wait_send()
        whole(kv.at[:, few], kv_s, kv_r.at[0, 0]).wait_send()


def spread(done, span_out, first_out, second_out, span, first, second, sems):
    span[...] = done[0:4, :].astype(BF16)
    first[...] = done[4:6, :].astype(BF16)
    second[...] = done[6:7, :].astype(BF16)
    pairs = ((span, span_out), (first, first_out), (second, second_out))
    copies = [pltpu.make_async_copy(a, o, sems.at[i]) for i, (a, o) in enumerate(pairs)]
    for copy in copies:
        copy.start()
    for copy in copies:
        copy.wait()


def per_device(
    dims, cache_k, cache_v, span_q, span_k, span_v, span_frames, action_ids, action_table,
    frame_q, frame_k, frame_v, revealed_k, revealed_v, mask_k, mask_v, pass1_idx, pass2_idx,
    out_gain,
):
    nx, nz = dims
    nb = nx * nz
    ng = NY * NC
    rows = cache_k.shape[0]
    cols = span_k.shape[1]
    dma = pltpu.SemaphoreType.DMA
    vm = pltpu.VMEM
    anywhere = pl.BlockSpec(memory_space=pl.ANY)
    local = pl.BlockSpec(memory_space=pltpu.VMEM)
    outs = [jax.ShapeDtypeStruct((n, span_q.shape[1]), BF16) for n in (4, 2, 1)]
    row = lambda v: v.reshape(1, -1)
    small = (
        span_q, span_k, span_v, row(span_frames), row(action_ids), action_table, frame_q, frame_k,
        frame_v, revealed_k, revealed_v, mask_k, mask_v, row(pass1_idx), row(pass2_idx),
        row(out_gain),
    )
    done = pl.pallas_call(
        functools.partial(kernel, dims),
        out_shape=pltpu.VMEM((8, span_q.shape[1]), F32),
        in_specs=[anywhere] * 18,
        out_specs=local,
        scratch_shapes=[vm(v.shape, v.dtype) for v in small]
        + [
            vm((2, ng, rows, HD), BF16),
            vm((2, ng, 16, HD), BF16),
            vm((2, NY, 16, HD), BF16),
            vm((16, cols), F32),
            vm((8, span_q.shape[1]), F32),
            vm((ng, 8, 256), BF16),
            vm((ng, 8, 256), BF16),
            vm((2, 64, HD), F32),
            vm((nb, 64, 256), BF16),
            vm((32 * nb, 32 * nb), BF16),
            vm((nb, 48, HD), BF16),
            vm((nb, 32, 128), F32),
            vm((8, 128), F32),
            vm((nb, 64, HD), BF16),
            vm((nb, 64, HD), BF16),
            vm((nb, 48, HD), BF16),
            vm((nb, 48, HD), BF16),
            vm((nb, 2, 128), F32),
            vm((nb, 2, 128), F32),
            vm((nb, 2, 128), F32),
            vm((nb, 2, 128), F32),
            vm((128, 128), F32),
            vm((2, 64, HD), F32),
            vm((64, 128), F32),
            vm((ng, 8, 256), F32),
            vm((ng, 8, 256), F32),
            vm((ng, 8, 128), F32),
            vm((ng, 8, 128), F32),
            dma((18,)),
            dma,
            dma,
            dma,
            dma((2, 2 * NY)),
            dma,
            dma,
            dma,
            dma((nz,)),
            dma((nz,)),
        ]
        + [dma] * 12
        + [pltpu.SemaphoreType.REGULAR((2, nz // 2 - 1)), pltpu.SemaphoreType.REGULAR],
        compiler_params=pltpu.CompilerParams(
            collective_id=0, has_side_effects=True, vmem_limit_bytes=60 << 20
        ),
        name="frame_attention",
    )(cache_k, cache_v, *small)
    return pl.pallas_call(
        spread,
        out_shape=outs,
        in_specs=[local],
        out_specs=[anywhere] * 3,
        scratch_shapes=[vm(v.shape, v.dtype) for v in outs] + [dma((3,))],
        name="spread",
    )(pltpu.with_memory_space_constraint(done, pltpu.VMEM))


def solution(mesh):
    both = P("ctx", "tp")
    in_specs = (
        both, both, both, both, both, P(), P("ctx"), P(None, "tp"), both, both, both, both, both,
        P("tp"), P("tp"), P(), P(), P("tp"),
    )
    nz = NZ
    nx = mesh.shape["ctx"] // (NY * NC * nz)
    return jax.shard_map(
        functools.partial(per_device, (nx, nz)),
        mesh=mesh,
        in_specs=in_specs,
        out_specs=(both, both, both),
        check_vma=False,
    )
```

```python
import functools

import jax
import jax.numpy as jnp
from jax import lax
from jax.experimental import pallas as pl
from jax.experimental.pallas import tpu as pltpu
from jax.sharding import PartitionSpec as P

H = 32
HD = 128
NX, NY, NZ, NC = 2, 4, 8, 2
LOG2E = 1.4426950408889634
MESH = pl.DeviceIdType.MESH
F32 = jnp.float32
BF16 = jnp.bfloat16
NEG = -1e30


def kernel(
    dims,
    ck, cv, *refs,
):
    nx, nz = dims
    hbm, refs = refs[:16], refs[16:]
    out, refs = refs[0], refs[1:]
    vmem, refs = refs[:16], refs[16:]
    sq, sk, sv, frames, ids, table, fq, fk, fv, rk, rv, mk, mv, p1, p2, gain = vmem
    (
        kv, ex, exst, ex32, q32, qa, qast, t32, qbuf, hot, qfs, qf, kfr,
        nst, nbuf, fst, fbuf, sst, sbuf, gst, gbuf, m32, at32, sq32, abst, ab, sqst, sqr,
        loc_sem, qa_s, qa_r, kv_s, kv_r, ex_s, ex_r,
        q_s, qz_r, qx_r, n_s, n_r, st_s, st_r, f_s, f_r, gt_s, gt_r,
        ab_s, ab_r, sq_s, sq_r, zr, tr,
    ) = refs
    nb = nx * nz
    ny, nc = NY, NC
    ng = ny * nc
    total = ny * nc * nb * 4
    scale = HD ** (-0.5) * LOG2E
    me = lax.axis_index("ctx")
    tp = lax.axis_index("tp")
    c = me % nc
    z = (me // nc) % nz
    y = (me // (nc * nz)) % ny
    x = me // (nc * nz * ny)
    g = y * nc + c
    b = x * nz + z

    def ctx_of(xx, yy, zz, cc):
        return ((xx * ny + yy) * nz + zz) * nc + cc

    def in_group(d):
        return {"ctx": ctx_of(x, d // nc, z, d % nc), "tp": tp}

    def twin(d):
        return {"ctx": ctx_of(x, d // nc, z, d % nc), "tp": 1 - tp}

    def at_block(xx, zz):
        return {"ctx": ctx_of(xx, y, zz, c), "tp": tp}

    def remote(src, dst, ss, rs, dev):
        return pltpu.make_async_remote_copy(
            src_ref=src, dst_ref=dst, send_sem=ss, recv_sem=rs, device_id=dev, device_id_type=MESH
        )

    def whole(part, ss, rs):
        return remote(part, part, ss, rs, at_block((x + 1) % nx, z))

    barrier = pltpu.get_barrier_semaphore()

    def greet(k, _):
        pl.semaphore_signal(barrier, inc=1, device_id=in_group((g + k) % ng), device_id_type=MESH)
        return 0

    pl.semaphore_signal(barrier, inc=1, device_id=at_block(x, (z + 1) % nz), device_id_type=MESH)
    pl.semaphore_signal(
        barrier, inc=1, device_id=at_block(x, (z + nz - 1) % nz), device_id_type=MESH
    )
    pl.semaphore_signal(barrier, inc=1, device_id=at_block((x + 1) % nx, z), device_id_type=MESH)
    pl.semaphore_signal(barrier, inc=1, device_id=twin(g), device_id_type=MESH)
    lax.fori_loop(1, ng, greet, 0)

    def tell(n):
        for way in range(2):
            zz = (z + 1 + way * (nz - 2)) % nz
            pl.semaphore_signal(
                zr.at[way, n], inc=1, device_id=at_block(x, zz), device_id_type=MESH
            )

    def told(n):
        for way in range(2):
            pl.semaphore_wait(zr.at[way, n], 1)

    def load(i):
        return pltpu.make_async_copy(hbm[i], vmem[i], loc_sem.at[2 + i])

    for i in (0, 6, 1, 2, 3, 4, 5, 7, 8, 9, 10, 11, 12, 13, 14, 15):
        load(i).start()
    col = pl.ds(pl.multiple_of(y * HD, HD), HD)
    own_k = pltpu.make_async_copy(ck.at[:, col], kv.at[0, g], loc_sem.at[0])
    own_v = pltpu.make_async_copy(cv.at[:, col], kv.at[1, g], loc_sem.at[1])
    own_k.start()
    own_v.start()

    load(0).wait()
    load(6).wait()
    q32[0:4, :] = sq[...].astype(F32)
    q32[4:8, :] = fq[...].astype(F32)
    for d in range(ng):
        qast[d] = q32[:, d * 256 : (d + 1) * 256].astype(BF16)

    def qa_copy(k):
        d = (g + k) % ng
        return remote(qast.at[d], qa.at[g], qa_s, qa_r, in_group(d))

    def ex_copy(k):
        d = (g + k) % ng
        return remote(exst.at[:, d // nc], ex.at[:, g], ex_s, ex_r, in_group(d))

    def kv_copy(n, k):
        d = (g + nc * k) % ng
        head = pl.ds(pl.multiple_of((d // nc) * HD, HD), HD)
        source = (ck, cv)[n]
        return remote(
            source.at[:, head], kv.at[n, g], kv_s, kv_r.at[n, k], in_group(d)
        )

    def relay(n, k):
        origin = (g + ng - nc * k) % ng
        peer = y * nc + 1 - c
        src = ((ck, cv)[n].at[:, col]) if k == 0 else kv.at[n, origin]
        return remote(src, kv.at[n, origin], kv_s, kv_r.at[n, ny + k], in_group(peer))

    with jax.named_scope("w_barrier"):
        pl.semaphore_wait(barrier, 4 + (ng - 1))

    reach = nz // 2 - 1
    tell(0)
    for k in range(1, ng):
        qa_copy(k).start()
    pl.semaphore_signal(tr, inc=1, device_id=twin(g), device_id_type=MESH)
    for k in (2, 1, 3):
        kv_copy(0, k).start()
    relay(0, 0).start()
    qa[g] = qast[g]

    told(0)
    tell(1)
    for k in (2, 1, 3):
        kv_copy(1, k).start()
    relay(1, 0).start()
    for n in range(1, reach - 1):
        told(n)
        tell(n + 1)

    with jax.named_scope("w_qa"):
        whole(qa.at[pl.ds(0, ng - 1)], qa_s, qa_r).wait_recv()
    for h in range(2):
        cols = slice(h * HD, (h + 1) * HD)
        t32[h] = qa[:, :, cols].astype(F32).reshape(64, HD)
        for i in range(4):
            pair = [t32[h, pl.ds(2 * i + r, 8, stride=8), :] for r in range(2)]
            qbuf[b, 16 * i : 16 * i + 16, cols] = jnp.concatenate(pair, axis=0).astype(BF16)

    def off(k):
        near = k // 2
        return near + 1 if k % 2 else (nz - near) % nz

    def off_dyn(k):
        near = k // 2
        odd = k % 2
        return (odd * (near + 1) + (1 - odd) * (nz - near)) % nz

    def qz_copy(k):
        return remote(
            qbuf.at[b], qbuf.at[b], q_s, qz_r.at[k], at_block(x, (z + off(k)) % nz)
        )

    def qx_copy(k):
        blk = x * nz + (z + nz - off(k)) % nz
        return remote(
            qbuf.at[blk], qbuf.at[blk], q_s, qx_r.at[k], at_block((x + 1) % nx, z)
        )

    qx_copy(0).start()
    for k in range(1, nz - 1):
        qz_copy(k).start()
    told(reach - 1)
    qz_copy(nz - 1).start()

    for i in (1, 2, 3, 4, 5, 7, 8, 9, 10, 11, 12, 13, 14, 15):
        load(i).wait()

    row4 = lax.broadcasted_iota(jnp.int32, (4, 4), 0)
    lane4 = lax.broadcasted_iota(jnp.int32, (4, 4), 1)
    ids_col = jnp.sum(jnp.where(row4 == lane4, ids[...], 0), axis=1, keepdims=True)
    action = jnp.zeros(sk.shape, F32)
    tab = table[...].astype(F32)
    for a in range(table.shape[0]):
        action = jnp.where(ids_col == a, tab[a : a + 1, :], action)
    pos = me * 4 + lax.broadcasted_iota(jnp.int32, (4, 1), 0)
    in1 = jnp.sum(jnp.where(p1[...] == pos, 1.0, 0.0), axis=1, keepdims=True) > 0.5
    in2 = jnp.sum(jnp.where(p2[...] == pos, 1.0, 0.0), axis=1, keepdims=True) > 0.5

    def masked(frame, revealed, mask):
        shape = frame.shape
        frame, revealed = frame[...].astype(F32), revealed[...].astype(F32)
        mask = jnp.broadcast_to(mask[...].astype(F32).reshape(1, -1), shape)
        first = jnp.where(in1, mask, frame)
        second = jnp.where(in2, mask, jnp.where(in1, revealed, frame))
        return first, second

    for n, (span, pair) in enumerate(
        (
            (sk[...].astype(F32) + action, masked(fk, rk, mk)),
            (sv[...].astype(F32), masked(fv, rv, mv)),
        )
    ):
        ex32[0:4, :] = span
        ex32[4:8, :] = pair[0]
        ex32[8:12, :] = pair[1]
        ex32[12:16, :] = jnp.zeros_like(span)
        for d in range(ny):
            exst[n, d] = ex32[:, d * HD : (d + 1) * HD].astype(BF16)
    for k in range(1, ng):
        ex_copy(k).start()
    for n in range(2):
        ex[n, g] = exst[n, y]


    rows = 32 * nb

    def owners(width):
        r = lax.broadcasted_iota(jnp.int32, (rows, width), 0)
        ll = lax.broadcasted_iota(jnp.int32, (rows, width), 1)
        rb, rt, ro = r >> 5, (r >> 3) & 3, r & 7
        rx = jnp.where(rb >= nz, 1, 0)
        rz = rb - nz * rx
        return ll, rt, ((rx * ny + (ro >> 1)) * nz + rz) * nc + (ro & 1)

    lane, rt, owner = owners(total)
    fr = jnp.broadcast_to(frames[...].astype(F32), (rows, total))
    qframe = jnp.sum(jnp.where(lane == 4 * owner + rt, fr, 0.0), axis=1, keepdims=True)
    qf[...] = jnp.broadcast_to(qframe, (rows, 128)).reshape(nb, 32, 128)

    key = lax.broadcasted_iota(jnp.int32, (total, 128), 0)
    kl = lax.broadcasted_iota(jnp.int32, (total, 128), 1)
    ko, ks = kl >> 4, kl & 15
    kwant = 4 * (((x * ny + (ko >> 1)) * nz + z) * nc + (ko & 1)) + ks
    khit = jnp.where((key == kwant) & (ks < 4), 1.0, 0.0).astype(BF16)
    fr8 = jnp.broadcast_to(frames[...].astype(F32), (8, total)).astype(BF16)
    kfr[...] = jnp.dot(fr8, khit, preferred_element_type=F32)

    l1, t1, o1 = owners(p1.shape[1])
    l2, t2, o2 = owners(p2.shape[1])
    v1 = jnp.broadcast_to(p1[...].astype(F32), l1.shape)
    v2 = jnp.broadcast_to(p2[...].astype(F32), l2.shape)
    found = jnp.sum(
        jnp.where((l1 == 2 * o1 + t1) & (t1 < 2), v1, 0.0), axis=1, keepdims=True
    ) + jnp.sum(jnp.where((l2 == o2) & (t2 == 2), v2, 0.0), axis=1, keepdims=True)
    found = found.astype(jnp.int32)
    bits = nz.bit_length() - 1
    dev = found >> 2
    from_z = (dev >> 1) & (nz - 1)
    from_y = (dev >> (1 + bits)) & (ny - 1)
    from_x = dev >> (3 + bits)
    place = (from_x * nz + from_z) * 32 + (found & 3) * 8 + from_y * nc + (dev & 1)
    lanes = lax.broadcasted_iota(jnp.int32, (rows, rows), 1)
    hot[...] = jnp.where(lanes == place, 1.0, 0.0).astype(BF16)

    with jax.named_scope("w_kv"):
        for n in range(2):
            for k in (1, 3, 2):
                kv_copy(n, k).wait_recv()
                relay(n, k).start()

    def from_z_half(k):
        qz_copy(k).wait_recv()
        qx_copy(k).start()

    with jax.named_scope("w_qz"):
        for k in range(1, 4):
            from_z_half(k)

    with jax.named_scope("w_relay"):
        whole(ex.at[:, pl.ds(0, ng - 1)], ex_s, ex_r).wait_recv()
        own_k.wait()
        own_v.wait()
        for k in range(ny):
            for n in range(2):
                relay(n, k).wait_recv()

    keys = kv.shape[1] * kv.shape[2]
    nt = (((1,), (1,)), ((), ()))

    def dest(k):
        return (x + k // nz) % nx, (z + nz - off_dyn(k % nz)) % nz

    def scores(q, bias):
        s1 = lax.dot_general(q, kv[0].reshape(keys, HD), nt, preferred_element_type=F32)
        s2 = lax.dot_general(q, ex[0].reshape(128, HD), nt, preferred_element_type=F32) + bias
        return s1, s2

    def weigh(s1, s2):
        m = jnp.maximum(s1.max(axis=1, keepdims=True), s2.max(axis=1, keepdims=True))
        w1 = jnp.exp2((s1 - m) * scale)
        w2 = jnp.exp2((s2 - m) * scale)
        tot = w1.sum(axis=1, keepdims=True) + w2.sum(axis=1, keepdims=True)
        o = jnp.dot(w1.astype(BF16), kv[1].reshape(keys, HD), preferred_element_type=F32)
        o = o + jnp.dot(w2.astype(BF16), ex[1].reshape(128, HD), preferred_element_type=F32)
        return o, jnp.where(lax.broadcasted_iota(jnp.int32, o.shape, 1) == 0, m, tot)

    def attention(tiles):
        return [weigh(*pair) for pair in [scores(*tile) for tile in tiles]]

    def n_copy(k, blk, dev):
        return remote(nst.at[blk], nbuf.at[b], n_s, n_r, dev)

    def st_copy(k, blk, dev):
        return remote(sst.at[blk], sbuf.at[b], st_s, st_r, dev)

    def f_copy(k, blk, dev):
        return remote(fst.at[blk], fbuf.at[b], f_s, f_r, dev)

    def gt_copy(k, blk, dev):
        return remote(gst.at[blk], gbuf.at[b], gt_s, gt_r, dev)

    def put_stats(stats, into, blks):
        turned = stats.T[0:8, :]
        for q in range(4):
            tile = turned[:, (q // 2) * 128 : (q // 2) * 128 + 128]
            if q % 2:
                tile = pltpu.roll(tile, 64, 1)
            into[blks[q]] = tile[0:2]

    def push(s, blks, dests, copies):
        for q in (3, 2, 1, 0):
            dev = at_block(*dests[q])

            def go(q=q, dev=dev):
                for copy in copies:
                    copy(4 * s + q, blks[q], dev).start()

            if q == 0:
                pl.when(s > 0)(go)
            else:
                go()

    slot32 = lax.broadcasted_iota(jnp.int32, (32, 128), 1) & 15
    half = nz // 4

    def spans(s, _):
        for u in range(half, 2 * half):

            @pl.when(s == u)
            def _(u=u):
                with jax.named_scope(f"wx{u}"):
                    for q in range(4):
                        qx_copy(4 * (u - half) + q).wait_recv()

        for u in range(1, half):

            @pl.when(s == u)
            def _(u=u):
                with jax.named_scope(f"wz{u}"):
                    for q in range(4):
                        from_z_half(4 * u + q)

        dests = [dest(4 * s + q) for q in range(4)]
        blks = [xx * nz + zz for xx, zz in dests]
        parts, bias = [], []
        for blk in blks:
            mask = jnp.where((slot32 < 4) & (kfr[0:1, :] <= qf[blk]), 0.0, NEG)
            bias += [mask, mask]
            parts += [qbuf[blk, 0:32, 0:HD], qbuf[blk, 0:32, HD : 2 * HD]]
        done = attention(
            [
                (jnp.concatenate(parts[u : u + 4], axis=0), jnp.concatenate(bias[u : u + 4], axis=0))
                for u in (0, 4)
            ]
        )
        for q in range(4):
            low = 64 * (q % 2)
            nst[blks[q]] = done[q // 2][0][low : low + 64].astype(BF16)
        put_stats(jnp.concatenate([st for _, st in done], axis=0), sst, blks)
        push(s, blks, dests, (st_copy, n_copy))
        return 0

    with jax.named_scope("spans"):
        lax.fori_loop(0, 2 * half, spans, 0)

    frame_q = qbuf[:, 32:64, :].reshape(rows, 256)
    picked = jnp.dot(hot[...], frame_q, preferred_element_type=F32)
    for blk in range(nb):
        both = [picked[32 * blk : 32 * blk + 24, h * HD : (h + 1) * HD] for h in range(2)]
        qfs[blk] = jnp.concatenate(both, axis=0).astype(BF16)

    r48 = lax.broadcasted_iota(jnp.int32, (48, 128), 0)
    slot48 = lax.broadcasted_iota(jnp.int32, (48, 128), 1) & 15
    t48 = (jnp.where(r48 >= 24, r48 - 24, r48)) >> 3
    allowed = (slot48 < 4) | ((slot48 < 8) & (t48 < 2)) | (
        (slot48 >= 8) & (slot48 < 12) & (t48 == 2)
    )
    mask48 = jnp.where(allowed, 0.0, NEG)

    mask192 = jnp.concatenate([mask48] * 4, axis=0)

    def picks(i, _):
        steps = [2 * half - 1 - i, half - 1 - i]
        dests = [[dest(4 * s + q) for q in range(4)] for s in steps]
        blks = [[xx * nz + zz for xx, zz in group] for group in dests]
        done = attention(
            [(jnp.concatenate([qfs[blk] for blk in group], axis=0), mask192) for group in blks]
        )
        pad = jnp.zeros((16, 128), F32)
        for s, group, where, (o, stats) in zip(steps, blks, dests, done):
            padded = []
            for q in range(4):
                fst[group[q]] = o[48 * q : 48 * q + 48].astype(BF16)
                padded += [stats[48 * q : 48 * q + 48], pad]
            put_stats(jnp.concatenate(padded, axis=0), gst, group)
        for s, group, where in zip(steps, blks, dests):
            push(s, group, where, (gt_copy, f_copy))
        return 0

    with jax.named_scope("picks"):
        lax.fori_loop(0, half, picks, 0)
    nbuf[b] = nst[b]
    sbuf[b] = sst[b]
    fbuf[b] = fst[b]
    gbuf[b] = gst[b]
    most = pl.ds(0, nb - 1)

    def shares(stats, n):
        for s in range(nb):
            m32[2 * s : 2 * s + 2, :] = stats[s]
        st = m32[...].T[0:n]
        lanes = lax.broadcasted_iota(jnp.int32, (n, 128), 1)
        is_m = ((lanes & 1) == 0) & (lanes < 2 * nb)
        top = jnp.max(jnp.where(is_m, st, NEG), axis=1, keepdims=True)
        tot = pltpu.roll(st, 127, 1)
        e = jnp.where(is_m, jnp.exp2((jnp.where(is_m, st, top) - top) * scale), 0.0)
        den = jnp.sum(jnp.where(is_m, e * tot, 0.0), axis=1, keepdims=True)
        return e / den

    def merge(data, w, n):
        acc = jnp.zeros((n, HD), F32)
        for s in range(nb):
            acc = acc + w[:, 2 * s : 2 * s + 1] * data[s].astype(F32)
        return acc

    def settle(acc, low, n):
        squares = jnp.sum(acc * acc, axis=1, keepdims=True)
        at32[0, low : low + n, :] = acc[0:n]
        at32[1, low : low + n, :] = acc[n : 2 * n]
        sq32[low : low + n, :] = jnp.broadcast_to(squares[0:n] + squares[n : 2 * n], (n, 128))

    m32[...] = jnp.zeros((128, 128), F32)
    with jax.named_scope("w_st"):
        whole(sbuf.at[most], st_s, st_r).wait_recv()
    w_span = shares(sbuf, 64)
    with jax.named_scope("w_n"):
        whole(nbuf.at[most], n_s, n_r).wait_recv()
    settle(merge(nbuf, w_span, 64), 0, 32)
    with jax.named_scope("w_gt"):
        whole(gbuf.at[most], gt_s, gt_r).wait_recv()
    w_frame = shares(gbuf, 48)
    with jax.named_scope("w_f"):
        whole(fbuf.at[most], f_s, f_r).wait_recv()
    settle(merge(fbuf, w_frame, 48), 32, 24)
    at32[:, 56:64, :] = jnp.zeros((2, 8, HD), F32)
    sq32[56:64, :] = jnp.zeros((8, 128), F32)
    for d in range(ng):
        for h in range(2):
            abst[d, :, h * HD : (h + 1) * HD] = at32[h, pl.ds(d, 8, stride=8), :]
        sqst[d] = sq32[pl.ds(d, 8, stride=8), :]

    pl.semaphore_wait(tr, 1)

    def ab_copy(k):
        d = (g + k) % ng
        return remote(abst.at[d], ab.at[g], ab_s, ab_r, in_group(d))

    def sq_copy(k):
        d = (g + k) % ng
        return remote(sqst.at[d], sqr.at[g], sq_s, sq_r, twin(d))

    for k in (4, 5, 3, 6, 2, 7, 1, 0):
        if k:
            ab_copy(k).start()
        sq_copy(k).start()
    ab[g] = abst[g]
    with jax.named_scope("w_ab"):
        whole(ab.at[pl.ds(0, ng - 1)], ab_s, ab_r).wait_recv()
        whole(sqr, sq_s, sq_r).wait_recv()
    pieces = [ab[d] for d in range(ng)]
    square = sqr[0]
    for d in range(1, ng):
        square = square + sqr[d]
    square = square[:, 0:1]
    for piece in pieces:
        square = square + jnp.sum(piece * piece, axis=1, keepdims=True)
    inv = lax.rsqrt(square / (H * HD) + 1e-06)
    for d in range(ng):
        cols = slice(d * 256, (d + 1) * 256)
        out[:, cols] = pieces[d] * inv * gain[:, cols]

    with jax.named_scope("drain"):
        for buf, ss, rs in (
            (nbuf, n_s, n_r), (sbuf, st_s, st_r), (fbuf, f_s, f_r), (gbuf, gt_s, gt_r),
            (qbuf, q_s, qz_r.at[0]),
        ):
            whole(buf.at[most], ss, rs).wait_send()
        few = pl.ds(0, ng - 1)
        whole(qa.at[few], qa_s, qa_r).wait_send()
        whole(ab.at[few], ab_s, ab_r).wait_send()
        whole(ex.at[:, few], ex_s, ex_r).wait_send()
        whole(sqr, sq_s, sq_r).wait_send()
        whole(kv.at[:, few], kv_s, kv_r.at[0, 0]).wait_send()


def spread(done, span_out, first_out, second_out, span, first, second, sems):
    span[...] = done[0:4, :].astype(BF16)
    first[...] = done[4:6, :].astype(BF16)
    second[...] = done[6:7, :].astype(BF16)
    pairs = ((span, span_out), (first, first_out), (second, second_out))
    copies = [pltpu.make_async_copy(a, o, sems.at[i]) for i, (a, o) in enumerate(pairs)]
    for copy in copies:
        copy.start()
    for copy in copies:
        copy.wait()


def per_device(
    dims, cache_k, cache_v, span_q, span_k, span_v, span_frames, action_ids, action_table,
    frame_q, frame_k, frame_v, revealed_k, revealed_v, mask_k, mask_v, pass1_idx, pass2_idx,
    out_gain,
):
    nx, nz = dims
    nb = nx * nz
    ng = NY * NC
    rows = cache_k.shape[0]
    cols = span_k.shape[1]
    dma = pltpu.SemaphoreType.DMA
    vm = pltpu.VMEM
    anywhere = pl.BlockSpec(memory_space=pl.ANY)
    local = pl.BlockSpec(memory_space=pltpu.VMEM)
    outs = [jax.ShapeDtypeStruct((n, span_q.shape[1]), BF16) for n in (4, 2, 1)]
    row = lambda v: v.reshape(1, -1)
    small = (
        span_q, span_k, span_v, row(span_frames), row(action_ids), action_table, frame_q, frame_k,
        frame_v, revealed_k, revealed_v, mask_k, mask_v, row(pass1_idx), row(pass2_idx),
        row(out_gain),
    )
    done = pl.pallas_call(
        functools.partial(kernel, dims),
        out_shape=pltpu.VMEM((8, span_q.shape[1]), F32),
        in_specs=[anywhere] * 18,
        out_specs=local,
        scratch_shapes=[vm(v.shape, v.dtype) for v in small]
        + [
            vm((2, ng, rows, HD), BF16),
            vm((2, ng, 16, HD), BF16),
            vm((2, NY, 16, HD), BF16),
            vm((16, cols), F32),
            vm((8, span_q.shape[1]), F32),
            vm((ng, 8, 256), BF16),
            vm((ng, 8, 256), BF16),
            vm((2, 64, HD), F32),
            vm((nb, 64, 256), BF16),
            vm((32 * nb, 32 * nb), BF16),
            vm((nb, 48, HD), BF16),
            vm((nb, 32, 128), F32),
            vm((8, 128), F32),
            vm((nb, 64, HD), BF16),
            vm((nb, 64, HD), BF16),
            vm((nb, 48, HD), BF16),
            vm((nb, 48, HD), BF16),
            vm((nb, 2, 128), F32),
            vm((nb, 2, 128), F32),
            vm((nb, 2, 128), F32),
            vm((nb, 2, 128), F32),
            vm((128, 128), F32),
            vm((2, 64, HD), F32),
            vm((64, 128), F32),
            vm((ng, 8, 256), F32),
            vm((ng, 8, 256), F32),
            vm((ng, 8, 128), F32),
            vm((ng, 8, 128), F32),
            dma((18,)),
            dma,
            dma,
            dma,
            dma((2, 2 * NY)),
            dma,
            dma,
            dma,
            dma((nz,)),
            dma((nz,)),
        ]
        + [dma] * 12
        + [pltpu.SemaphoreType.REGULAR((2, nz // 2 - 1)), pltpu.SemaphoreType.REGULAR],
        compiler_params=pltpu.CompilerParams(
            collective_id=0, has_side_effects=True, vmem_limit_bytes=60 << 20
        ),
        name="frame_attention",
    )(cache_k, cache_v, *small)
    return pl.pallas_call(
        spread,
        out_shape=outs,
        in_specs=[local],
        out_specs=[anywhere] * 3,
        scratch_shapes=[vm(v.shape, v.dtype) for v in outs] + [dma((3,))],
        name="spread",
    )(pltpu.with_memory_space_constraint(done, pltpu.VMEM))


def solution(mesh):
    both = P("ctx", "tp")
    in_specs = (
        both, both, both, both, both, P(), P("ctx"), P(None, "tp"), both, both, both, both, both,
        P("tp"), P("tp"), P(), P(), P("tp"),
    )
    nz = NZ
    nx = mesh.shape["ctx"] // (NY * NC * nz)
    return jax.shard_map(
        functools.partial(per_device, (nx, nz)),
        mesh=mesh,
        in_specs=in_specs,
        out_specs=(both, both, both),
        check_vma=False,
    )
```
